32 devices in a mesh: section: 4 (over z), dp: 8 (over y, x, core).
Axes of the slice: x: 2, y: 2, z: 4, core: 2. Of those that a mesh axis runs over, the one named last changes fastest.
Arguments:
- held: bfloat16 [4, 2, 1024, 2048], P('section', None, 'dp'), may hold values from -70 to 70
- norm_gain: float32 [4, 2048], P('section'), may hold values from 0.3 to 3
- w_qkv: bfloat16 [4, 2048, 2560], P('section', None, 'dp'), may hold values from -1 to 1
- q_gain: float32 [4, 128], P('section'), may hold values from 0.5 to 7
- k_gain: float32 [4, 128], P('section'), may hold values from 0.5 to 7
- w_out: bfloat16 [4, 2048, 2048], P('section', None, 'dp'), may hold values from -0.125 to 0.125
- lengths: int32 [4, 2, 8], P('section'), may hold values from 1 to 512, 1024 in all within a row
Outputs:
- handed: bfloat16 [4, 2, 1024, 2048], P('section', None, 'dp')
The draws below stay inside these ranges and needn't reach their ends.
Inputs may be any that keep to these rules, and one draw needn't show every extreme that they name: Each row lists the 8 document lengths of one packed micro-batch in order; they sum to 1024 and the longest is exactly 512.
All inputs are finite; a program needn't handle non-finite values.
Results may differ from the reference program's by a relative error of at most 0.0086.
Values may be sent and summed in bfloat16 or wider, within the bound.
No kernel may reach another device: no remote copies, remote signals or barrier semaphores. Data moves between devices by JAX's collectives and lax.ppermute only.
A program may use at most 128 MiB of HBM per device.

```python
import math
import jax
import jax.numpy as jnp
import numpy as np
from jax import lax

D = 2048
HEADS = 16
KV_HEADS = 2
HEAD = 128
MICRO = 2
DOCS = 8
GROUP = 8
INNER = 2048
QKV = 2560
TOKENS = 1024
DOC_MOST = 512
N_SECTION = 4


def draw_held(key, part):
    first = jax.random.fold_in(key, 0)
    shape = (N_SECTION, MICRO, TOKENS, D)
    base = jax.random.truncated_normal(first, -6.0, 6.0, shape, jnp.float32)
    return base.astype(jnp.bfloat16)


def draw_w_qkv(key, part):
    first = jax.random.fold_in(key, 0)
    weights = jax.random.truncated_normal(first, -4.0, 4.0, (N_SECTION, D, QKV), jnp.float32) * D ** (-0.5)
    return weights.astype(jnp.bfloat16)


def gain_draw(key, salt):
    salted = jax.random.fold_in(key, salt)
    return jnp.exp(jax.random.uniform(salted, (N_SECTION, HEAD), jnp.float32, math.log(0.5), math.log(2.0)))


def draw_q_gain(key, part):
    return gain_draw(key, 11)


def draw_k_gain(key, part):
    return gain_draw(key, 12)


def levels(key, extent, cuts, smallest, top_value):
    factor_of = 1.0
    for dim, blocks in cuts:
        draws = jax.random.uniform(jax.random.fold_in(jax.random.fold_in(key, 6), dim), (blocks,), jnp.float32, smallest / len(cuts), top_value / len(cuts))
        factor_of = factor_of * jnp.repeat(jnp.exp(draws), extent[dim] // blocks).reshape((-1,) + (1,) * (len(extent) - 1 - dim))
    return factor_of


def profile(amount, total, limit, skew):
    portions = [(1 << 20) // math.isqrt(rank ** skew) + 1 for rank in range(2, amount + 1)]
    rest, holding = total - limit - (amount - 1), [1] * (amount - 1)
    while rest > 0:
        candidates = [i for i in range(amount - 1) if holding[i] < limit]
        pool, budget = sum([portions[i] for i in candidates]), rest
        for i in candidates:
            more = min(limit - holding[i], max(1, budget * portions[i] // pool), rest)
            holding[i] = holding[i] + more
            rest = rest - more
    return np.array([limit] + holding)


def uneven(rng, number_of, total, limit, slope):
    if number_of == 2:
        one = jax.random.randint(rng, (), max(1, total - limit), min(limit, total - 1) + 1)
        return jnp.stack([one, total - one])
    sizes = jnp.asarray(profile(number_of, total, limit, slope), jnp.int32)
    twos = (number_of - 1) // 2
    source_of, sink = sizes[1:1 + 2 * twos:2], sizes[2:2 + 2 * twos:2]
    room = jnp.minimum(source_of - 1, limit - sink)
    passed = jax.random.randint(jax.random.fold_in(rng, 1), (twos,), 0, 1 << 20) % (room + 1)
    sizes = sizes.at[1:1 + 2 * twos:2].set(source_of - passed).at[2:2 + 2 * twos:2].set(sink + passed)
    return sizes[jax.random.permutation(jax.random.fold_in(rng, 2), number_of)]


def normal_values(own_key, extent, scale, most, cuts=(), kind=jnp.bfloat16):
    entries = jax.random.normal(own_key, extent, jnp.float32) * scale
    if len(cuts) > 0:
        entries = levels(own_key, extent, cuts, -0.22, 0.18) * entries
    return jnp.clip(entries, min=-most, max=most).astype(kind)


def setup_inputs(seed: int = 0) -> dict:
    key_of = jax.random.split(jax.random.key(seed), 8)
    return {
        "held": draw_held(jax.random.fold_in(key_of[7], 71), 0),
        "norm_gain": jnp.clip(jnp.exp(math.log(3.0) - 2.3025851 * jax.random.uniform(key_of[1], (N_SECTION, D), jnp.float32) ** levels(key_of[1], (N_SECTION, D), ((0, 4),), -0.2, 0.2)), 0.3, 3.0),
        "w_qkv": draw_w_qkv(jax.random.fold_in(key_of[7], 71), 0),
        "q_gain": draw_q_gain(jax.random.fold_in(key_of[7], 71), 0),
        "k_gain": draw_k_gain(jax.random.fold_in(key_of[7], 71), 0),
        "w_out": normal_values(key_of[5], (N_SECTION, INNER, D), INNER ** -0.5, 0.125, ((0, 4), (2, 8))),
        "lengths": jax.vmap(lambda own: uneven(own, DOCS, TOKENS, DOC_MOST, 2))(jax.random.split(key_of[6], N_SECTION * MICRO)).reshape((N_SECTION, MICRO, DOCS)).astype(jnp.int32),
    }


EPSILON = 1e-06
THETA = 1000000.0

def rms_scale(values, gain):
    return values * lax.rsqrt(lax.optimization_barrier(jnp.mean(values * values, axis=-1, keepdims=True)) + EPSILON) * gain

def rotary(values, places):
    width = values.shape[-1]
    middle = width // 2
    spacing = jnp.exp(jnp.arange(middle, dtype=jnp.float32) * (-2.0 * math.log(THETA) / width))
    angle = places.astype(jnp.float32)[..., None] * spacing
    cosine = jnp.cos(angle)[..., None, :]
    sine = jnp.sin(angle)[..., None, :]
    former = values[..., :middle]
    latter = values[..., middle:]
    return jnp.concatenate([former * cosine - latter * sine, latter * cosine + former * sine], axis=-1)

def layer(resident_bf, gain, weight_in, query_gain, key_gain, weight_out, doc_lengths):
    total = resident_bf.shape[0]
    inner = HEADS * HEAD
    key_width = KV_HEADS * HEAD
    resident = resident_bf.astype(jnp.float32)
    normed = rms_scale(resident, gain).astype(jnp.bfloat16)
    projected = jnp.dot(normed, weight_in, preferred_element_type=jnp.float32)
    index = jnp.arange(total, dtype=jnp.int32)
    ends = jnp.cumsum(doc_lengths)
    before = (ends[None, :] <= index[:, None]).astype(jnp.int32)
    doc_start = lax.optimization_barrier(jnp.sum(before * doc_lengths[None, :], axis=-1))
    doc_number = lax.optimization_barrier(jnp.sum(before, axis=-1))
    places = index - doc_start
    queries = rotary(rms_scale(projected[:, :inner].reshape(total, HEADS, HEAD), query_gain), places).astype(jnp.bfloat16)
    keys = rotary(rms_scale(projected[:, inner:inner + key_width].reshape(total, KV_HEADS, HEAD), key_gain), places).astype(jnp.bfloat16)
    values = projected[:, inner + key_width:].reshape(total, KV_HEADS, HEAD).astype(jnp.bfloat16)
    block = math.gcd(total, 512)
    reach = min(total, block + DOC_MOST)

    def attend(number):
        first = (number * block).astype(jnp.int32)
        key_first = jnp.clip(first + block - reach, 0, total - reach).astype(jnp.int32)
        query_rows = lax.dynamic_slice_in_dim(queries, first, block, 0).reshape(block, KV_HEADS, GROUP, HEAD).astype(jnp.float32)
        key_rows = lax.dynamic_slice_in_dim(keys, key_first, reach, 0).astype(jnp.float32)
        value_rows = lax.dynamic_slice_in_dim(values, key_first, reach, 0).astype(jnp.float32)
        query_index = first + jnp.arange(block, dtype=jnp.int32)
        key_index = key_first + jnp.arange(reach, dtype=jnp.int32)
        query_doc = lax.dynamic_slice_in_dim(doc_number, first, block, 0)
        key_doc = lax.dynamic_slice_in_dim(doc_number, key_first, reach, 0)
        scores = jnp.einsum('qkgd,nkd->kgqn', query_rows, key_rows) / math.sqrt(HEAD)
        allowed = (query_doc[:, None] == key_doc[None, :]) & (query_index[:, None] >= key_index[None, :])
        highest = lax.optimization_barrier(jnp.max(jnp.where(allowed, scores, -jnp.inf), axis=-1, keepdims=True))
        weights = lax.optimization_barrier(jnp.where(allowed, jnp.exp(scores - highest), 0.0).astype(jnp.bfloat16)).astype(jnp.float32)
        numer = jnp.einsum('kgqn,nkd->qkgd', weights, value_rows)
        denom = jnp.transpose(lax.optimization_barrier(jnp.sum(weights, axis=-1)), (2, 0, 1))
        return (numer / denom[..., None]).astype(jnp.bfloat16).reshape(block, inner)
    attended = lax.map(attend, jnp.arange(total // block, dtype=jnp.int32)).reshape(total, inner)
    mixed = jnp.dot(attended, weight_out, preferred_element_type=jnp.float32)
    return (resident + mixed).astype(jnp.bfloat16)

def reference(held, norm_gain, w_qkv, q_gain, k_gain, w_out, lengths):
    sections = held.shape[0]
    micro = held.shape[1]

    def one(number):
        section = number // micro
        which = number % micro
        return layer(held[section, which], norm_gain[section], w_qkv[section], q_gain[section], k_gain[section], w_out[section], lengths[section, which])
    results = lax.map(one, jnp.arange(sections * micro, dtype=jnp.int32)).reshape(held.shape)
    return jnp.roll(results, 1, axis=0)
```

```python
import functools
import math

import jax
import jax.numpy as jnp
from jax import lax
from jax.experimental import pallas as pl
from jax.experimental.pallas import tpu as pltpu
from jax.sharding import PartitionSpec as P

HEADS = 16
KV_HEADS = 2
HEAD = 128
GROUP = 8


EPSILON = 1e-06
THETA = 1000000.0
NEGATIVE = -1e30


def from_behind(value, axis, steps):
    count = lax.axis_size(axis)
    pairs = [(source, (source + steps) % count) for source in range(count)]
    return lax.ppermute(value, axis, pairs)


def rms_scale(values, gain):
    return values * lax.rsqrt(jnp.mean(values * values, axis=-1, keepdims=True) + EPSILON) * gain


def rotary(values, places):
    width = values.shape[-1]
    middle = width // 2
    spacing = jnp.exp(jnp.arange(middle, dtype=jnp.float32) * (-2.0 * math.log(THETA) / width))
    angle = places.astype(jnp.float32)[..., None] * spacing
    cosine = jnp.cos(angle)[..., None, :]
    sine = jnp.sin(angle)[..., None, :]
    former = values[..., :middle]
    latter = values[..., middle:]
    return jnp.concatenate(
        [former * cosine - latter * sine, latter * cosine + former * sine], axis=-1
    )


def locate(positions, doc_lengths):
    ends = jnp.cumsum(doc_lengths, axis=-1)
    before = (ends[:, None, :] <= positions[None, :, None]).astype(jnp.int32)
    return (jnp.sum(before, axis=-1), jnp.sum(before * doc_lengths[:, None, :], axis=-1))


def attend_rows(query_rows, key_rows, value_rows, allowed):
    scores = jnp.einsum(
        "kqd,nkd->kqn", query_rows, key_rows, preferred_element_type=jnp.float32
    ) / math.sqrt(HEAD)
    highest = jnp.max(jnp.where(allowed[None], scores, NEGATIVE), axis=-1)
    weights = jnp.where(allowed[None], jnp.exp(scores - highest[..., None]), 0.0).astype(
        jnp.bfloat16
    )
    total = jnp.sum(weights.astype(jnp.float32), axis=-1)
    summed = jnp.einsum("kqn,nkd->kqd", weights, value_rows, preferred_element_type=jnp.float32)
    return summed / total[..., None]


def on_device(held, norm_gain, w_qkv, q_gain, k_gain, w_out, lengths):
    micro = held.shape[1]
    rows = held.shape[2]
    width = held.shape[3]
    inner = HEADS * HEAD
    key_width = KV_HEADS * HEAD
    middle = rows // 2
    devices = lax.axis_size("dp")
    here = lax.axis_index("dp")
    total_tokens = rows * devices
    doc_most = min(4096, total_tokens // 2)
    reach = min(total_tokens, doc_most + middle)
    doc_lengths = lengths[0]
    resident = held[0].astype(jnp.float32).reshape(micro * rows, width)
    normed = rms_scale(resident, norm_gain[0]).astype(jnp.bfloat16)
    projected = jnp.dot(
        normed,
        lax.all_gather(w_qkv[0], "dp", axis=1, tiled=True),
        preferred_element_type=jnp.float32,
    ).reshape(micro, rows, inner + 2 * key_width)
    own_index = here * rows + jnp.arange(rows, dtype=jnp.int32)
    own_start = locate(own_index, doc_lengths)[1]
    places = own_index[None, :] - own_start
    queries = rotary(
        rms_scale(projected[..., :inner].reshape(micro, rows, HEADS, HEAD), q_gain[0]), places
    ).astype(jnp.bfloat16)
    keys = rotary(
        rms_scale(
            projected[..., inner : inner + key_width].reshape(micro, rows, KV_HEADS, HEAD),
            k_gain[0],
        ),
        places,
    ).astype(jnp.bfloat16)
    values = projected[..., inner + key_width :].astype(jnp.bfloat16)
    packed = jnp.concatenate([keys.reshape(micro, rows, key_width), values], axis=-1)
    gathered = lax.all_gather(packed, "dp", axis=1, tiled=True)
    latter_queries = queries[:, middle:]
    latter_index = own_index[middle:]
    group_index = jnp.stack([own_index[:middle], latter_index])
    group_doc = locate(group_index.reshape(-1), doc_lengths)[0].reshape(micro, 2, middle)
    arranged = jnp.stack([queries[:, :middle], latter_queries], axis=1)
    arranged = arranged.reshape(micro, 2, middle, KV_HEADS, GROUP, HEAD).transpose(0, 1, 3, 4, 2, 5)
    arranged = arranged.reshape(micro, 2, KV_HEADS, GROUP * middle, HEAD)
    row_index = jnp.tile(group_index, (1, GROUP))
    row_doc = jnp.tile(group_doc, (1, 1, GROUP))
    finished = []
    for which_micro in range(micro):
        for which_half in range(2):
            first = group_index[which_half, 0]
            key_first = jnp.clip(first + middle - reach, 0, total_tokens - reach)
            window = lax.dynamic_slice_in_dim(gathered[which_micro], key_first, reach, 0)
            key_index = key_first + jnp.arange(reach, dtype=jnp.int32)
            key_doc = locate(key_index, doc_lengths[which_micro : which_micro + 1])[0][0]
            key_part = window[:, :key_width].reshape(reach, KV_HEADS, HEAD)
            value_part = window[:, key_width:].reshape(reach, KV_HEADS, HEAD)
            allowed = (row_doc[which_micro, which_half][:, None] == key_doc[None, :]) & (
                row_index[which_half][:, None] >= key_index[None, :]
            )
            ratio = attend_rows(
                arranged[which_micro, which_half], key_part, value_part, allowed
            ).astype(jnp.bfloat16)
            finished.append(
                ratio.reshape(KV_HEADS, GROUP, middle, HEAD)
                .transpose(2, 0, 1, 3)
                .reshape(middle, inner)
            )
    former_part = jnp.stack(finished[0::2])
    latter_part = jnp.stack(finished[1::2])
    attended = jnp.concatenate([former_part, latter_part], axis=1).reshape(micro * rows, inner)
    mixed = jnp.dot(
        attended,
        lax.all_gather(w_out[0], "dp", axis=1, tiled=True),
        preferred_element_type=jnp.float32,
    )
    result = (resident + mixed).astype(jnp.bfloat16).reshape(1, micro, rows, width)
    return from_behind(result, "section", 1)


MIB = 1 << 20
VMEM = pl.BlockSpec(memory_space=pltpu.VMEM)
SMEM = pl.BlockSpec(memory_space=pltpu.SMEM)


def local_kernel(body, outs, inputs, scratch=(), flops=0, grant=24, scalars=1):
    moved = sum(math.prod(s.shape) * s.dtype.itemsize for s in (*outs, *inputs))
    return pl.pallas_call(
        body,
        out_shape=tuple(outs),
        in_specs=[SMEM] * scalars + [VMEM] * (len(inputs) - scalars),
        out_specs=tuple(VMEM for _ in outs),
        scratch_shapes=list(scratch),
        compiler_params=pltpu.CompilerParams(vmem_limit_bytes=grant * MIB),
        cost_estimate=pl.CostEstimate(flops=flops, bytes_accessed=moved, transcendentals=0),
    )(*inputs)


def project_kernel(
    normalise,
    merge,
    place_ref,
    *refs,
):
    if normalise:
        x_refs, refs = refs[:4], refs[4:]
        gain_ref, refs = refs[0], refs[1:]
    else:
        normed_in, refs = refs[0], refs[1:]
    w_own, w_partner, cos_ref, sin_ref, gains_ref = refs[:5]
    refs = refs[5:]
    if merge:
        before_ref, refs = refs[0], refs[1:]
        queries_ref, swap_ref, kv_ref, wide, full = refs
    elif normalise:
        out_ref, normed_ref, wide = refs
    line, column, core = place_ref[0], place_ref[1], place_ref[2]
    part = w_own.shape[1]
    chip_width = 2 * part
    if normalise:
        rows = x_refs[0].shape[0]
        for number, x_ref in enumerate(x_refs):
            x = x_ref[...].astype(jnp.float32)
            scale = lax.rsqrt(jnp.mean(x * x, axis=-1, keepdims=True) + EPSILON)
            normed_ref[number * rows : (number + 1) * rows, :] = (
                x * scale * gain_ref[...]
            ).astype(jnp.bfloat16)
        normed_in = normed_ref

    @pl.when(core == 0)
    def _():
        wide[:, :part] = w_own[...]
        wide[:, part:] = w_partner[...]

    @pl.when(core == 1)
    def _():
        wide[:, :part] = w_partner[...]
        wide[:, part:] = w_own[...]

    which = 1 - column if merge else column
    blocks = chip_width // HEAD
    total = normed_in.shape[0]
    step = total // 2
    for first in range(0, total, step):
        span = slice(first, first + step)
        projected = jnp.dot(
            normed_in[span, :], wide[...], preferred_element_type=jnp.float32
        )
        cosine = cos_ref[span, :]
        sine = sin_ref[span, :]
        for block in range(blocks):
            head = (line * 2 + which) * blocks + block
            is_value = head >= HEADS + KV_HEADS
            is_query = head < HEADS
            u = projected[:, block * HEAD : (block + 1) * HEAD]
            gain = jnp.where(is_query, gains_ref[0:1, :], gains_ref[1:2, :])
            v = u * lax.rsqrt(jnp.mean(u * u, axis=-1, keepdims=True) + EPSILON) * gain
            turned = v * cosine + pltpu.roll(v, HEAD // 2, 1) * sine
            done = jnp.where(is_value, u, turned).astype(jnp.bfloat16)
            if merge:
                start = pl.multiple_of(which * chip_width + block * HEAD, HEAD)
                full[span, pl.ds(start, HEAD)] = done
            else:
                out_ref[span, block * HEAD : (block + 1) * HEAD] = done
    if merge:
        own = pl.multiple_of(column * chip_width, HEAD)
        full[:, pl.ds(own, chip_width)] = before_ref[...]
        inner = queries_ref.shape[1]
        pair = swap_ref.shape[1]
        half = pair // 2

        turns = ((slice(0, step), slice(step, total)), (slice(step, total), slice(0, step)))

        @pl.when(line == 0)
        def _():
            queries_ref[...] = full[:, :inner]
            for there, here in turns:
                swap_ref[there, :] = full[here, inner : inner + pair]
            kv_ref[...] = jnp.zeros_like(kv_ref)

        @pl.when(line == 1)
        def _():
            left = inner - pair
            queries_ref[:, :pair] = jnp.zeros((total, pair), jnp.bfloat16)
            queries_ref[:, pair:] = full[:, :left]
            for there, here in turns:
                swap_ref[there, :half] = full[here, left : left + half]
                swap_ref[there, half:] = full[here, left + 2 * half : left + 3 * half]
            kv_ref[:, :half] = full[:, left + half : left + 2 * half]
            kv_ref[:, half:] = full[:, left + 3 * half : left + 4 * half]


def attend_kernel(place_ref, q_ref, swapped_ref, kv_ref, other_ref, bias_ref, out_ref):
    line = place_ref[0]
    pair = swapped_ref.shape[1]
    half = pair // 2
    rows = kv_ref.shape[0]
    heads = q_ref.shape[1] // HEAD
    shrink = math.log2(math.e) / math.sqrt(HEAD)
    keys = jnp.concatenate([kv_ref[:, :half], other_ref[:, :half]], axis=0)
    values = jnp.concatenate([kv_ref[:, half:], other_ref[:, half:]], axis=0)
    step = rows // 2
    for first in range(0, rows, step):
        span = slice(first, first + step)
        for head in range(heads):
            lanes = slice(head * HEAD, (head + 1) * HEAD)
            q = q_ref[span, lanes]
            if head < pair // HEAD:
                q = jnp.where(line == 1, swapped_ref[span, lanes], q)
            s = lax.dot_general(
                q, keys, (((1,), (1,)), ((), ())), preferred_element_type=jnp.float32
            )
            s = s + bias_ref[span, :]
            top = jnp.max(s, axis=-1, keepdims=True)
            weight = jnp.exp2((s - top) * shrink).astype(jnp.bfloat16)
            total = jnp.sum(weight.astype(jnp.float32), axis=-1, keepdims=True)
            summed = jnp.dot(weight, values, preferred_element_type=jnp.float32)
            out_ref[span, lanes] = (summed / total).astype(jnp.bfloat16)


def share_kernel(place_ref, a_ref, w0_ref, w1_ref, out_ref):
    core = place_ref[2]
    width = w0_ref.shape[1]
    rows = out_ref.shape[0]
    for turn, w_ref in enumerate((w0_ref, w1_ref)):
        start = pl.multiple_of((core ^ turn) * width, HEAD)
        out_ref[:, pl.ds(start, width)] = jnp.dot(
            a_ref[rows : 2 * rows, :], w_ref[...], preferred_element_type=jnp.float32
        ).astype(jnp.bfloat16)


def finish_kernel(
    relative, place_ref, a_ref, w0_ref, w1_ref, came_ref, x0_ref, x1_ref, own_ref, pair_ref
):
    chip = place_ref[0] * 2 + place_ref[1]
    core = place_ref[2]
    width = w0_ref.shape[1]
    rows = own_ref.shape[0]
    for turn, w_ref in enumerate((w0_ref, w1_ref)):
        start = pl.multiple_of((core ^ turn) * width, HEAD)
        mixed = jnp.dot(
            a_ref[: 2 * rows, :], w_ref[...], preferred_element_type=jnp.float32
        ) + came_ref[:, pl.ds(start, width)].astype(jnp.float32)
        where = pl.multiple_of((chip ^ relative) * 2 * width + start, HEAD)
        for number, (x_ref, out_ref) in enumerate(((x0_ref, own_ref), (x1_ref, pair_ref))):
            out_ref[:, pl.ds(start, width)] = (
                x_ref[:, pl.ds(where, width)].astype(jnp.float32)
                + mixed[number * rows : (number + 1) * rows, :]
            ).astype(jnp.bfloat16)


def gather_kernel(place_ref, *refs):
    out_ref = refs[-1]
    chip = place_ref[0] * 2 + place_ref[1]
    core = place_ref[2]
    for turn in range(2):
        for relative in range(4):
            piece = refs[turn * 4 + relative]
            width = piece.shape[1]
            start = pl.multiple_of((chip ^ relative) * width, HEAD)
            out_ref[core ^ turn, :, pl.ds(start, width)] = piece[...]


def on_chip_grid(held, norm_gain, w_qkv, q_gain, k_gain, w_out, lengths):
    micro, rows, width = held.shape[1:]
    devices = lax.axis_size("dp")
    sections = lax.axis_size("section")
    here = lax.axis_index("dp")
    line, column, core = here // 4, (here // 2) % 2, here % 2
    place = jnp.stack([line, column, core]).astype(jnp.int32)
    inner = w_out.shape[1]
    pair = KV_HEADS * HEAD

    def swap(value, bits):
        return lax.ppermute(value, "dp", [(i, i ^ bits) for i in range(devices)])

    def after(value, *others):
        return lax.optimization_barrier((value, *others))[0]

    kept = lax.dynamic_index_in_dim(held[0], core, 0, keepdims=False)
    given = lax.dynamic_index_in_dim(held[0], 1 - core, 0, keepdims=False)
    w_in = w_qkv[0]
    w_across = swap(w_in, 2)
    x_y = swap(kept, 4)
    x_yc = swap(given, 5)
    x_c = swap(given, 1)
    w_c = swap(w_in, 1)
    w_across_c = swap(w_across, 1)
    x_parts = (kept, x_c, x_y, x_yc)

    doc_lengths = lax.dynamic_slice_in_dim(lengths[0], core, 1, 0)
    steps = jnp.arange(rows, dtype=jnp.int32)

    def index_of(bits):
        return jnp.concatenate([(here ^ bit) * rows + steps for bit in bits])

    own_index = index_of((0, 1, 4, 5))
    key_index = index_of((0, 1, 4, 5, 2, 3, 6, 7))
    own_doc, own_start = (value[0] for value in locate(own_index, doc_lengths))
    key_doc = locate(key_index, doc_lengths)[0][0]
    allowed = (own_doc[:, None] == key_doc[None, :]) & (own_index[:, None] >= key_index[None, :])
    bias = jnp.where(allowed, 0.0, NEGATIVE).astype(jnp.float32)
    middle = HEAD // 2
    spacing = jnp.exp(jnp.arange(middle, dtype=jnp.float32) * (-2.0 * math.log(THETA) / HEAD))
    angle = (own_index - own_start).astype(jnp.float32)[:, None] * spacing
    cosine, sine = jnp.cos(angle), jnp.sin(angle)
    cosine = jnp.concatenate([cosine, cosine], axis=-1)
    sine = jnp.concatenate([-sine, sine], axis=-1)
    gains = jnp.concatenate([q_gain, k_gain], axis=0)

    own_rows = micro * 2 * rows
    part = w_in.shape[1]
    bf16 = jnp.bfloat16
    shape = jax.ShapeDtypeStruct
    flops = 2 * own_rows * width * 2 * part
    near, normed = local_kernel(
        functools.partial(project_kernel, True, False),
        [shape((own_rows, 2 * part), bf16), shape((own_rows, width), bf16)],
        [place, *x_parts, norm_gain, w_in, w_c, cosine, sine, gains],
        [pltpu.VMEM((width, 2 * part), bf16)],
        flops,
    )
    queries, swapping, kv = local_kernel(
        functools.partial(project_kernel, False, True),
        [shape((own_rows, inner // 2), bf16), shape((own_rows, pair), bf16), shape((own_rows, pair), bf16)],
        [place, normed, w_across, w_across_c, cosine, sine, gains, near],
        [pltpu.VMEM((width, 2 * part), bf16), pltpu.VMEM((own_rows, 4 * part), bf16)],
        flops,
    )
    swapped = swap(swapping, 4)
    kv = jnp.where(line == 0, swapped, kv)
    kv_other = swap(kv, 2)

    w_o = w_out[0]
    half = inner // 2
    o_here = lax.dynamic_slice_in_dim(w_o, line * half, half, 0)
    o_there = lax.dynamic_slice_in_dim(w_o, (1 - line) * half, half, 0)
    o_y = swap(after(o_there, x_y, x_yc), 4)
    o_x = swap(after(o_here, w_across), 2)
    o_xy = swap(after(o_y, kv_other), 2)
    out_pieces = [(value, swap(value, 1)) for value in (o_here, o_x, o_y, o_xy)]

    (attended,) = local_kernel(
        attend_kernel,
        [shape((own_rows, half), bf16)],
        [place, queries, swapped, kv, kv_other, bias],
        flops=4 * own_rows * 2 * own_rows * half,
    )

    chunk = 2 * w_o.shape[1]
    came = {}
    for relative in (0, 1, 2, 3):
        (share,) = local_kernel(
            share_kernel,
            [shape((own_rows // 2, chunk), bf16)],
            [place, attended, *out_pieces[relative]],
            flops=own_rows * half * chunk,
        )
        came[relative ^ 2] = swap(share, 4)
    ring = [
        (s * devices + i, (s + 1) % sections * devices + i)
        for s in range(sections)
        for i in range(devices)
    ]
    cross = [(source, target ^ 1) for source, target in ring]
    arrived = {}
    for relative in (2, 3, 0, 1):
        own, other = local_kernel(
            functools.partial(finish_kernel, relative),
            [shape((rows, chunk), bf16)] * 2,
            [place, attended, *out_pieces[relative], came[relative], kept, x_c],
            flops=own_rows * half * chunk,
        )
        arrived[0, relative] = lax.ppermute(own, ("section", "dp"), ring)
        arrived[1, relative] = lax.ppermute(other, ("section", "dp"), cross)
    (result,) = local_kernel(
        gather_kernel,
        [shape((micro, rows, width), bf16)],
        [place, *[arrived[turn, relative] for turn in range(2) for relative in range(4)]],
    )
    return result[None]


def solution(mesh):
    devices = mesh.shape["dp"]

    def body(held, norm_gain, w_qkv, q_gain, k_gain, w_out, lengths):
        paired = KV_HEADS == 2 and HEADS == KV_HEADS * GROUP and held.shape[1] == 2
        whole_heads = (2 * w_qkv.shape[2]) % HEAD == 0
        form = on_chip_grid if devices == 8 and paired and whole_heads else on_device
        return form(held, norm_gain, w_qkv, q_gain, k_gain, w_out, lengths)

    in_specs = (
        P("section", None, "dp", None),
        P("section", None),
        P("section", None, "dp"),
        P("section", None),
        P("section", None),
        P("section", None, "dp"),
        P("section", None, None),
    )
    out_specs = P("section", None, "dp", None)
    return jax.shard_map(
        body, mesh=mesh, in_specs=in_specs, out_specs=out_specs, check_vma=False
    )
```

```python
import functools
import math

import jax
import jax.numpy as jnp
from jax import lax
from jax.experimental import pallas as pl
from jax.experimental.pallas import tpu as pltpu
from jax.sharding import PartitionSpec as P

HEADS = 16
KV_HEADS = 2
HEAD = 128
GROUP = 8


EPSILON = 1e-06
THETA = 1000000.0
NEGATIVE = -1e30


def from_behind(value, axis, steps):
    count = lax.axis_size(axis)
    pairs = [(source, (source + steps) % count) for source in range(count)]
    return lax.ppermute(value, axis, pairs)


def rms_scale(values, gain):
    return values * lax.rsqrt(jnp.mean(values * values, axis=-1, keepdims=True) + EPSILON) * gain


def rotary(values, places):
    width = values.shape[-1]
    middle = width // 2
    spacing = jnp.exp(jnp.arange(middle, dtype=jnp.float32) * (-2.0 * math.log(THETA) / width))
    angle = places.astype(jnp.float32)[..., None] * spacing
    cosine = jnp.cos(angle)[..., None, :]
    sine = jnp.sin(angle)[..., None, :]
    former = values[..., :middle]
    latter = values[..., middle:]
    return jnp.concatenate(
        [former * cosine - latter * sine, latter * cosine + former * sine], axis=-1
    )


def locate(positions, doc_lengths):
    ends = jnp.cumsum(doc_lengths, axis=-1)
    before = (ends[:, None, :] <= positions[None, :, None]).astype(jnp.int32)
    return (jnp.sum(before, axis=-1), jnp.sum(before * doc_lengths[:, None, :], axis=-1))


def attend_rows(query_rows, key_rows, value_rows, allowed):
    scores = jnp.einsum(
        "kqd,nkd->kqn", query_rows, key_rows, preferred_element_type=jnp.float32
    ) / math.sqrt(HEAD)
    highest = jnp.max(jnp.where(allowed[None], scores, NEGATIVE), axis=-1)
    weights = jnp.where(allowed[None], jnp.exp(scores - highest[..., None]), 0.0).astype(
        jnp.bfloat16
    )
    total = jnp.sum(weights.astype(jnp.float32), axis=-1)
    summed = jnp.einsum("kqn,nkd->kqd", weights, value_rows, preferred_element_type=jnp.float32)
    return summed / total[..., None]


def on_device(held, norm_gain, w_qkv, q_gain, k_gain, w_out, lengths):
    micro = held.shape[1]
    rows = held.shape[2]
    width = held.shape[3]
    inner = HEADS * HEAD
    key_width = KV_HEADS * HEAD
    middle = rows // 2
    devices = lax.axis_size("dp")
    here = lax.axis_index("dp")
    total_tokens = rows * devices
    doc_most = min(4096, total_tokens // 2)
    reach = min(total_tokens, doc_most + middle)
    doc_lengths = lengths[0]
    resident = held[0].astype(jnp.float32).reshape(micro * rows, width)
    normed = rms_scale(resident, norm_gain[0]).astype(jnp.bfloat16)
    projected = jnp.dot(
        normed,
        lax.all_gather(w_qkv[0], "dp", axis=1, tiled=True),
        preferred_element_type=jnp.float32,
    ).reshape(micro, rows, inner + 2 * key_width)
    own_index = here * rows + jnp.arange(rows, dtype=jnp.int32)
    own_start = locate(own_index, doc_lengths)[1]
    places = own_index[None, :] - own_start
    queries = rotary(
        rms_scale(projected[..., :inner].reshape(micro, rows, HEADS, HEAD), q_gain[0]), places
    ).astype(jnp.bfloat16)
    keys = rotary(
        rms_scale(
            projected[..., inner : inner + key_width].reshape(micro, rows, KV_HEADS, HEAD),
            k_gain[0],
        ),
        places,
    ).astype(jnp.bfloat16)
    values = projected[..., inner + key_width :].astype(jnp.bfloat16)
    packed = jnp.concatenate([keys.reshape(micro, rows, key_width), values], axis=-1)
    gathered = lax.all_gather(packed, "dp", axis=1, tiled=True)
    latter_queries = queries[:, middle:]
    latter_index = own_index[middle:]
    group_index = jnp.stack([own_index[:middle], latter_index])
    group_doc = locate(group_index.reshape(-1), doc_lengths)[0].reshape(micro, 2, middle)
    arranged = jnp.stack([queries[:, :middle], latter_queries], axis=1)
    arranged = arranged.reshape(micro, 2, middle, KV_HEADS, GROUP, HEAD).transpose(0, 1, 3, 4, 2, 5)
    arranged = arranged.reshape(micro, 2, KV_HEADS, GROUP * middle, HEAD)
    row_index = jnp.tile(group_index, (1, GROUP))
    row_doc = jnp.tile(group_doc, (1, 1, GROUP))
    finished = []
    for which_micro in range(micro):
        for which_half in range(2):
            first = group_index[which_half, 0]
            key_first = jnp.clip(first + middle - reach, 0, total_tokens - reach)
            window = lax.dynamic_slice_in_dim(gathered[which_micro], key_first, reach, 0)
            key_index = key_first + jnp.arange(reach, dtype=jnp.int32)
            key_doc = locate(key_index, doc_lengths[which_micro : which_micro + 1])[0][0]
            key_part = window[:, :key_width].reshape(reach, KV_HEADS, HEAD)
            value_part = window[:, key_width:].reshape(reach, KV_HEADS, HEAD)
            allowed = (row_doc[which_micro, which_half][:, None] == key_doc[None, :]) & (
                row_index[which_half][:, None] >= key_index[None, :]
            )
            ratio = attend_rows(
                arranged[which_micro, which_half], key_part, value_part, allowed
            ).astype(jnp.bfloat16)
            finished.append(
                ratio.reshape(KV_HEADS, GROUP, middle, HEAD)
                .transpose(2, 0, 1, 3)
                .reshape(middle, inner)
            )
    former_part = jnp.stack(finished[0::2])
    latter_part = jnp.stack(finished[1::2])
    attended = jnp.concatenate([former_part, latter_part], axis=1).reshape(micro * rows, inner)
    mixed = jnp.dot(
        attended,
        lax.all_gather(w_out[0], "dp", axis=1, tiled=True),
        preferred_element_type=jnp.float32,
    )
    result = (resident + mixed).astype(jnp.bfloat16).reshape(1, micro, rows, width)
    return from_behind(result, "section", 1)


MIB = 1 << 20
VMEM = pl.BlockSpec(memory_space=pltpu.VMEM)
SMEM = pl.BlockSpec(memory_space=pltpu.SMEM)


def local_kernel(body, outs, inputs, scratch=(), flops=0, grant=24, scalars=1):
    moved = sum(math.prod(s.shape) * s.dtype.itemsize for s in (*outs, *inputs))
    return pl.pallas_call(
        body,
        out_shape=tuple(outs),
        in_specs=[SMEM] * scalars + [VMEM] * (len(inputs) - scalars),
        out_specs=tuple(VMEM for _ in outs),
        scratch_shapes=list(scratch),
        compiler_params=pltpu.CompilerParams(vmem_limit_bytes=grant * MIB),
        cost_estimate=pl.CostEstimate(flops=flops, bytes_accessed=moved, transcendentals=0),
    )(*inputs)


def project_kernel(
    normalise,
    merge,
    place_ref,
    *refs,
):
    if normalise:
        x_refs, refs = refs[:4], refs[4:]
        gain_ref, refs = refs[0], refs[1:]
    else:
        normed_in, refs = refs[0], refs[1:]
    w_own, w_partner, cos_ref, sin_ref, gains_ref = refs[:5]
    refs = refs[5:]
    if merge:
        before_ref, refs = refs[0], refs[1:]
        queries_ref, swap_ref, kv_ref, wide, full = refs
    elif normalise:
        out_ref, normed_ref, wide = refs
    line, column, core = place_ref[0], place_ref[1], place_ref[2]
    part = w_own.shape[0]
    chip_width = 2 * part
    if normalise:
        rows = x_refs[0].shape[1]
        for number, x_ref in enumerate(x_refs):
            x = x_ref[core].astype(jnp.float32)
            scale = lax.rsqrt(jnp.mean(x * x, axis=-1, keepdims=True) + EPSILON)
            normed_ref[number * rows : (number + 1) * rows, :] = (
                x * scale * gain_ref[...]
            ).astype(jnp.bfloat16)
        normed_in = normed_ref

    @pl.when(core == 0)
    def _():
        wide[:part, :] = w_own[...]
        wide[part:, :] = w_partner[...]

    @pl.when(core == 1)
    def _():
        wide[:part, :] = w_partner[...]
        wide[part:, :] = w_own[...]

    which = 1 - column if merge else column
    blocks = chip_width // HEAD
    total = normed_in.shape[0]
    step = total // 2
    for first in range(0, total, step):
        span = slice(first, first + step)
        projected = lax.dot_general(
            normed_in[span, :],
            wide[...],
            (((1,), (1,)), ((), ())),
            preferred_element_type=jnp.float32,
        )
        cosine = cos_ref[span, :]
        sine = sin_ref[span, :]
        for block in range(blocks):
            head = (line * 2 + which) * blocks + block
            is_value = head >= HEADS + KV_HEADS
            is_query = head < HEADS
            u = projected[:, block * HEAD : (block + 1) * HEAD]
            gain = jnp.where(is_query, gains_ref[0:1, :], gains_ref[1:2, :])
            v = u * lax.rsqrt(jnp.mean(u * u, axis=-1, keepdims=True) + EPSILON) * gain
            turned = v * cosine + pltpu.roll(v, HEAD // 2, 1) * sine
            done = jnp.where(is_value, u, turned).astype(jnp.bfloat16)
            if merge:
                start = pl.multiple_of(which * chip_width + block * HEAD, HEAD)
                full[span, pl.ds(start, HEAD)] = done
            else:
                out_ref[span, block * HEAD : (block + 1) * HEAD] = done
    if merge:
        own = pl.multiple_of(column * chip_width, HEAD)
        full[:, pl.ds(own, chip_width)] = before_ref[...]
        inner = queries_ref.shape[1]
        pair = swap_ref.shape[1]
        half = pair // 2

        turns = ((slice(0, step), slice(step, total)), (slice(step, total), slice(0, step)))

        @pl.when(line == 0)
        def _():
            queries_ref[...] = full[:, :inner]
            for there, here in turns:
                swap_ref[there, :] = full[here, inner : inner + pair]
            kv_ref[...] = jnp.zeros_like(kv_ref)

        @pl.when(line == 1)
        def _():
            left = inner - pair
            queries_ref[:, :pair] = jnp.zeros((total, pair), jnp.bfloat16)
            queries_ref[:, pair:] = full[:, :left]
            for there, here in turns:
                swap_ref[there, :half] = full[here, left : left + half]
                swap_ref[there, half:] = full[here, left + 2 * half : left + 3 * half]
            kv_ref[:, :half] = full[:, left + half : left + 2 * half]
            kv_ref[:, half:] = full[:, left + 3 * half : left + 4 * half]


def attend_kernel(part, place_ref, q_ref, swapped_ref, kv_ref, far0_ref, far1_ref, bias_ref, out_ref):
    line = place_ref[0]
    pair = swapped_ref.shape[1]
    half = pair // 2
    rows = out_ref.shape[0]
    heads = q_ref.shape[1] // HEAD
    shrink = math.log2(math.e) / math.sqrt(HEAD)
    near = jnp.where(line == 0, swapped_ref[...], kv_ref[...])
    far = jnp.where(line == 0, far0_ref[...], far1_ref[...])
    keys = jnp.concatenate([near[:, :half], far[:, :half]], axis=0)
    values = jnp.concatenate([near[:, half:], far[:, half:]], axis=0)
    span = slice(part * rows, (part + 1) * rows)
    for head in range(heads):
        lanes = slice(head * HEAD, (head + 1) * HEAD)
        q = q_ref[span, lanes]
        if head < pair // HEAD:
            q = jnp.where(line == 1, swapped_ref[span, lanes], q)
        s = lax.dot_general(
            q, keys, (((1,), (1,)), ((), ())), preferred_element_type=jnp.float32
        )
        s = s + bias_ref[span, :]
        top = jnp.max(s, axis=-1, keepdims=True)
        weight = jnp.exp2((s - top) * shrink).astype(jnp.bfloat16)
        total = jnp.sum(weight.astype(jnp.float32), axis=-1, keepdims=True)
        summed = jnp.dot(weight, values, preferred_element_type=jnp.float32)
        out_ref[:, lanes] = (summed / total).astype(jnp.bfloat16)


def share_kernel(place_ref, a_ref, w0_ref, w1_ref, out_ref):
    core = place_ref[2]
    width = w0_ref.shape[1]
    for turn, w_ref in enumerate((w0_ref, w1_ref)):
        start = pl.multiple_of((core ^ turn) * width, HEAD)
        out_ref[:, pl.ds(start, width)] = jnp.dot(
            a_ref[...], w_ref[...], preferred_element_type=jnp.float32
        ).astype(jnp.bfloat16)


def finish_kernel(
    relative, place_ref, a_ref, w0_ref, w1_ref, came_ref, x0_ref, x1_ref, own_ref, pair_ref
):
    chip = place_ref[0] * 2 + place_ref[1]
    core = place_ref[2]
    width = w0_ref.shape[1]
    rows = own_ref.shape[0]
    for turn, w_ref in enumerate((w0_ref, w1_ref)):
        start = pl.multiple_of((core ^ turn) * width, HEAD)
        mixed = jnp.dot(
            a_ref[...], w_ref[...], preferred_element_type=jnp.float32
        ) + came_ref[:, pl.ds(start, width)].astype(jnp.float32)
        where = pl.multiple_of((chip ^ relative) * 2 * width + start, HEAD)
        for number, (x_ref, out_ref) in enumerate(((x0_ref, own_ref), (x1_ref, pair_ref))):
            out_ref[:, pl.ds(start, width)] = (
                x_ref[core, :, pl.ds(where, width)].astype(jnp.float32)
                + mixed[number * rows : (number + 1) * rows, :]
            ).astype(jnp.bfloat16)


def gather_kernel(place_ref, *refs):
    out_ref = refs[-1]
    chip = place_ref[0] * 2 + place_ref[1]
    core = place_ref[2]
    for turn in range(2):
        for relative in range(4):
            piece = refs[turn * 4 + relative]
            width = piece.shape[1]
            start = pl.multiple_of((chip ^ relative) * width, HEAD)
            out_ref[core ^ turn, :, pl.ds(start, width)] = piece[...]


def on_chip_grid(held, norm_gain, w_qkv, q_gain, k_gain, w_out, lengths):
    micro, rows, width = held.shape[1:]
    devices = lax.axis_size("dp")
    sections = lax.axis_size("section")
    here = lax.axis_index("dp")
    line, column, core = here // 4, (here // 2) % 2, here % 2
    place = jnp.stack([line, column, core]).astype(jnp.int32)
    inner = w_out.shape[1]
    pair = KV_HEADS * HEAD

    def swap(value, bits, among=range(8)):
        return lax.ppermute(value, "dp", [(i, i ^ bits) for i in among])

    def after(value, *others):
        return lax.optimization_barrier((value, *others))[0]

    kept = held[0]
    w_in = w_qkv[0].T
    w_across = swap(w_in, 2)
    x_y = swap(kept, 4)
    x_c = swap(kept, 1)
    w_c = swap(w_in, 1)
    x_yc = swap(x_y, 1)
    x_parts = (kept, x_c, x_y, x_yc)

    w_o = w_out[0]
    half = inner // 2
    o_here = lax.dynamic_slice_in_dim(w_o, line * half, half, 0)
    o_there = lax.dynamic_slice_in_dim(w_o, (1 - line) * half, half, 0)
    o_here_c = swap(o_here, 1)

    doc_lengths = lax.dynamic_slice_in_dim(lengths[0], core, 1, 0)
    steps = jnp.arange(rows, dtype=jnp.int32)

    def index_of(bits):
        return jnp.concatenate([(here ^ bit) * rows + steps for bit in bits])

    own_index = index_of((0, 1, 4, 5))
    key_index = index_of((0, 1, 4, 5, 2, 3, 6, 7))
    own_doc, own_start = (value[0] for value in locate(own_index, doc_lengths))
    key_doc = locate(key_index, doc_lengths)[0][0]
    allowed = (own_doc[:, None] == key_doc[None, :]) & (own_index[:, None] >= key_index[None, :])
    bias = jnp.where(allowed, 0.0, NEGATIVE).astype(jnp.float32)
    middle = HEAD // 2
    spacing = jnp.exp(jnp.arange(middle, dtype=jnp.float32) * (-2.0 * math.log(THETA) / HEAD))
    angle = (own_index - own_start).astype(jnp.float32)[:, None] * spacing
    cosine, sine = jnp.cos(angle), jnp.sin(angle)
    cosine = jnp.concatenate([cosine, cosine], axis=-1)
    sine = jnp.concatenate([-sine, sine], axis=-1)
    gains = jnp.concatenate([q_gain, k_gain], axis=0)

    own_rows = micro * 2 * rows
    part = w_in.shape[0]
    bf16 = jnp.bfloat16
    shape = jax.ShapeDtypeStruct
    flops = 2 * own_rows * width * 2 * part
    ready = after(norm_gain, bias, o_here, o_there, o_here_c)
    near, normed = local_kernel(
        functools.partial(project_kernel, True, False),
        [shape((own_rows, 2 * part), bf16), shape((own_rows, width), bf16)],
        [place, *x_parts, ready, w_in, w_c, cosine, sine, gains],
        [pltpu.VMEM((2 * part, width), bf16)],
        flops,
    )
    o_y = swap(after(o_there, x_y), 4)
    w_across_c = swap(after(w_across, near), 1)
    o_x = swap(after(o_here, w_across), 2)
    queries, swapping, kv = local_kernel(
        functools.partial(project_kernel, False, True),
        [shape((own_rows, inner // 2), bf16), shape((own_rows, pair), bf16), shape((own_rows, pair), bf16)],
        [place, normed, w_across, w_across_c, cosine, sine, gains, near],
        [pltpu.VMEM((2 * part, width), bf16), pltpu.VMEM((own_rows, 4 * part), bf16)],
        flops,
    )
    swapped = swap(swapping, 4)
    far1 = swap(kv, 2, range(4, 8))
    far0 = swap(swapped, 2, range(4))
    o_y_c = swap(after(o_y, swapping), 1)

    def attend(part, *others):
        return local_kernel(
            functools.partial(attend_kernel, part),
            [shape((own_rows // 2, half), bf16)],
            [place, queries, swapped, kv, far0, far1, after(bias, *others)],
            flops=2 * own_rows * 2 * own_rows * half,
        )[0]

    attended_there = attend(1)
    o_xy = swap(after(o_y, far0, far1), 2)

    chunk = 2 * w_o.shape[1]
    came = {}

    def share(relative, rows_there, *pieces):
        (value,) = local_kernel(
            share_kernel,
            [shape((own_rows // 2, chunk), bf16)],
            [place, rows_there, *pieces],
            flops=own_rows * half * chunk,
        )
        came[relative ^ 2] = swap(value, 4)
        return value

    share(0, attended_there, o_here, o_here_c)
    second = share(2, attended_there, o_y, o_y_c)
    attended_here = attend(0, second)
    attended_there = after(attended_there, attended_here)
    o_x_c = swap(after(o_x, attended_here), 1)
    third = share(1, attended_there, o_x, o_x_c)
    o_xy_c = swap(after(o_xy, third), 1)
    share(3, attended_there, o_xy, o_xy_c)
    out_pieces = [(o_here, o_here_c), (o_x, o_x_c), (o_y, o_y_c), (o_xy, o_xy_c)]
    ring = [
        (s * devices + i, (s + 1) % sections * devices + i)
        for s in range(sections)
        for i in range(devices)
    ]
    cross = [(source, target ^ 1) for source, target in ring]
    arrived = {}
    for relative in (2, 0, 3, 1):
        own, other = local_kernel(
            functools.partial(finish_kernel, relative),
            [shape((rows, chunk), bf16)] * 2,
            [place, attended_here, *out_pieces[relative], came[relative], kept, x_c],
            flops=own_rows * half * chunk,
        )
        arrived[0, relative] = lax.ppermute(own, ("section", "dp"), ring)
        arrived[1, relative] = lax.ppermute(other, ("section", "dp"), cross)
    (result,) = local_kernel(
        gather_kernel,
        [shape((micro, rows, width), bf16)],
        [place, *[arrived[turn, relative] for turn in range(2) for relative in range(4)]],
    )
    return result[None]


def solution(mesh):
    devices = mesh.shape["dp"]

    def body(held, norm_gain, w_qkv, q_gain, k_gain, w_out, lengths):
        paired = KV_HEADS == 2 and HEADS == KV_HEADS * GROUP and held.shape[1] == 2
        whole_heads = (2 * w_qkv.shape[2]) % HEAD == 0
        form = on_chip_grid if devices == 8 and paired and whole_heads else on_device
        return form(held, norm_gain, w_qkv, q_gain, k_gain, w_out, lengths)

    in_specs = (
        P("section", None, "dp", None),
        P("section", None),
        P("section", None, "dp"),
        P("section", None),
        P("section", None),
        P("section", None, "dp"),
        P("section", None, None),
    )
    out_specs = P("section", None, "dp", None)
    return jax.shard_map(
        body, mesh=mesh, in_specs=in_specs, out_specs=out_specs, check_vma=False
    )
```

```python
import functools
import math

import jax
import jax.numpy as jnp
from jax import lax
from jax.experimental import pallas as pl
from jax.experimental.pallas import tpu as pltpu
from jax.sharding import PartitionSpec as P

HEADS = 16
KV_HEADS = 2
HEAD = 128
GROUP = 8


EPSILON = 1e-06
THETA = 1000000.0
NEGATIVE = -1e30


def from_behind(value, axis, steps):
    count = lax.axis_size(axis)
    pairs = [(source, (source + steps) % count) for source in range(count)]
    return lax.ppermute(value, axis, pairs)


def rms_scale(values, gain):
    return values * lax.rsqrt(jnp.mean(values * values, axis=-1, keepdims=True) + EPSILON) * gain


def rotary(values, places):
    width = values.shape[-1]
    middle = width // 2
    spacing = jnp.exp(jnp.arange(middle, dtype=jnp.float32) * (-2.0 * math.log(THETA) / width))
    angle = places.astype(jnp.float32)[..., None] * spacing
    cosine = jnp.cos(angle)[..., None, :]
    sine = jnp.sin(angle)[..., None, :]
    former = values[..., :middle]
    latter = values[..., middle:]
    return jnp.concatenate(
        [former * cosine - latter * sine, latter * cosine + former * sine], axis=-1
    )


def locate(positions, doc_lengths):
    ends = jnp.cumsum(doc_lengths, axis=-1)
    before = (ends[:, None, :] <= positions[None, :, None]).astype(jnp.int32)
    return (jnp.sum(before, axis=-1), jnp.sum(before * doc_lengths[:, None, :], axis=-1))


def attend_rows(query_rows, key_rows, value_rows, allowed):
    scores = jnp.einsum(
        "kqd,nkd->kqn", query_rows, key_rows, preferred_element_type=jnp.float32
    ) / math.sqrt(HEAD)
    highest = jnp.max(jnp.where(allowed[None], scores, NEGATIVE), axis=-1)
    weights = jnp.where(allowed[None], jnp.exp(scores - highest[..., None]), 0.0).astype(
        jnp.bfloat16
    )
    total = jnp.sum(weights.astype(jnp.float32), axis=-1)
    summed = jnp.einsum("kqn,nkd->kqd", weights, value_rows, preferred_element_type=jnp.float32)
    return summed / total[..., None]


def on_device(held, norm_gain, w_qkv, q_gain, k_gain, w_out, lengths):
    micro = held.shape[1]
    rows = held.shape[2]
    width = held.shape[3]
    inner = HEADS * HEAD
    key_width = KV_HEADS * HEAD
    middle = rows // 2
    devices = lax.axis_size("dp")
    here = lax.axis_index("dp")
    total_tokens = rows * devices
    doc_most = min(4096, total_tokens // 2)
    reach = min(total_tokens, doc_most + middle)
    doc_lengths = lengths[0]
    resident = held[0].astype(jnp.float32).reshape(micro * rows, width)
    normed = rms_scale(resident, norm_gain[0]).astype(jnp.bfloat16)
    projected = jnp.dot(
        normed,
        lax.all_gather(w_qkv[0], "dp", axis=1, tiled=True),
        preferred_element_type=jnp.float32,
    ).reshape(micro, rows, inner + 2 * key_width)
    own_index = here * rows + jnp.arange(rows, dtype=jnp.int32)
    own_start = locate(own_index, doc_lengths)[1]
    places = own_index[None, :] - own_start
    queries = rotary(
        rms_scale(projected[..., :inner].reshape(micro, rows, HEADS, HEAD), q_gain[0]), places
    ).astype(jnp.bfloat16)
    keys = rotary(
        rms_scale(
            projected[..., inner : inner + key_width].reshape(micro, rows, KV_HEADS, HEAD),
            k_gain[0],
        ),
        places,
    ).astype(jnp.bfloat16)
    values = projected[..., inner + key_width :].astype(jnp.bfloat16)
    packed = jnp.concatenate([keys.reshape(micro, rows, key_width), values], axis=-1)
    gathered = lax.all_gather(packed, "dp", axis=1, tiled=True)
    latter_queries = queries[:, middle:]
    latter_index = own_index[middle:]
    group_index = jnp.stack([own_index[:middle], latter_index])
    group_doc = locate(group_index.reshape(-1), doc_lengths)[0].reshape(micro, 2, middle)
    arranged = jnp.stack([queries[:, :middle], latter_queries], axis=1)
    arranged = arranged.reshape(micro, 2, middle, KV_HEADS, GROUP, HEAD).transpose(0, 1, 3, 4, 2, 5)
    arranged = arranged.reshape(micro, 2, KV_HEADS, GROUP * middle, HEAD)
    row_index = jnp.tile(group_index, (1, GROUP))
    row_doc = jnp.tile(group_doc, (1, 1, GROUP))
    finished = []
    for which_micro in range(micro):
        for which_half in range(2):
            first = group_index[which_half, 0]
            key_first = jnp.clip(first + middle - reach, 0, total_tokens - reach)
            window = lax.dynamic_slice_in_dim(gathered[which_micro], key_first, reach, 0)
            key_index = key_first + jnp.arange(reach, dtype=jnp.int32)
            key_doc = locate(key_index, doc_lengths[which_micro : which_micro + 1])[0][0]
            key_part = window[:, :key_width].reshape(reach, KV_HEADS, HEAD)
            value_part = window[:, key_width:].reshape(reach, KV_HEADS, HEAD)
            allowed = (row_doc[which_micro, which_half][:, None] == key_doc[None, :]) & (
                row_index[which_half][:, None] >= key_index[None, :]
            )
            ratio = attend_rows(
                arranged[which_micro, which_half], key_part, value_part, allowed
            ).astype(jnp.bfloat16)
            finished.append(
                ratio.reshape(KV_HEADS, GROUP, middle, HEAD)
                .transpose(2, 0, 1, 3)
                .reshape(middle, inner)
            )
    former_part = jnp.stack(finished[0::2])
    latter_part = jnp.stack(finished[1::2])
    attended = jnp.concatenate([former_part, latter_part], axis=1).reshape(micro * rows, inner)
    mixed = jnp.dot(
        attended,
        lax.all_gather(w_out[0], "dp", axis=1, tiled=True),
        preferred_element_type=jnp.float32,
    )
    result = (resident + mixed).astype(jnp.bfloat16).reshape(1, micro, rows, width)
    return from_behind(result, "section", 1)


MIB = 1 << 20
VMEM = pl.BlockSpec(memory_space=pltpu.VMEM)
SMEM = pl.BlockSpec(memory_space=pltpu.SMEM)


def local_kernel(body, outs, inputs, scratch=(), flops=0, grant=24, scalars=1):
    moved = sum(math.prod(s.shape) * s.dtype.itemsize for s in (*outs, *inputs))
    return pl.pallas_call(
        body,
        out_shape=tuple(outs),
        in_specs=[SMEM] * scalars + [VMEM] * (len(inputs) - scalars),
        out_specs=tuple(VMEM for _ in outs),
        scratch_shapes=list(scratch),
        compiler_params=pltpu.CompilerParams(vmem_limit_bytes=grant * MIB),
        cost_estimate=pl.CostEstimate(flops=flops, bytes_accessed=moved, transcendentals=0),
    )(*inputs)


def prepare_kernel(
    here_ref,
    lengths_ref,
    spacing_ref,
    w_ref,
    place_ref,
    bias_ref,
    cos_ref,
    sin_ref,
    here_out,
    there_out,
):
    here = here_ref[0]
    line, column, core = here >> 2, (here >> 1) & 1, here & 1
    chip = here >> 1
    half = here_out.shape[0]
    here_out[...] = w_ref[pl.ds(pl.multiple_of(line * half, half), half), :]
    there_out[...] = w_ref[pl.ds(pl.multiple_of((1 - line) * half, half), half), :]
    documents = lengths_ref.shape[1]
    sizes = [lengths_ref[core, j] for j in range(documents)]
    ends = [sizes[0]]
    for size in sizes[1:]:
        ends.append(ends[-1] + size)

    def locate_in(index):
        number = jnp.zeros_like(index)
        start = jnp.zeros_like(index)
        for end, size in zip(ends, sizes):
            past = (end <= index).astype(jnp.int32)
            number = number + past
            start = start + past * size
        return number, start

    rows = cos_ref.shape[0] // 4
    lane = lax.broadcasted_iota(jnp.int32, (1, rows), 1)
    keys = []
    for bits in (0, 1, 4, 5, 2, 3, 6, 7):
        index = (here ^ bits) * rows + lane
        keys.append((index, locate_in(index)[0]))
    first_half = lax.broadcasted_iota(jnp.int32, (rows, HEAD), 1) < HEAD // 2
    for block, bits in enumerate((0, 1, 4, 5)):
        span = slice(block * rows, (block + 1) * rows)
        index = (here ^ bits) * rows + lax.broadcasted_iota(jnp.int32, (rows, HEAD), 0)
        number, start = locate_in(index)
        angle = (index - start).astype(jnp.float32) * spacing_ref[...]
        sine = jnp.sin(angle)
        cos_ref[span, :] = jnp.cos(angle)
        sin_ref[span, :] = jnp.where(first_half, -sine, sine)
        for other, (key_index, key_number) in enumerate(keys):
            allowed = (number[:, :1] == key_number) & (index[:, :1] >= key_index)
            bias_ref[span, other * rows : (other + 1) * rows] = jnp.where(
                allowed, 0.0, NEGATIVE
            ).astype(jnp.float32)

    def number_at(index):
        number = jnp.int32(0)
        for end in ends:
            number = number + jnp.where(end <= index, 1, 0)
        return number

    place_ref[0] = line
    place_ref[1] = column
    place_ref[2] = core
    for row, row_bits in enumerate((0, 2)):
        row_chip = chip ^ row_bits
        for key, key_bits in enumerate((0, 2, 1, 3)):
            key_chip = chip ^ key_bits
            shares = number_at(key_chip * 2 * rows + 2 * rows - 1) >= number_at(row_chip * 2 * rows)
            meets = (key_chip == row_chip) | ((key_chip < row_chip) & shares)
            place_ref[3 + 4 * row + key] = jnp.where(meets, 1, 0)


def project_block(projected, head, cosine, sine, gains_ref):
    is_value = head >= HEADS + KV_HEADS
    is_query = head < HEADS
    gain = jnp.where(is_query, gains_ref[0][...], gains_ref[1][...])
    scale = lax.rsqrt(jnp.mean(projected * projected, axis=-1, keepdims=True) + EPSILON)
    v = projected * scale * gain
    turned = v * cosine + pltpu.roll(v, HEAD // 2, 1) * sine
    return jnp.where(is_value, projected, turned).astype(jnp.bfloat16)


def project_with(normed, w_own, w_partner, middle, core, write):
    part = w_own.shape[0]
    whole = part // HEAD
    rest = part - whole * HEAD
    spread = whole + 1 if rest else whole
    for piece, turn in ((w_own, core), (w_partner, 1 - core)):
        start = pl.multiple_of(turn * rest, rest) if rest else 0
        projected = lax.dot_general(
            normed,
            piece[pl.ds(start, whole * HEAD), :],
            (((1,), (1,)), ((), ())),
            preferred_element_type=jnp.float32,
        )
        for block in range(whole):
            write(turn * spread + block, projected[:, block * HEAD : (block + 1) * HEAD])
    if rest:
        projected = lax.dot_general(
            normed, middle[...], (((1,), (1,)), ((), ())), preferred_element_type=jnp.float32
        )
        write(whole, projected)


def join_middle(core, middle, w_own, w_partner):
    part = w_own.shape[0]
    rest = part % HEAD
    if rest:
        for piece, turn in ((w_own, core), (w_partner, 1 - core)):
            there = pl.multiple_of(turn * rest, rest)
            here = pl.multiple_of((1 - turn) * (part - rest), rest)
            middle[pl.ds(there, rest), :] = piece[pl.ds(here, rest), :]


def project_own_kernel(
    offset,
    place_ref,
    x0_ref,
    x1_ref,
    gain_ref,
    w_own,
    w_partner,
    cos_ref,
    sin_ref,
    q_gain_ref,
    k_gain_ref,
    out_ref,
    normed_ref,
    middle,
):
    line, column, core = place_ref[0], place_ref[1], place_ref[2]
    rows = x0_ref.shape[1]
    join_middle(core, middle, w_own, w_partner)
    for number, x_ref in enumerate((x0_ref, x1_ref)):
        x = x_ref[core].astype(jnp.float32)
        scale = lax.rsqrt(jnp.mean(x * x, axis=-1, keepdims=True) + EPSILON)
        normed_ref[number * rows : (number + 1) * rows, :] = (x * scale * gain_ref[...]).astype(
            jnp.bfloat16
        )
    blocks = out_ref.shape[1] // HEAD
    span = slice(offset, offset + 2 * rows)

    def write(block, projected):
        head = (line * 2 + column) * blocks + block
        out_ref[:, pl.ds(pl.multiple_of(block * HEAD, HEAD), HEAD)] = project_block(
            projected, head, cos_ref[span, :], sin_ref[span, :], (q_gain_ref, k_gain_ref)
        )

    project_with(normed_ref[...], w_own, w_partner, middle, core, write)


def project_far_kernel(
    place_ref,
    normed0_ref,
    normed1_ref,
    w_own,
    w_partner,
    cos_ref,
    sin_ref,
    q_gain_ref,
    k_gain_ref,
    near0_ref,
    near1_ref,
    full,
    swap_a_ref,
    swap_b_ref,
    kv_a_ref,
    kv_b_ref,
    middle,
):
    line, column, core = place_ref[0], place_ref[1], place_ref[2]
    join_middle(core, middle, w_own, w_partner)
    chip_width = near0_ref.shape[1]
    blocks = chip_width // HEAD
    which = 1 - column
    step = normed0_ref.shape[0]
    own = pl.multiple_of(column * chip_width, HEAD)
    for number, (normed_ref, near_ref) in enumerate(
        ((normed0_ref, near0_ref), (normed1_ref, near1_ref))
    ):
        span = slice(number * step, (number + 1) * step)
        full[span, pl.ds(own, chip_width)] = near_ref[...]

        def write(block, projected, span=span):
            head = (line * 2 + which) * blocks + block
            start = pl.multiple_of((which * blocks + block) * HEAD, HEAD)
            full[span, pl.ds(start, HEAD)] = project_block(
                projected, head, cos_ref[span, :], sin_ref[span, :], (q_gain_ref, k_gain_ref)
            )

        project_with(normed_ref[...], w_own, w_partner, middle, core, write)
    inner = HEADS // 2 * HEAD
    pair = swap_a_ref.shape[1]
    half = pair // 2
    left = inner - pair
    first = pl.ds(pl.multiple_of(column * step, step), step)
    second = pl.ds(pl.multiple_of((1 - column) * step, step), step)

    @pl.when(line == 0)
    def _():
        swap_a_ref[...] = full[first, inner : inner + pair]
        swap_b_ref[...] = full[second, inner : inner + pair]
        kv_a_ref[...] = jnp.zeros_like(kv_a_ref)
        kv_b_ref[...] = jnp.zeros_like(kv_b_ref)

    @pl.when(line == 1)
    def _():
        for out, rows, skip in (
            (swap_a_ref, first, 0),
            (swap_b_ref, second, 0),
            (kv_a_ref, second, half),
            (kv_b_ref, first, half),
        ):
            out[:, :half] = full[rows, left + skip : left + skip + half]
            out[:, half:] = full[rows, left + skip + pair : left + skip + pair + half]


SHRINK = math.log2(math.e) / math.sqrt(HEAD)


def with_ones(values):
    return jnp.concatenate([values, jnp.ones_like(values)], axis=1)


def query_of(head, part, place_ref, full_ref, swap_a_ref, swap_b_ref):
    line, column = place_ref[0], place_ref[1]
    rows = swap_a_ref.shape[0]
    span = slice(part * rows, (part + 1) * rows)
    moved = swap_a_ref.shape[1] // HEAD
    lanes = slice(head * HEAD, (head + 1) * HEAD)
    if head < moved:
        came = jnp.where(column == 1 - part, swap_a_ref[:, lanes], swap_b_ref[:, lanes])
        return jnp.where(line == 1, came, full_ref[span, lanes])
    start = pl.multiple_of((head - moved * line) * HEAD, HEAD)
    return full_ref[span, pl.ds(start, HEAD)]


def scores_of(q, keys, bias):
    return (
        lax.dot_general(q, keys, (((1,), (1,)), ((), ())), preferred_element_type=jnp.float32)
        + bias
    )


def attend_near_kernel(
    part,
    place_ref,
    full_ref,
    swap_a_ref,
    swap_b_ref,
    kv_a_ref,
    kv_b_ref,
    bias_ref,
    sum_ref,
    top_ref,
    near,
):
    line, column = place_ref[0], place_ref[1]
    rows = sum_ref.shape[0]
    half = kv_a_ref.shape[1] // 2
    heads = top_ref.shape[1] // HEAD
    span = slice(part * rows, (part + 1) * rows)
    for turn, swap_ref, kv_ref in ((1 - column, swap_a_ref, kv_a_ref), (column, swap_b_ref, kv_b_ref)):
        start = pl.multiple_of(turn * rows, rows)
        near[pl.ds(start, rows), :] = jnp.where(line == 0, swap_ref[...], kv_ref[...])

    def attend(block):
        keys = near[block, :half]
        values = with_ones(near[block, half:])
        bias = bias_ref[span, block]
        for head in range(heads):
            q = query_of(head, part, place_ref, full_ref, swap_a_ref, swap_b_ref)
            s = scores_of(q, keys, bias)
            top = jnp.max(s, axis=-1, keepdims=True)
            weight = jnp.exp2((s - top) * SHRINK).astype(jnp.bfloat16)
            sum_ref[:, 2 * head * HEAD : 2 * (head + 1) * HEAD] = jnp.dot(
                weight, values, preferred_element_type=jnp.float32
            )
            top_ref[:, head * HEAD : (head + 1) * HEAD] = jnp.broadcast_to(top, (rows, HEAD))

    both = place_ref[3 + part * 4 + 1 - part] == 1

    @pl.when(both)
    def _():
        attend(slice(0, 2 * rows))

    @pl.when(jnp.logical_not(both))
    def _():
        attend(span)


def attend_far_kernel(
    part,
    place_ref,
    full_ref,
    swap_a_ref,
    swap_b_ref,
    far0_ref,
    far1_ref,
    bias_ref,
    sum_ref,
    top_ref,
    out_ref,
):
    line, column = place_ref[0], place_ref[1]
    rows = out_ref.shape[0]
    half = far0_ref.shape[1] // 2
    heads = top_ref.shape[1] // HEAD
    span = slice(part * rows, (part + 1) * rows)
    block = 2 + column if part == 1 else 3 - column
    meets = place_ref[3 + part * 4 + block] == 1

    def finish(head, summed):
        out_ref[:, head * HEAD : (head + 1) * HEAD] = (
            summed[:, :HEAD] / summed[:, HEAD:]
        ).astype(jnp.bfloat16)

    @pl.when(jnp.logical_not(meets))
    def _():
        for head in range(heads):
            finish(head, sum_ref[:, 2 * head * HEAD : 2 * (head + 1) * HEAD])

    @pl.when(meets)
    def _():
        far = jnp.where(line == 0, far0_ref[...], far1_ref[...])
        keys = far[:, :half]
        values = with_ones(far[:, half:])
        bias = bias_ref[span, pl.ds(pl.multiple_of(block * rows, rows), rows)]
        for head in range(heads):
            q = query_of(head, part, place_ref, full_ref, swap_a_ref, swap_b_ref)
            s = scores_of(q, keys, bias)
            before = top_ref[:, head * HEAD : (head + 1) * HEAD]
            top = jnp.maximum(before, jnp.max(s, axis=-1, keepdims=True))
            wide = jnp.concatenate([top] * (rows // HEAD), axis=1)
            weight = jnp.exp2((s - wide) * SHRINK).astype(jnp.bfloat16)
            kept = jnp.exp2((before - top) * SHRINK)
            kept = jnp.concatenate([kept, kept], axis=1)
            summed = sum_ref[:, 2 * head * HEAD : 2 * (head + 1) * HEAD] * kept + jnp.dot(
                weight, values, preferred_element_type=jnp.float32
            )
            finish(head, summed)


def share_kernel(place_ref, a_ref, w0_ref, w1_ref, out_ref):
    core = place_ref[2]
    width = w0_ref.shape[1]
    for turn, w_ref in enumerate((w0_ref, w1_ref)):
        start = pl.multiple_of((core ^ turn) * width, HEAD)
        out_ref[:, pl.ds(start, width)] = jnp.dot(
            a_ref[...], w_ref[...], preferred_element_type=jnp.float32
        ).astype(jnp.bfloat16)


def finish_kernel(
    relative, place_ref, a_ref, w0_ref, w1_ref, came_ref, x0_ref, x1_ref, own_ref, pair_ref
):
    chip = place_ref[0] * 2 + place_ref[1]
    core = place_ref[2]
    width = w0_ref.shape[1]
    rows = own_ref.shape[0]
    for turn, w_ref in enumerate((w0_ref, w1_ref)):
        start = pl.multiple_of((core ^ turn) * width, HEAD)
        mixed = jnp.dot(
            a_ref[...], w_ref[...], preferred_element_type=jnp.float32
        ) + came_ref[:, pl.ds(start, width)].astype(jnp.float32)
        where = pl.multiple_of((chip ^ relative) * 2 * width + start, HEAD)
        for number, (x_ref, out_ref) in enumerate(((x0_ref, own_ref), (x1_ref, pair_ref))):
            out_ref[:, pl.ds(start, width)] = (
                x_ref[core, :, pl.ds(where, width)].astype(jnp.float32)
                + mixed[number * rows : (number + 1) * rows, :]
            ).astype(jnp.bfloat16)


def gather_kernel(place_ref, *refs):
    out_ref = refs[-1]
    chip = place_ref[0] * 2 + place_ref[1]
    core = place_ref[2]
    for turn in range(2):
        for relative in range(4):
            piece = refs[turn * 4 + relative]
            width = piece.shape[1]
            start = pl.multiple_of((chip ^ relative) * width, HEAD)
            out_ref[core ^ turn, :, pl.ds(start, width)] = piece[...]


def on_chip_grid(held, norm_gain, w_qkv, q_gain, k_gain, w_out, lengths):
    micro, rows, width = held.shape[1:]
    devices = lax.axis_size("dp")
    sections = lax.axis_size("section")
    here = lax.axis_index("dp")
    inner = w_out.shape[1]
    pair = KV_HEADS * HEAD

    def swap(value, bits, among=range(8)):
        return lax.ppermute(value, "dp", [(i, i ^ bits) for i in among])

    def after(value, *others):
        return lax.optimization_barrier((value, *others))[0]

    kept = held[0]
    w_in = w_qkv[0].T
    w_across = swap(w_in, 2)
    x_y = swap(kept, 4)
    x_c = swap(kept, 1)
    w_c = swap(w_in, 1)

    w_o = w_out[0]
    half = inner // 2
    own_rows = micro * 2 * rows
    spread = [-2.0 * math.log(THETA) / HEAD * (lane % (HEAD // 2)) for lane in range(HEAD)]
    spacing = jnp.asarray([[math.exp(value) for value in spread]], jnp.float32)
    f32, bf16 = jnp.float32, jnp.bfloat16
    shape = jax.ShapeDtypeStruct
    place, bias, cosine, sine, o_here, o_there = pl.pallas_call(
        prepare_kernel,
        out_shape=(
            shape((11,), jnp.int32),
            shape((own_rows, 2 * own_rows), f32),
            shape((own_rows, HEAD), f32),
            shape((own_rows, HEAD), f32),
            shape((half, w_o.shape[1]), bf16),
            shape((half, w_o.shape[1]), bf16),
        ),
        in_specs=[SMEM, SMEM, VMEM, VMEM],
        out_specs=(SMEM, VMEM, VMEM, VMEM, VMEM, VMEM),
        compiler_params=pltpu.CompilerParams(vmem_limit_bytes=12 * MIB),
    )(here[None], lengths[0], spacing, w_o)
    o_here_c = swap(o_here, 1)

    part = w_in.shape[0]
    flops = 2 * own_rows * width * 2 * part
    chip_rows = own_rows // 2

    def project_own(offset, gain, first, second):
        return local_kernel(
            functools.partial(project_own_kernel, offset),
            [shape((chip_rows, 2 * part), bf16), shape((chip_rows, width), bf16)],
            [place, first, second, gain, w_in, w_c, cosine, sine, q_gain, k_gain],
            [pltpu.VMEM((HEAD, width), bf16)],
            flops // 2,
        )

    near0, normed0 = project_own(0, norm_gain, kept, x_c)
    x_y, near0 = lax.optimization_barrier((x_y, near0))
    x_yc = swap(x_y, 1)
    near1, normed1 = project_own(chip_rows, norm_gain, x_y, x_yc)
    o_y = swap(o_there, 4)
    w_across_c = swap(after(w_across, x_yc), 1)
    full, swapping_a, swapping_b, kv_a, kv_b = local_kernel(
        project_far_kernel,
        [shape((own_rows, 4 * part), bf16)] + [shape((chip_rows, pair), bf16)] * 4,
        [place, normed0, normed1, w_across, w_across_c, cosine, sine, q_gain, k_gain, near0, near1],
        [pltpu.VMEM((HEAD, width), bf16)],
        flops,
    )
    swap_a = swap(swapping_a, 4)
    swap_b = swap(swapping_b, 4)
    far1_a = swap(kv_a, 2, range(4, 8))
    far1_b = swap(kv_b, 2, range(4, 8))
    far0_a = swap(swap_a, 2, range(4))
    far0_b = swap(swap_b, 2, range(4))
    o_x = swap(after(o_here, w_across), 2)
    o_x_c = swap(after(o_x, swap_a), 1)
    o_xy = swap(after(o_y, far0_b, far1_b), 2)
    o_y_c = swap(after(o_y, kv_a), 1)

    def attend_near(part):
        return local_kernel(
            functools.partial(attend_near_kernel, part),
            [shape((chip_rows, 2 * half), f32), shape((chip_rows, half), f32)],
            [place, full, swap_a, swap_b, kv_a, kv_b, bias],
            [pltpu.VMEM((own_rows, pair), bf16)],
            flops=2 * own_rows * own_rows * half,
        )

    def attend_far(part, before, far0, far1, *others):
        return local_kernel(
            functools.partial(attend_far_kernel, part),
            [shape((chip_rows, half), bf16)],
            [place, full, swap_a, swap_b, far0, far1, after(bias, *others), *before],
            flops=own_rows * own_rows * half,
        )[0]

    sums_there = attend_near(1)
    sums_here = attend_near(0)
    attended_there = attend_far(1, sums_there, far0_a, far1_a)

    chunk = 2 * w_o.shape[1]
    came = {}

    def share(relative, rows_there, *pieces):
        (value,) = local_kernel(
            share_kernel,
            [shape((own_rows // 2, chunk), bf16)],
            [place, rows_there, *pieces],
            flops=own_rows * half * chunk,
        )
        came[relative ^ 2] = swap(value, 4)
        return value

    ring = [
        (s * devices + i, (s + 1) % sections * devices + i)
        for s in range(sections)
        for i in range(devices)
    ]
    cross = [(source, target ^ 1) for source, target in ring]
    arrived = {}

    def finish(relative, *pieces):
        own, other = local_kernel(
            functools.partial(finish_kernel, relative),
            [shape((rows, chunk), bf16)] * 2,
            [place, attended_here, *pieces, came[relative], kept, x_c],
            flops=own_rows * half * chunk,
        )
        arrived[0, relative] = lax.ppermute(own, ("section", "dp"), ring)
        arrived[1, relative] = lax.ppermute(other, ("section", "dp"), cross)
        return own

    last = share(0, attended_there, o_here, o_here_c)
    last = share(2, after(attended_there, last), o_y, o_y_c)
    last = share(1, after(attended_there, last), o_x, o_x_c)
    attended_here = attend_far(0, sums_here, far0_b, far1_b, last)
    last = finish(2, o_y, o_y_c)
    o_xy_c = swap(after(o_xy, last), 1)
    share(3, attended_there, o_xy, o_xy_c)
    finish(0, o_here, o_here_c)
    finish(3, o_xy, o_xy_c)
    finish(1, o_x, o_x_c)
    (result,) = local_kernel(
        gather_kernel,
        [shape((micro, rows, width), bf16)],
        [place, *[arrived[turn, relative] for turn in range(2) for relative in range(4)]],
    )
    return result[None]


def solution(mesh):
    devices = mesh.shape["dp"]

    def body(held, norm_gain, w_qkv, q_gain, k_gain, w_out, lengths):
        paired = KV_HEADS == 2 and HEADS == KV_HEADS * GROUP and held.shape[1] == 2
        whole_heads = (2 * w_qkv.shape[2]) % HEAD == 0
        form = on_chip_grid if devices == 8 and paired and whole_heads else on_device
        return form(held, norm_gain, w_qkv, q_gain, k_gain, w_out, lengths)

    in_specs = (
        P("section", None, "dp", None),
        P("section", None),
        P("section", None, "dp"),
        P("section", None),
        P("section", None),
        P("section", None, "dp"),
        P("section", None, None),
    )
    out_specs = P("section", None, "dp", None)
    return jax.shard_map(
        body, mesh=mesh, in_specs=in_specs, out_specs=out_specs, check_vma=False
    )
```

```python
import functools
import math

import jax
import jax.numpy as jnp
from jax import lax
from jax.experimental import pallas as pl
from jax.experimental.pallas import tpu as pltpu
from jax.sharding import PartitionSpec as P

HEADS = 16
KV_HEADS = 2
HEAD = 128
GROUP = 8


EPSILON = 1e-06
THETA = 1000000.0
NEGATIVE = -1e30


def from_behind(value, axis, steps):
    count = lax.axis_size(axis)
    pairs = [(source, (source + steps) % count) for source in range(count)]
    return lax.ppermute(value, axis, pairs)


def rms_scale(values, gain):
    return values * lax.rsqrt(jnp.mean(values * values, axis=-1, keepdims=True) + EPSILON) * gain


def rotary(values, places):
    width = values.shape[-1]
    middle = width // 2
    spacing = jnp.exp(jnp.arange(middle, dtype=jnp.float32) * (-2.0 * math.log(THETA) / width))
    angle = places.astype(jnp.float32)[..., None] * spacing
    cosine = jnp.cos(angle)[..., None, :]
    sine = jnp.sin(angle)[..., None, :]
    former = values[..., :middle]
    latter = values[..., middle:]
    return jnp.concatenate(
        [former * cosine - latter * sine, latter * cosine + former * sine], axis=-1
    )


def locate(positions, doc_lengths):
    ends = jnp.cumsum(doc_lengths, axis=-1)
    before = (ends[:, None, :] <= positions[None, :, None]).astype(jnp.int32)
    return (jnp.sum(before, axis=-1), jnp.sum(before * doc_lengths[:, None, :], axis=-1))


def attend_rows(query_rows, key_rows, value_rows, allowed):
    scores = jnp.einsum(
        "kqd,nkd->kqn", query_rows, key_rows, preferred_element_type=jnp.float32
    ) / math.sqrt(HEAD)
    highest = jnp.max(jnp.where(allowed[None], scores, NEGATIVE), axis=-1)
    weights = jnp.where(allowed[None], jnp.exp(scores - highest[..., None]), 0.0).astype(
        jnp.bfloat16
    )
    total = jnp.sum(weights.astype(jnp.float32), axis=-1)
    summed = jnp.einsum("kqn,nkd->kqd", weights, value_rows, preferred_element_type=jnp.float32)
    return summed / total[..., None]


def on_device(held, norm_gain, w_qkv, q_gain, k_gain, w_out, lengths):
    micro = held.shape[1]
    rows = held.shape[2]
    width = held.shape[3]
    inner = HEADS * HEAD
    key_width = KV_HEADS * HEAD
    middle = rows // 2
    devices = lax.axis_size("dp")
    here = lax.axis_index("dp")
    total_tokens = rows * devices
    doc_most = min(4096, total_tokens // 2)
    reach = min(total_tokens, doc_most + middle)
    doc_lengths = lengths[0]
    resident = held[0].astype(jnp.float32).reshape(micro * rows, width)
    normed = rms_scale(resident, norm_gain[0]).astype(jnp.bfloat16)
    projected = jnp.dot(
        normed,
        lax.all_gather(w_qkv[0], "dp", axis=1, tiled=True),
        preferred_element_type=jnp.float32,
    ).reshape(micro, rows, inner + 2 * key_width)
    own_index = here * rows + jnp.arange(rows, dtype=jnp.int32)
    own_start = locate(own_index, doc_lengths)[1]
    places = own_index[None, :] - own_start
    queries = rotary(
        rms_scale(projected[..., :inner].reshape(micro, rows, HEADS, HEAD), q_gain[0]), places
    ).astype(jnp.bfloat16)
    keys = rotary(
        rms_scale(
            projected[..., inner : inner + key_width].reshape(micro, rows, KV_HEADS, HEAD),
            k_gain[0],
        ),
        places,
    ).astype(jnp.bfloat16)
    values = projected[..., inner + key_width :].astype(jnp.bfloat16)
    packed = jnp.concatenate([keys.reshape(micro, rows, key_width), values], axis=-1)
    gathered = lax.all_gather(packed, "dp", axis=1, tiled=True)
    latter_queries = queries[:, middle:]
    latter_index = own_index[middle:]
    group_index = jnp.stack([own_index[:middle], latter_index])
    group_doc = locate(group_index.reshape(-1), doc_lengths)[0].reshape(micro, 2, middle)
    arranged = jnp.stack([queries[:, :middle], latter_queries], axis=1)
    arranged = arranged.reshape(micro, 2, middle, KV_HEADS, GROUP, HEAD).transpose(0, 1, 3, 4, 2, 5)
    arranged = arranged.reshape(micro, 2, KV_HEADS, GROUP * middle, HEAD)
    row_index = jnp.tile(group_index, (1, GROUP))
    row_doc = jnp.tile(group_doc, (1, 1, GROUP))
    finished = []
    for which_micro in range(micro):
        for which_half in range(2):
            first = group_index[which_half, 0]
            key_first = jnp.clip(first + middle - reach, 0, total_tokens - reach)
            window = lax.dynamic_slice_in_dim(gathered[which_micro], key_first, reach, 0)
            key_index = key_first + jnp.arange(reach, dtype=jnp.int32)
            key_doc = locate(key_index, doc_lengths[which_micro : which_micro + 1])[0][0]
            key_part = window[:, :key_width].reshape(reach, KV_HEADS, HEAD)
            value_part = window[:, key_width:].reshape(reach, KV_HEADS, HEAD)
            allowed = (row_doc[which_micro, which_half][:, None] == key_doc[None, :]) & (
                row_index[which_half][:, None] >= key_index[None, :]
            )
            ratio = attend_rows(
                arranged[which_micro, which_half], key_part, value_part, allowed
            ).astype(jnp.bfloat16)
            finished.append(
                ratio.reshape(KV_HEADS, GROUP, middle, HEAD)
                .transpose(2, 0, 1, 3)
                .reshape(middle, inner)
            )
    former_part = jnp.stack(finished[0::2])
    latter_part = jnp.stack(finished[1::2])
    attended = jnp.concatenate([former_part, latter_part], axis=1).reshape(micro * rows, inner)
    mixed = jnp.dot(
        attended,
        lax.all_gather(w_out[0], "dp", axis=1, tiled=True),
        preferred_element_type=jnp.float32,
    )
    result = (resident + mixed).astype(jnp.bfloat16).reshape(1, micro, rows, width)
    return from_behind(result, "section", 1)


MIB = 1 << 20
VMEM = pl.BlockSpec(memory_space=pltpu.VMEM)
SMEM = pl.BlockSpec(memory_space=pltpu.SMEM)


def local_kernel(body, outs, inputs, scratch=(), flops=0, grant=24, scalars=1):
    moved = sum(math.prod(s.shape) * s.dtype.itemsize for s in (*outs, *inputs))
    return pl.pallas_call(
        body,
        out_shape=tuple(outs),
        in_specs=[SMEM] * scalars + [VMEM] * (len(inputs) - scalars),
        out_specs=tuple(VMEM for _ in outs),
        scratch_shapes=list(scratch),
        compiler_params=pltpu.CompilerParams(vmem_limit_bytes=grant * MIB),
        cost_estimate=pl.CostEstimate(flops=flops, bytes_accessed=moved, transcendentals=0),
    )(*inputs)


def prepare_kernel(
    here_ref,
    lengths_ref,
    spacing_ref,
    w_ref,
    place_ref,
    bias_ref,
    cos_ref,
    sin_ref,
    here_out,
    there_out,
):
    here = here_ref[0]
    line, column, core = here >> 2, (here >> 1) & 1, here & 1
    chip = here >> 1
    half = here_out.shape[0]
    here_out[...] = w_ref[pl.ds(pl.multiple_of(line * half, half), half), :]
    there_out[...] = w_ref[pl.ds(pl.multiple_of((1 - line) * half, half), half), :]
    documents = lengths_ref.shape[1]
    sizes = [lengths_ref[core, j] for j in range(documents)]
    ends = [sizes[0]]
    for size in sizes[1:]:
        ends.append(ends[-1] + size)

    def locate_in(index):
        number = jnp.zeros_like(index)
        start = jnp.zeros_like(index)
        for end, size in zip(ends, sizes):
            past = (end <= index).astype(jnp.int32)
            number = number + past
            start = start + past * size
        return number, start

    rows = cos_ref.shape[0] // 4
    lane = lax.broadcasted_iota(jnp.int32, (1, rows), 1)
    keys = []
    for bits in (0, 1, 4, 5, 2, 3, 6, 7):
        index = (here ^ bits) * rows + lane
        keys.append((index, locate_in(index)[0]))
    first_half = lax.broadcasted_iota(jnp.int32, (rows, HEAD), 1) < HEAD // 2
    for block, bits in enumerate((0, 1, 4, 5)):
        span = slice(block * rows, (block + 1) * rows)
        index = (here ^ bits) * rows + lax.broadcasted_iota(jnp.int32, (rows, HEAD), 0)
        number, start = locate_in(index)
        angle = (index - start).astype(jnp.float32) * spacing_ref[...]
        sine = jnp.sin(angle)
        cos_ref[span, :] = jnp.cos(angle)
        sin_ref[span, :] = jnp.where(first_half, -sine, sine)
        for other, (key_index, key_number) in enumerate(keys):
            allowed = (number[:, :1] == key_number) & (index[:, :1] >= key_index)
            bias_ref[span, other * rows : (other + 1) * rows] = jnp.where(
                allowed, 0.0, NEGATIVE
            ).astype(jnp.float32)

    def number_at(index):
        number = jnp.int32(0)
        for end in ends:
            number = number + jnp.where(end <= index, 1, 0)
        return number

    place_ref[0] = line
    place_ref[1] = column
    place_ref[2] = core
    for row, row_bits in enumerate((0, 2)):
        row_chip = chip ^ row_bits
        for key, key_bits in enumerate((0, 2, 1, 3)):
            key_chip = chip ^ key_bits
            shares = number_at(key_chip * 2 * rows + 2 * rows - 1) >= number_at(row_chip * 2 * rows)
            meets = (key_chip == row_chip) | ((key_chip < row_chip) & shares)
            place_ref[3 + 4 * row + key] = jnp.where(meets, 1, 0)


def project_block(projected, head, cosine, sine, gains_ref):
    is_value = head >= HEADS + KV_HEADS
    is_query = head < HEADS
    gain = jnp.where(is_query, gains_ref[0][...], gains_ref[1][...])
    scale = lax.rsqrt(jnp.mean(projected * projected, axis=-1, keepdims=True) + EPSILON)
    v = projected * scale * gain
    turned = v * cosine + pltpu.roll(v, HEAD // 2, 1) * sine
    return jnp.where(is_value, projected, turned).astype(jnp.bfloat16)


def project_with(normed, w_own, w_partner, middle, core, write):
    part = w_own.shape[0]
    whole = part // HEAD
    rest = part - whole * HEAD
    spread = whole + 1 if rest else whole
    for piece, turn in ((w_own, core), (w_partner, 1 - core)):
        start = pl.multiple_of(turn * rest, rest) if rest else 0
        projected = lax.dot_general(
            normed,
            piece[pl.ds(start, whole * HEAD), :],
            (((1,), (1,)), ((), ())),
            preferred_element_type=jnp.float32,
        )
        for block in range(whole):
            write(turn * spread + block, projected[:, block * HEAD : (block + 1) * HEAD])
    if rest:
        projected = lax.dot_general(
            normed, middle[...], (((1,), (1,)), ((), ())), preferred_element_type=jnp.float32
        )
        write(whole, projected)


def join_middle(core, middle, w_own, w_partner):
    part = w_own.shape[0]
    rest = part % HEAD
    if rest:
        for piece, turn in ((w_own, core), (w_partner, 1 - core)):
            there = pl.multiple_of(turn * rest, rest)
            here = pl.multiple_of((1 - turn) * (part - rest), rest)
            middle[pl.ds(there, rest), :] = piece[pl.ds(here, rest), :]


def project_own_kernel(
    offset,
    place_ref,
    x0_ref,
    x1_ref,
    gain_ref,
    w_own,
    w_partner,
    cos_ref,
    sin_ref,
    q_gain_ref,
    k_gain_ref,
    out_ref,
    normed_ref,
    middle,
):
    line, column, core = place_ref[0], place_ref[1], place_ref[2]
    rows = x0_ref.shape[1]
    join_middle(core, middle, w_own, w_partner)
    for number, x_ref in enumerate((x0_ref, x1_ref)):
        x = x_ref[core].astype(jnp.float32)
        scale = lax.rsqrt(jnp.mean(x * x, axis=-1, keepdims=True) + EPSILON)
        normed_ref[number * rows : (number + 1) * rows, :] = (x * scale * gain_ref[...]).astype(
            jnp.bfloat16
        )
    blocks = out_ref.shape[1] // HEAD
    span = slice(offset, offset + 2 * rows)

    def write(block, projected):
        head = (line * 2 + column) * blocks + block
        out_ref[:, pl.ds(pl.multiple_of(block * HEAD, HEAD), HEAD)] = project_block(
            projected, head, cos_ref[span, :], sin_ref[span, :], (q_gain_ref, k_gain_ref)
        )

    project_with(normed_ref[...], w_own, w_partner, middle, core, write)


def project_far_kernel(
    place_ref,
    normed0_ref,
    normed1_ref,
    w_own,
    w_partner,
    cos_ref,
    sin_ref,
    q_gain_ref,
    k_gain_ref,
    near0_ref,
    near1_ref,
    full,
    swap_a_ref,
    swap_b_ref,
    kv_a_ref,
    kv_b_ref,
    middle,
):
    line, column, core = place_ref[0], place_ref[1], place_ref[2]
    join_middle(core, middle, w_own, w_partner)
    chip_width = near0_ref.shape[1]
    blocks = chip_width // HEAD
    which = 1 - column
    step = normed0_ref.shape[0]
    own = pl.multiple_of(column * chip_width, HEAD)
    for number, (normed_ref, near_ref) in enumerate(
        ((normed0_ref, near0_ref), (normed1_ref, near1_ref))
    ):
        span = slice(number * step, (number + 1) * step)
        full[span, pl.ds(own, chip_width)] = near_ref[...]

        def write(block, projected, span=span):
            head = (line * 2 + which) * blocks + block
            start = pl.multiple_of((which * blocks + block) * HEAD, HEAD)
            full[span, pl.ds(start, HEAD)] = project_block(
                projected, head, cos_ref[span, :], sin_ref[span, :], (q_gain_ref, k_gain_ref)
            )

        project_with(normed_ref[...], w_own, w_partner, middle, core, write)
    inner = HEADS // 2 * HEAD
    pair = swap_a_ref.shape[1]
    half = pair // 2
    left = inner - pair
    first = pl.ds(pl.multiple_of(column * step, step), step)
    second = pl.ds(pl.multiple_of((1 - column) * step, step), step)

    @pl.when(line == 0)
    def _():
        swap_a_ref[...] = full[first, inner : inner + pair]
        swap_b_ref[...] = full[second, inner : inner + pair]
        kv_a_ref[...] = jnp.zeros_like(kv_a_ref)
        kv_b_ref[...] = jnp.zeros_like(kv_b_ref)

    @pl.when(line == 1)
    def _():
        for out, rows, skip in (
            (swap_a_ref, first, 0),
            (swap_b_ref, second, 0),
            (kv_a_ref, second, half),
            (kv_b_ref, first, half),
        ):
            out[:, :half] = full[rows, left + skip : left + skip + half]
            out[:, half:] = full[rows, left + skip + pair : left + skip + pair + half]


SHRINK = math.log2(math.e) / math.sqrt(HEAD)


def with_ones(values):
    return jnp.concatenate([values, jnp.ones_like(values)], axis=1)


def query_of(head, part, place_ref, full_ref, swap_a_ref, swap_b_ref):
    line, column = place_ref[0], place_ref[1]
    rows = swap_a_ref.shape[0]
    span = slice(part * rows, (part + 1) * rows)
    moved = swap_a_ref.shape[1] // HEAD
    lanes = slice(head * HEAD, (head + 1) * HEAD)
    if head < moved:
        came = jnp.where(column == 1 - part, swap_a_ref[:, lanes], swap_b_ref[:, lanes])
        return jnp.where(line == 1, came, full_ref[span, lanes])
    start = pl.multiple_of((head - moved * line) * HEAD, HEAD)
    return full_ref[span, pl.ds(start, HEAD)]


def scores_of(q, keys, bias):
    return (
        lax.dot_general(q, keys, (((1,), (1,)), ((), ())), preferred_element_type=jnp.float32)
        + bias
    )


def attend_near_kernel(
    part,
    place_ref,
    full_ref,
    swap_a_ref,
    swap_b_ref,
    kv_a_ref,
    kv_b_ref,
    bias_ref,
    sum_ref,
    top_ref,
    near,
):
    line, column = place_ref[0], place_ref[1]
    rows = sum_ref.shape[0]
    half = kv_a_ref.shape[1] // 2
    heads = top_ref.shape[1] // HEAD
    span = slice(part * rows, (part + 1) * rows)
    for turn, swap_ref, kv_ref in ((1 - column, swap_a_ref, kv_a_ref), (column, swap_b_ref, kv_b_ref)):
        start = pl.multiple_of(turn * rows, rows)
        near[pl.ds(start, rows), :] = jnp.where(line == 0, swap_ref[...], kv_ref[...])

    def attend(block):
        keys = near[block, :half]
        values = with_ones(near[block, half:])
        bias = bias_ref[span, block]
        for head in range(heads):
            q = query_of(head, part, place_ref, full_ref, swap_a_ref, swap_b_ref)
            s = scores_of(q, keys, bias)
            top = jnp.max(s, axis=-1, keepdims=True)
            weight = jnp.exp2((s - top) * SHRINK).astype(jnp.bfloat16)
            sum_ref[:, 2 * head * HEAD : 2 * (head + 1) * HEAD] = jnp.dot(
                weight, values, preferred_element_type=jnp.float32
            )
            top_ref[:, head * HEAD : (head + 1) * HEAD] = jnp.broadcast_to(top, (rows, HEAD))

    both = place_ref[3 + part * 4 + 1 - part] == 1

    @pl.when(both)
    def _():
        attend(slice(0, 2 * rows))

    @pl.when(jnp.logical_not(both))
    def _():
        attend(span)


def attend_far_kernel(
    part,
    place_ref,
    full_ref,
    swap_a_ref,
    swap_b_ref,
    far0_ref,
    far1_ref,
    bias_ref,
    sum_ref,
    top_ref,
    out_ref,
):
    line, column = place_ref[0], place_ref[1]
    rows = out_ref.shape[0]
    half = far0_ref.shape[1] // 2
    heads = top_ref.shape[1] // HEAD
    span = slice(part * rows, (part + 1) * rows)
    block = 2 + column if part == 1 else 3 - column
    meets = place_ref[3 + part * 4 + block] == 1

    def finish(head, summed):
        out_ref[:, head * HEAD : (head + 1) * HEAD] = (
            summed[:, :HEAD] / summed[:, HEAD:]
        ).astype(jnp.bfloat16)

    @pl.when(jnp.logical_not(meets))
    def _():
        for head in range(heads):
            finish(head, sum_ref[:, 2 * head * HEAD : 2 * (head + 1) * HEAD])

    @pl.when(meets)
    def _():
        far = jnp.where(line == 0, far0_ref[...], far1_ref[...])
        keys = far[:, :half]
        values = with_ones(far[:, half:])
        bias = bias_ref[span, pl.ds(pl.multiple_of(block * rows, rows), rows)]
        for head in range(heads):
            q = query_of(head, part, place_ref, full_ref, swap_a_ref, swap_b_ref)
            s = scores_of(q, keys, bias)
            before = top_ref[:, head * HEAD : (head + 1) * HEAD]
            top = jnp.maximum(before, jnp.max(s, axis=-1, keepdims=True))
            wide = jnp.concatenate([top] * (rows // HEAD), axis=1)
            weight = jnp.exp2((s - wide) * SHRINK).astype(jnp.bfloat16)
            kept = jnp.exp2((before - top) * SHRINK)
            kept = jnp.concatenate([kept, kept], axis=1)
            summed = sum_ref[:, 2 * head * HEAD : 2 * (head + 1) * HEAD] * kept + jnp.dot(
                weight, values, preferred_element_type=jnp.float32
            )
            finish(head, summed)


def share_kernel(place_ref, a_ref, w0_ref, w1_ref, out_ref):
    core = place_ref[2]
    width = w0_ref.shape[1]
    for turn, w_ref in enumerate((w0_ref, w1_ref)):
        start = pl.multiple_of((core ^ turn) * width, HEAD)
        out_ref[:, pl.ds(start, width)] = jnp.dot(
            a_ref[...], w_ref[...], preferred_element_type=jnp.float32
        ).astype(jnp.bfloat16)


def finish_kernel(
    relative, place_ref, a_ref, w0_ref, w1_ref, came_ref, x0_ref, x1_ref, own_ref, pair_ref
):
    chip = place_ref[0] * 2 + place_ref[1]
    core = place_ref[2]
    width = w0_ref.shape[1]
    rows = own_ref.shape[0]
    for turn, w_ref in enumerate((w0_ref, w1_ref)):
        start = pl.multiple_of((core ^ turn) * width, HEAD)
        mixed = jnp.dot(
            a_ref[...], w_ref[...], preferred_element_type=jnp.float32
        ) + came_ref[:, pl.ds(start, width)].astype(jnp.float32)
        where = pl.multiple_of((chip ^ relative) * 2 * width + start, HEAD)
        for number, (x_ref, out_ref) in enumerate(((x0_ref, own_ref), (x1_ref, pair_ref))):
            out_ref[:, pl.ds(start, width)] = (
                x_ref[core, :, pl.ds(where, width)].astype(jnp.float32)
                + mixed[number * rows : (number + 1) * rows, :]
            ).astype(jnp.bfloat16)


def gather_kernel(place_ref, *refs):
    out_ref = refs[-1]
    chip = place_ref[0] * 2 + place_ref[1]
    core = place_ref[2]
    for turn in range(2):
        for relative in range(4):
            piece = refs[turn * 4 + relative]
            width = piece.shape[1]
            start = pl.multiple_of((chip ^ relative) * width, HEAD)
            out_ref[core ^ turn, :, pl.ds(start, width)] = piece[...]


def on_chip_grid(held, norm_gain, w_qkv, q_gain, k_gain, w_out, lengths):
    micro, rows, width = held.shape[1:]
    devices = lax.axis_size("dp")
    sections = lax.axis_size("section")
    here = lax.axis_index("dp")
    inner = w_out.shape[1]
    pair = KV_HEADS * HEAD

    def swap(value, bits, among=range(8)):
        return lax.ppermute(value, "dp", [(i, i ^ bits) for i in among])

    def after(value, *others):
        return lax.optimization_barrier((value, *others))[0]

    kept = held[0]
    w_in = w_qkv[0].T
    w_across = swap(w_in, 2)
    x_y = swap(kept, 4)
    x_c = swap(kept, 1)
    w_c = swap(w_in, 1)

    w_o = w_out[0]
    half = inner // 2
    own_rows = micro * 2 * rows
    spread = [-2.0 * math.log(THETA) / HEAD * (lane % (HEAD // 2)) for lane in range(HEAD)]
    spacing = jnp.asarray([[math.exp(value) for value in spread]], jnp.float32)
    f32, bf16 = jnp.float32, jnp.bfloat16
    shape = jax.ShapeDtypeStruct
    place, bias, cosine, sine, o_here, o_there = pl.pallas_call(
        prepare_kernel,
        out_shape=(
            shape((11,), jnp.int32),
            shape((own_rows, 2 * own_rows), f32),
            shape((own_rows, HEAD), f32),
            shape((own_rows, HEAD), f32),
            shape((half, w_o.shape[1]), bf16),
            shape((half, w_o.shape[1]), bf16),
        ),
        in_specs=[SMEM, SMEM, VMEM, VMEM],
        out_specs=(SMEM, VMEM, VMEM, VMEM, VMEM, VMEM),
        compiler_params=pltpu.CompilerParams(vmem_limit_bytes=12 * MIB),
    )(here[None], lengths[0], spacing, w_o)
    o_here_c = swap(o_here, 1)

    part = w_in.shape[0]
    flops = 2 * own_rows * width * 2 * part
    chip_rows = own_rows // 2

    def project_own(offset, gain, first, second):
        return local_kernel(
            functools.partial(project_own_kernel, offset),
            [shape((chip_rows, 2 * part), bf16), shape((chip_rows, width), bf16)],
            [place, first, second, gain, w_in, w_c, cosine, sine, q_gain, k_gain],
            [pltpu.VMEM((HEAD, width), bf16)],
            flops // 2,
        )

    near0, normed0 = project_own(0, norm_gain, kept, x_c)
    x_y, near0 = lax.optimization_barrier((x_y, near0))
    x_yc = swap(x_y, 1)
    near1, normed1 = project_own(chip_rows, norm_gain, x_y, x_yc)
    o_y = swap(o_there, 4)
    w_across_c = swap(after(w_across, x_yc), 1)
    full, swapping_a, swapping_b, kv_a, kv_b = local_kernel(
        project_far_kernel,
        [shape((own_rows, 4 * part), bf16)] + [shape((chip_rows, pair), bf16)] * 4,
        [place, normed0, normed1, w_across, w_across_c, cosine, sine, q_gain, k_gain, near0, near1],
        [pltpu.VMEM((HEAD, width), bf16)],
        flops,
    )
    swap_a = swap(swapping_a, 4)
    swap_b = swap(swapping_b, 4)
    far1_a = swap(kv_a, 2, range(4, 8))
    far1_b = swap(kv_b, 2, range(4, 8))
    far0_a = swap(swap_a, 2, range(4))
    far0_b = swap(swap_b, 2, range(4))
    o_x = swap(after(o_here, w_across), 2)
    o_y_c = swap(after(o_y, kv_a), 1)

    def attend_near(part, gate):
        return local_kernel(
            functools.partial(attend_near_kernel, part),
            [shape((chip_rows, 2 * half), f32), shape((chip_rows, half), f32)],
            [place, full, swap_a, swap_b, kv_a, kv_b, after(bias, gate)],
            [pltpu.VMEM((own_rows, pair), bf16)],
            flops=2 * own_rows * own_rows * half,
        )

    def attend_far(part, before, far0, far1, *others):
        return local_kernel(
            functools.partial(attend_far_kernel, part),
            [shape((chip_rows, half), bf16)],
            [place, full, swap_a, swap_b, far0, far1, after(bias, *others), *before],
            flops=own_rows * own_rows * half,
        )[0]

    sums_there = attend_near(1, bias)
    o_xy = swap(after(o_y, far0_a, far1_a), 2)
    attended_there = attend_far(1, sums_there, far0_a, far1_a)
    o_x_c = swap(after(o_x, attended_there), 1)

    chunk = 2 * w_o.shape[1]
    came = {}

    def share(relative, rows_there, *pieces):
        (value,) = local_kernel(
            share_kernel,
            [shape((own_rows // 2, chunk), bf16)],
            [place, rows_there, *pieces],
            flops=own_rows * half * chunk,
        )
        came[relative ^ 2] = swap(value, 4)
        return value

    ring = [
        (s * devices + i, (s + 1) % sections * devices + i)
        for s in range(sections)
        for i in range(devices)
    ]
    cross = [(source, target ^ 1) for source, target in ring]
    arrived = {}

    def finish(relative, *pieces):
        own, other = local_kernel(
            functools.partial(finish_kernel, relative),
            [shape((rows, chunk), bf16)] * 2,
            [place, attended_here, *pieces, came[relative], kept, x_c],
            flops=own_rows * half * chunk,
        )
        arrived[0, relative] = lax.ppermute(own, ("section", "dp"), ring)
        arrived[1, relative] = lax.ppermute(other, ("section", "dp"), cross)
        return own

    last = share(0, attended_there, o_here, o_here_c)
    last = share(2, after(attended_there, last), o_y, o_y_c)
    sums_here = attend_near(0, last)
    last = share(1, after(attended_there, sums_here[1]), o_x, o_x_c)
    attended_here = attend_far(0, sums_here, far0_b, far1_b, last)
    last = finish(2, o_y, o_y_c)
    o_xy_c = swap(after(o_xy, last), 1)
    last = finish(0, o_here, o_here_c)
    share(3, after(attended_there, last), o_xy, o_xy_c)
    finish(3, o_xy, o_xy_c)
    finish(1, o_x, o_x_c)
    (result,) = local_kernel(
        gather_kernel,
        [shape((micro, rows, width), bf16)],
        [place, *[arrived[turn, relative] for turn in range(2) for relative in range(4)]],
    )
    return result[None]


def solution(mesh):
    devices = mesh.shape["dp"]

    def body(held, norm_gain, w_qkv, q_gain, k_gain, w_out, lengths):
        paired = KV_HEADS == 2 and HEADS == KV_HEADS * GROUP and held.shape[1] == 2
        whole_heads = (2 * w_qkv.shape[2]) % HEAD == 0
        form = on_chip_grid if devices == 8 and paired and whole_heads else on_device
        return form(held, norm_gain, w_qkv, q_gain, k_gain, w_out, lengths)

    in_specs = (
        P("section", None, "dp", None),
        P("section", None),
        P("section", None, "dp"),
        P("section", None),
        P("section", None),
        P("section", None, "dp"),
        P("section", None, None),
    )
    out_specs = P("section", None, "dp", None)
    return jax.shard_map(
        body, mesh=mesh, in_specs=in_specs, out_specs=out_specs, check_vma=False
    )
```

```python
import functools
import math

import jax
import jax.numpy as jnp
from jax import lax
from jax.experimental import pallas as pl
from jax.experimental.pallas import tpu as pltpu
from jax.sharding import PartitionSpec as P

HEADS = 16
KV_HEADS = 2
HEAD = 128
GROUP = 8


EPSILON = 1e-06
THETA = 1000000.0
NEGATIVE = -1e30


def from_behind(value, axis, steps):
    count = lax.axis_size(axis)
    pairs = [(source, (source + steps) % count) for source in range(count)]
    return lax.ppermute(value, axis, pairs)


def rms_scale(values, gain):
    return values * lax.rsqrt(jnp.mean(values * values, axis=-1, keepdims=True) + EPSILON) * gain


def rotary(values, places):
    width = values.shape[-1]
    middle = width // 2
    spacing = jnp.exp(jnp.arange(middle, dtype=jnp.float32) * (-2.0 * math.log(THETA) / width))
    angle = places.astype(jnp.float32)[..., None] * spacing
    cosine = jnp.cos(angle)[..., None, :]
    sine = jnp.sin(angle)[..., None, :]
    former = values[..., :middle]
    latter = values[..., middle:]
    return jnp.concatenate(
        [former * cosine - latter * sine, latter * cosine + former * sine], axis=-1
    )


def locate(positions, doc_lengths):
    ends = jnp.cumsum(doc_lengths, axis=-1)
    before = (ends[:, None, :] <= positions[None, :, None]).astype(jnp.int32)
    return (jnp.sum(before, axis=-1), jnp.sum(before * doc_lengths[:, None, :], axis=-1))


def attend_rows(query_rows, key_rows, value_rows, allowed):
    scores = jnp.einsum(
        "kqd,nkd->kqn", query_rows, key_rows, preferred_element_type=jnp.float32
    ) / math.sqrt(HEAD)
    highest = jnp.max(jnp.where(allowed[None], scores, NEGATIVE), axis=-1)
    weights = jnp.where(allowed[None], jnp.exp(scores - highest[..., None]), 0.0).astype(
        jnp.bfloat16
    )
    total = jnp.sum(weights.astype(jnp.float32), axis=-1)
    summed = jnp.einsum("kqn,nkd->kqd", weights, value_rows, preferred_element_type=jnp.float32)
    return summed / total[..., None]


def on_device(held, norm_gain, w_qkv, q_gain, k_gain, w_out, lengths):
    micro = held.shape[1]
    rows = held.shape[2]
    width = held.shape[3]
    inner = HEADS * HEAD
    key_width = KV_HEADS * HEAD
    middle = rows // 2
    devices = lax.axis_size("dp")
    here = lax.axis_index("dp")
    total_tokens = rows * devices
    doc_most = min(4096, total_tokens // 2)
    reach = min(total_tokens, doc_most + middle)
    doc_lengths = lengths[0]
    resident = held[0].astype(jnp.float32).reshape(micro * rows, width)
    normed = rms_scale(resident, norm_gain[0]).astype(jnp.bfloat16)
    projected = jnp.dot(
        normed,
        lax.all_gather(w_qkv[0], "dp", axis=1, tiled=True),
        preferred_element_type=jnp.float32,
    ).reshape(micro, rows, inner + 2 * key_width)
    own_index = here * rows + jnp.arange(rows, dtype=jnp.int32)
    own_start = locate(own_index, doc_lengths)[1]
    places = own_index[None, :] - own_start
    queries = rotary(
        rms_scale(projected[..., :inner].reshape(micro, rows, HEADS, HEAD), q_gain[0]), places
    ).astype(jnp.bfloat16)
    keys = rotary(
        rms_scale(
            projected[..., inner : inner + key_width].reshape(micro, rows, KV_HEADS, HEAD),
            k_gain[0],
        ),
        places,
    ).astype(jnp.bfloat16)
    values = projected[..., inner + key_width :].astype(jnp.bfloat16)
    packed = jnp.concatenate([keys.reshape(micro, rows, key_width), values], axis=-1)
    gathered = lax.all_gather(packed, "dp", axis=1, tiled=True)
    latter_queries = queries[:, middle:]
    latter_index = own_index[middle:]
    group_index = jnp.stack([own_index[:middle], latter_index])
    group_doc = locate(group_index.reshape(-1), doc_lengths)[0].reshape(micro, 2, middle)
    arranged = jnp.stack([queries[:, :middle], latter_queries], axis=1)
    arranged = arranged.reshape(micro, 2, middle, KV_HEADS, GROUP, HEAD).transpose(0, 1, 3, 4, 2, 5)
    arranged = arranged.reshape(micro, 2, KV_HEADS, GROUP * middle, HEAD)
    row_index = jnp.tile(group_index, (1, GROUP))
    row_doc = jnp.tile(group_doc, (1, 1, GROUP))
    finished = []
    for which_micro in range(micro):
        for which_half in range(2):
            first = group_index[which_half, 0]
            key_first = jnp.clip(first + middle - reach, 0, total_tokens - reach)
            window = lax.dynamic_slice_in_dim(gathered[which_micro], key_first, reach, 0)
            key_index = key_first + jnp.arange(reach, dtype=jnp.int32)
            key_doc = locate(key_index, doc_lengths[which_micro : which_micro + 1])[0][0]
            key_part = window[:, :key_width].reshape(reach, KV_HEADS, HEAD)
            value_part = window[:, key_width:].reshape(reach, KV_HEADS, HEAD)
            allowed = (row_doc[which_micro, which_half][:, None] == key_doc[None, :]) & (
                row_index[which_half][:, None] >= key_index[None, :]
            )
            ratio = attend_rows(
                arranged[which_micro, which_half], key_part, value_part, allowed
            ).astype(jnp.bfloat16)
            finished.append(
                ratio.reshape(KV_HEADS, GROUP, middle, HEAD)
                .transpose(2, 0, 1, 3)
                .reshape(middle, inner)
            )
    former_part = jnp.stack(finished[0::2])
    latter_part = jnp.stack(finished[1::2])
    attended = jnp.concatenate([former_part, latter_part], axis=1).reshape(micro * rows, inner)
    mixed = jnp.dot(
        attended,
        lax.all_gather(w_out[0], "dp", axis=1, tiled=True),
        preferred_element_type=jnp.float32,
    )
    result = (resident + mixed).astype(jnp.bfloat16).reshape(1, micro, rows, width)
    return from_behind(result, "section", 1)


MIB = 1 << 20
VMEM = pl.BlockSpec(memory_space=pltpu.VMEM)
SMEM = pl.BlockSpec(memory_space=pltpu.SMEM)


def local_kernel(body, outs, inputs, scratch=(), flops=0, grant=12, scalars=1):
    moved = sum(math.prod(s.shape) * s.dtype.itemsize for s in (*outs, *inputs))
    return pl.pallas_call(
        body,
        out_shape=tuple(outs),
        in_specs=[SMEM] * scalars + [VMEM] * (len(inputs) - scalars),
        out_specs=tuple(VMEM for _ in outs),
        scratch_shapes=list(scratch),
        compiler_params=pltpu.CompilerParams(vmem_limit_bytes=grant * MIB),
        cost_estimate=pl.CostEstimate(flops=flops, bytes_accessed=moved, transcendentals=0),
    )(*inputs)


def prepare_kernel(
    here_ref,
    lengths_ref,
    spacing_ref,
    w_ref,
    place_ref,
    bias_ref,
    cos_ref,
    sin_ref,
    here_out,
    there_out,
):
    here = here_ref[0]
    line, column, core = here >> 2, (here >> 1) & 1, here & 1
    chip = here >> 1
    half = here_out.shape[0]
    here_out[...] = w_ref[pl.ds(pl.multiple_of(line * half, half), half), :]
    there_out[...] = w_ref[pl.ds(pl.multiple_of((1 - line) * half, half), half), :]
    documents = lengths_ref.shape[1]
    sizes = [lengths_ref[core, j] for j in range(documents)]
    ends = [sizes[0]]
    for size in sizes[1:]:
        ends.append(ends[-1] + size)

    def locate_in(index):
        number = jnp.zeros_like(index)
        start = jnp.zeros_like(index)
        for end, size in zip(ends, sizes):
            past = (end <= index).astype(jnp.int32)
            number = number + past
            start = start + past * size
        return number, start

    rows = cos_ref.shape[0] // 4
    lane = lax.broadcasted_iota(jnp.int32, (1, rows), 1)
    keys = []
    for bits in (0, 1, 4, 5, 2, 3, 6, 7):
        index = (here ^ bits) * rows + lane
        keys.append((index, locate_in(index)[0]))
    first_half = lax.broadcasted_iota(jnp.int32, (rows, HEAD), 1) < HEAD // 2
    for block, bits in enumerate((0, 1, 4, 5)):
        span = slice(block * rows, (block + 1) * rows)
        index = (here ^ bits) * rows + lax.broadcasted_iota(jnp.int32, (rows, HEAD), 0)
        number, start = locate_in(index)
        angle = (index - start).astype(jnp.float32) * spacing_ref[...]
        sine = jnp.sin(angle)
        cos_ref[span, :] = jnp.cos(angle)
        sin_ref[span, :] = jnp.where(first_half, -sine, sine)
        for other, (key_index, key_number) in enumerate(keys):
            allowed = (number[:, :1] == key_number) & (index[:, :1] >= key_index)
            bias_ref[span, other * rows : (other + 1) * rows] = jnp.where(
                allowed, 0.0, NEGATIVE
            ).astype(jnp.float32)

    def number_at(index):
        number = jnp.int32(0)
        for end in ends:
            number = number + jnp.where(end <= index, 1, 0)
        return number

    place_ref[0] = line
    place_ref[1] = column
    place_ref[2] = core
    for row, row_bits in enumerate((0, 2)):
        row_chip = chip ^ row_bits
        for key, key_bits in enumerate((0, 2, 1, 3)):
            key_chip = chip ^ key_bits
            shares = number_at(key_chip * 2 * rows + 2 * rows - 1) >= number_at(row_chip * 2 * rows)
            meets = (key_chip == row_chip) | ((key_chip < row_chip) & shares)
            place_ref[3 + 4 * row + key] = jnp.where(meets, 1, 0)


def project_block(projected, head, cosine, sine, gains_ref):
    is_value = head >= HEADS + KV_HEADS
    is_query = head < HEADS
    gain = jnp.where(is_query, gains_ref[0][...], gains_ref[1][...])
    scale = lax.rsqrt(jnp.mean(projected * projected, axis=-1, keepdims=True) + EPSILON)
    v = projected * scale * gain
    turned = v * cosine + pltpu.roll(v, HEAD // 2, 1) * sine
    return jnp.where(is_value, projected, turned).astype(jnp.bfloat16)


def project_with(normed, w_own, w_partner, middle, core, write):
    part = w_own.shape[0]
    whole = part // HEAD
    rest = part - whole * HEAD
    spread = whole + 1 if rest else whole
    for piece, turn in ((w_own, core), (w_partner, 1 - core)):
        start = pl.multiple_of(turn * rest, rest) if rest else 0
        projected = lax.dot_general(
            normed,
            piece[pl.ds(start, whole * HEAD), :],
            (((1,), (1,)), ((), ())),
            preferred_element_type=jnp.float32,
        )
        for block in range(whole):
            write(turn * spread + block, projected[:, block * HEAD : (block + 1) * HEAD])
    if rest:
        projected = lax.dot_general(
            normed, middle[...], (((1,), (1,)), ((), ())), preferred_element_type=jnp.float32
        )
        write(whole, projected)


def join_middle(core, middle, w_own, w_partner):
    part = w_own.shape[0]
    rest = part % HEAD
    if rest:
        for piece, turn in ((w_own, core), (w_partner, 1 - core)):
            there = pl.multiple_of(turn * rest, rest)
            here = pl.multiple_of((1 - turn) * (part - rest), rest)
            middle[pl.ds(there, rest), :] = piece[pl.ds(here, rest), :]


def norm_rows(core, x_ref, gain_ref):
    x = x_ref[core].astype(jnp.float32)
    scale = lax.rsqrt(jnp.mean(x * x, axis=-1, keepdims=True) + EPSILON)
    return (x * scale * gain_ref[...]).astype(jnp.bfloat16)


def norm_kernel(place_ref, x_ref, gain_ref, normed_ref):
    normed_ref[...] = norm_rows(place_ref[2], x_ref, gain_ref)


def project_own_kernel(
    offset,
    keep,
    place_ref,
    ready_ref,
    x_ref,
    gain_ref,
    w_own,
    w_partner,
    cos_ref,
    sin_ref,
    q_gain_ref,
    k_gain_ref,
    out_ref,
    normed_ref,
    *rest_refs,
):
    line, column, core = place_ref[0], place_ref[1], place_ref[2]
    *kept, middle = rest_refs
    join_middle(core, middle, w_own, w_partner)
    if keep:
        kept[0][...] = w_partner[...]
    rows = ready_ref.shape[0]
    normed_ref[:rows, :] = ready_ref[...]
    normed_ref[rows:, :] = norm_rows(core, x_ref, gain_ref)
    blocks = out_ref.shape[1] // HEAD
    span = slice(offset, offset + 2 * rows)

    def write(block, projected):
        head = (line * 2 + column) * blocks + block
        out_ref[:, pl.ds(pl.multiple_of(block * HEAD, HEAD), HEAD)] = project_block(
            projected, head, cos_ref[span, :], sin_ref[span, :], (q_gain_ref, k_gain_ref)
        )

    project_with(normed_ref[...], w_own, w_partner, middle, core, write)


def project_far_kernel(
    order,
    place_ref,
    normed0_ref,
    normed1_ref,
    w_own,
    w_partner,
    cos_ref,
    sin_ref,
    q_gain_ref,
    k_gain_ref,
    near0_ref,
    near1_ref,
    full,
    swap_ref,
    kv_ref,
    middle,
):
    line, column, core = place_ref[0], place_ref[1], place_ref[2]
    join_middle(core, middle, w_own, w_partner)
    chip_width = near0_ref.shape[1]
    blocks = chip_width // HEAD
    which = 1 - column
    step = normed0_ref.shape[0]
    part = column if order == 0 else 1 - column
    normed = jnp.where(part == 0, normed0_ref[...], normed1_ref[...])
    span = pl.ds(pl.multiple_of(part * step, step), step)
    cosine, sine = cos_ref[span, :], sin_ref[span, :]
    full[:, pl.ds(pl.multiple_of(column * chip_width, HEAD), chip_width)] = jnp.where(
        part == 0, near0_ref[...], near1_ref[...]
    )

    def write(block, projected):
        head = (line * 2 + which) * blocks + block
        start = pl.multiple_of((which * blocks + block) * HEAD, HEAD)
        full[:, pl.ds(start, HEAD)] = project_block(
            projected, head, cosine, sine, (q_gain_ref, k_gain_ref)
        )

    project_with(normed, w_own, w_partner, middle, core, write)
    inner = HEADS // 2 * HEAD
    pair = swap_ref.shape[1]
    half = pair // 2
    left = inner - pair

    @pl.when(line == 0)
    def _():
        swap_ref[...] = full[:, inner : inner + pair]
        kv_ref[...] = jnp.zeros_like(kv_ref)

    @pl.when(line == 1)
    def _():
        for out, skip in ((swap_ref, 0), (kv_ref, half)):
            out[:, :half] = full[:, left + skip : left + skip + half]
            out[:, half:] = full[:, left + skip + pair : left + skip + pair + half]


SHRINK = math.log2(math.e) / math.sqrt(HEAD)


def with_ones(values):
    return jnp.concatenate([values, jnp.ones_like(values)], axis=1)


def query_of(head, part, place_ref, full_refs, swap_refs):
    line, column = place_ref[0], place_ref[1]
    moved = swap_refs[0].shape[1] // HEAD
    start = pl.multiple_of(jnp.maximum(head - moved * line, 0) * HEAD, HEAD)
    lanes = pl.ds(start, HEAD)
    q = jnp.where(column == part, full_refs[0][:, lanes], full_refs[1][:, lanes])
    if head < moved:
        there = slice(head * HEAD, (head + 1) * HEAD)
        came = jnp.where(column == 1 - part, swap_refs[0][:, there], swap_refs[1][:, there])
        q = jnp.where(line == 1, came, q)
    return q


def scores_of(q, keys, bias):
    return (
        lax.dot_general(q, keys, (((1,), (1,)), ((), ())), preferred_element_type=jnp.float32)
        + bias
    )


def attend_near_kernel(
    part,
    place_ref,
    full0_ref,
    full1_ref,
    swap_a_ref,
    swap_b_ref,
    kv_a_ref,
    kv_b_ref,
    bias_ref,
    sum_ref,
    top_ref,
    near,
):
    line, column = place_ref[0], place_ref[1]
    rows = sum_ref.shape[0]
    half = kv_a_ref.shape[1] // 2
    heads = top_ref.shape[1] // HEAD
    span = slice(part * rows, (part + 1) * rows)
    for turn, swap_ref, kv_ref in ((1 - column, swap_a_ref, kv_a_ref), (column, swap_b_ref, kv_b_ref)):
        start = pl.multiple_of(turn * rows, rows)
        near[pl.ds(start, rows), :] = jnp.where(line == 0, swap_ref[...], kv_ref[...])

    def attend(block):
        keys = near[block, :half]
        values = with_ones(near[block, half:])
        bias = bias_ref[span, block]
        for head in range(heads):
            q = query_of(head, part, place_ref, (full0_ref, full1_ref), (swap_a_ref, swap_b_ref))
            s = scores_of(q, keys, bias)
            top = jnp.max(s, axis=-1, keepdims=True)
            weight = jnp.exp2((s - top) * SHRINK).astype(jnp.bfloat16)
            sum_ref[:, 2 * head * HEAD : 2 * (head + 1) * HEAD] = jnp.dot(
                weight, values, preferred_element_type=jnp.float32
            )
            top_ref[:, head * HEAD : (head + 1) * HEAD] = jnp.broadcast_to(top, (rows, HEAD))

    both = place_ref[3 + part * 4 + 1 - part] == 1

    @pl.when(both)
    def _():
        attend(slice(0, 2 * rows))

    @pl.when(jnp.logical_not(both))
    def _():
        attend(span)


def attend_far_kernel(
    part,
    place_ref,
    full0_ref,
    full1_ref,
    swap_a_ref,
    swap_b_ref,
    far0_ref,
    far1_ref,
    bias_ref,
    sum_ref,
    top_ref,
    out_ref,
):
    line, column = place_ref[0], place_ref[1]
    rows = out_ref.shape[0]
    half = far0_ref.shape[1] // 2
    heads = top_ref.shape[1] // HEAD
    span = slice(part * rows, (part + 1) * rows)
    block = 2 + column if part == 1 else 3 - column
    meets = place_ref[3 + part * 4 + block] == 1

    def finish(head, summed):
        out_ref[:, head * HEAD : (head + 1) * HEAD] = (
            summed[:, :HEAD] / summed[:, HEAD:]
        ).astype(jnp.bfloat16)

    @pl.when(jnp.logical_not(meets))
    def _():
        for head in range(heads):
            finish(head, sum_ref[:, 2 * head * HEAD : 2 * (head + 1) * HEAD])

    @pl.when(meets)
    def _():
        far = jnp.where(line == 0, far0_ref[...], far1_ref[...])
        keys = far[:, :half]
        values = with_ones(far[:, half:])
        bias = bias_ref[span, pl.ds(pl.multiple_of(block * rows, rows), rows)]
        for head in range(heads):
            q = query_of(head, part, place_ref, (full0_ref, full1_ref), (swap_a_ref, swap_b_ref))
            s = scores_of(q, keys, bias)
            before = top_ref[:, head * HEAD : (head + 1) * HEAD]
            top = jnp.maximum(before, jnp.max(s, axis=-1, keepdims=True))
            wide = jnp.concatenate([top] * (rows // HEAD), axis=1)
            weight = jnp.exp2((s - wide) * SHRINK).astype(jnp.bfloat16)
            kept = jnp.exp2((before - top) * SHRINK)
            kept = jnp.concatenate([kept, kept], axis=1)
            summed = sum_ref[:, 2 * head * HEAD : 2 * (head + 1) * HEAD] * kept + jnp.dot(
                weight, values, preferred_element_type=jnp.float32
            )
            finish(head, summed)


def attend_kernel(part, place_ref, *refs):
    fulls, swaps, kvs, fars, bias, (out_ref, near, sums, tops) = (
        refs[0:2], refs[2:4], refs[4:6], refs[6:8], refs[8], refs[9:13]
    )
    attend_near_kernel(part, place_ref, *fulls, *swaps, *kvs, bias, sums, tops, near)
    attend_far_kernel(part, place_ref, *fulls, *swaps, *fars, bias, sums, tops, out_ref)


def attend_share_kernel(part, place_ref, *refs):
    *before, w0_ref, w1_ref, out_ref, share_ref = refs
    attend_far_kernel(part, place_ref, *before, out_ref)
    share_kernel(place_ref, out_ref, w0_ref, w1_ref, share_ref)


def share_two_kernel(place_ref, a_ref, w0_ref, w1_ref, w2_ref, w3_ref, out0_ref, out1_ref):
    share_kernel(place_ref, a_ref, w0_ref, w1_ref, out0_ref)
    share_kernel(place_ref, a_ref, w2_ref, w3_ref, out1_ref)


def share_kernel(place_ref, a_ref, w0_ref, w1_ref, out_ref):
    core = place_ref[2]
    width = w0_ref.shape[1]
    for turn, w_ref in enumerate((w0_ref, w1_ref)):
        start = pl.multiple_of((core ^ turn) * width, HEAD)
        out_ref[:, pl.ds(start, width)] = jnp.dot(
            a_ref[...], w_ref[...], preferred_element_type=jnp.float32
        ).astype(jnp.bfloat16)


def finish_kernel(
    relative, place_ref, a_ref, w0_ref, w1_ref, came_ref, x0_ref, x1_ref, *out_refs
):
    chip = place_ref[0] * 2 + place_ref[1]
    core = place_ref[2]
    width = w0_ref.shape[1]
    rows = x0_ref.shape[1]
    for turn, w_ref in enumerate((w0_ref, w1_ref)):
        start = pl.multiple_of((core ^ turn) * width, HEAD)
        mixed = jnp.dot(
            a_ref[...], w_ref[...], preferred_element_type=jnp.float32
        ) + came_ref[:, pl.ds(start, width)].astype(jnp.float32)
        where = pl.multiple_of((chip ^ relative) * 2 * width + start, HEAD)
        for number, x_ref in enumerate((x0_ref, x1_ref)):
            span = slice(number * rows, (number + 1) * rows)
            value = (
                x_ref[core, :, pl.ds(where, width)].astype(jnp.float32) + mixed[span, :]
            ).astype(jnp.bfloat16)
            if len(out_refs) == 1:
                out_refs[0][span, pl.ds(start, width)] = value
            else:
                out_refs[number][:, pl.ds(start, width)] = value


def gather_kernel(place_ref, *refs):
    out_ref = refs[-1]
    chip = place_ref[0] * 2 + place_ref[1]
    core = place_ref[2]
    rows = out_ref.shape[1]
    for turn in range(2):
        for number, relative in enumerate(EARLY):
            piece = refs[turn * len(EARLY) + number]
            width = piece.shape[1]
            start = pl.multiple_of((chip ^ relative) * width, HEAD)
            out_ref[core ^ turn, :, pl.ds(start, width)] = piece[
                turn * rows : (turn + 1) * rows, :
            ]


def gather_last_kernel(place_ref, own_ref, other_ref, before_ref, out_ref, semaphores):
    width = own_ref.shape[1]
    start = pl.multiple_of(((place_ref[0] * 2 + place_ref[1]) ^ LATE) * width, HEAD)
    copies = [
        pltpu.make_async_copy(
            piece,
            out_ref.at[place_ref[2] ^ turn, :, pl.ds(start, width)],
            semaphores.at[turn],
        )
        for turn, piece in enumerate((own_ref, other_ref))
    ]
    for copy in copies:
        copy.start()
    for copy in copies:
        copy.wait()


EARLY = (2, 0, 3)
LATE = 1


def on_chip_grid(held, norm_gain, w_qkv, q_gain, k_gain, w_out, lengths):
    micro, rows, width = held.shape[1:]
    devices = lax.axis_size("dp")
    sections = lax.axis_size("section")
    here = lax.axis_index("dp")
    inner = w_out.shape[1]
    pair = KV_HEADS * HEAD

    def swap(value, bits, among=range(8)):
        return lax.ppermute(value, "dp", [(i, i ^ bits) for i in among])

    def after(value, *others):
        return lax.optimization_barrier((value, *others))[0]

    kept = held[0]
    w_in = w_qkv[0].T
    w_across = swap(w_in, 2)
    x_y = swap(kept, 4)
    x_c = swap(kept, 1)
    w_c = swap(w_in, 1)

    w_o = w_out[0]
    half = inner // 2
    own_rows = micro * 2 * rows
    spread = [-2.0 * math.log(THETA) / HEAD * (lane % (HEAD // 2)) for lane in range(HEAD)]
    spacing = jnp.asarray([[math.exp(value) for value in spread]], jnp.float32)
    f32, bf16 = jnp.float32, jnp.bfloat16
    shape = jax.ShapeDtypeStruct
    place, bias, cosine, sine, o_here, o_there = pl.pallas_call(
        prepare_kernel,
        out_shape=(
            shape((11,), jnp.int32),
            shape((own_rows, 2 * own_rows), f32),
            shape((own_rows, HEAD), f32),
            shape((own_rows, HEAD), f32),
            shape((half, w_o.shape[1]), bf16),
            shape((half, w_o.shape[1]), bf16),
        ),
        in_specs=[SMEM, SMEM, VMEM, VMEM],
        out_specs=(SMEM, VMEM, VMEM, VMEM, VMEM, VMEM),
        compiler_params=pltpu.CompilerParams(vmem_limit_bytes=12 * MIB),
    )(here[None], lengths[0], spacing, w_o)
    o_here_c = swap(o_here, 1)

    part = w_in.shape[0]
    flops = 2 * own_rows * width * 2 * part
    chip_rows = own_rows // 2

    def normalise(value):
        return local_kernel(
            norm_kernel, [shape((rows, width), bf16)], [place, value, norm_gain]
        )[0]

    def project_own(offset, ready, second, w_other, keep):
        return local_kernel(
            functools.partial(project_own_kernel, offset, keep),
            [shape((chip_rows, 2 * part), bf16), shape((chip_rows, width), bf16)]
            + [shape(w_c.shape, bf16)] * keep,
            [place, ready, second, norm_gain, w_in, w_other, cosine, sine, q_gain, k_gain],
            [pltpu.VMEM((HEAD, width), bf16)],
            flops // 2,
        )

    near0, normed0, w_c = project_own(0, normalise(kept), x_c, w_c, True)
    x_y, near0 = lax.optimization_barrier((x_y, near0))
    x_yc = swap(x_y, 1)
    ready = normalise(x_y)
    near1, normed1 = project_own(chip_rows, ready, x_yc, w_c, False)
    o_y = swap(o_there, 4)
    o_x = swap(o_here, 2)
    w_across_c = swap(after(w_across, ready), 1)

    def project_far(order, gate):
        return local_kernel(
            functools.partial(project_far_kernel, order),
            [shape((chip_rows, 4 * part), bf16)] + [shape((chip_rows, pair), bf16)] * 2,
            [
                place,
                normed0,
                normed1,
                w_across,
                w_across_c,
                cosine,
                sine,
                after(q_gain, gate),
                k_gain,
                near0,
                near1,
            ],
            [pltpu.VMEM((HEAD, width), bf16)],
            flops // 2,
        )

    full0, swapping_a, kv_b = project_far(0, near1)
    full1, swapping_b, kv_a = project_far(1, swapping_a)
    swap_a = swap(swapping_a, 4)
    swap_b = swap(swapping_b, 4)
    far1_a = swap(kv_a, 2, range(4, 8))
    far1_b = swap(kv_b, 2, range(4, 8))
    far0_a = swap(swap_a, 2, range(4))
    far0_b = swap(swap_b, 2, range(4))
    o_y_c = swap(after(o_y, kv_a), 1)

    queries = (full0, full1, swap_a, swap_b)
    partial_shapes = [shape((chip_rows, 2 * half), f32), shape((chip_rows, half), f32)]
    attend_flops = 2 * own_rows * own_rows * half
    chunk = 2 * w_o.shape[1]
    chunk_flops = own_rows * half * chunk
    chunk_shape = shape((chip_rows, chunk), bf16)
    rows_shape = shape((chip_rows, half), bf16)
    sums_there = local_kernel(
        functools.partial(attend_near_kernel, 1),
        partial_shapes,
        [place, *queries, kv_a, kv_b, bias],
        [pltpu.VMEM((own_rows, pair), bf16)],
        attend_flops,
    )
    o_xy = swap(after(o_y, far0_a, far1_a), 2)
    attended_there, share0 = local_kernel(
        functools.partial(attend_share_kernel, 1),
        [rows_shape, chunk_shape],
        [place, *queries, far0_a, far1_a, bias, *sums_there, o_here, o_here_c],
        flops=attend_flops // 2 + chunk_flops,
    )
    o_x_c = swap(after(o_x, kv_a), 1)

    ring = [
        (s * devices + i, (s + 1) % sections * devices + i)
        for s in range(sections)
        for i in range(devices)
    ]
    cross = [(source, target ^ 1) for source, target in ring]
    arrived = {}

    def finish(relative, *pieces):
        late = relative == LATE
        values = local_kernel(
            functools.partial(finish_kernel, relative),
            [shape((rows, chunk), bf16)] * 2 if late else [chunk_shape],
            [place, attended_here, *pieces, came[relative], kept, x_c],
            flops=chunk_flops,
        )
        arrived[0, relative] = lax.ppermute(values[0], ("section", "dp"), ring)
        if late:
            arrived[1, relative] = lax.ppermute(values[1], ("section", "dp"), cross)
        return values[0]

    came = {2: swap(share0, 4)}
    (attended_here,) = local_kernel(
        functools.partial(attend_kernel, 0),
        [rows_shape],
        [place, *queries, kv_a, kv_b, far0_b, far1_b, after(bias, share0)],
        [pltpu.VMEM((own_rows, pair), bf16)]
        + [pltpu.VMEM(each.shape, each.dtype) for each in partial_shapes],
        2 * attend_flops,
    )
    share2, share1 = local_kernel(
        share_two_kernel,
        [chunk_shape, chunk_shape],
        [place, after(attended_there, share0), o_y, o_y_c, o_x, o_x_c],
        flops=2 * chunk_flops,
    )
    came[0] = swap(share2, 4)
    came[3] = swap(share1, 4)
    attended_here = after(attended_here, share1)
    last = finish(2, o_y, o_y_c)
    o_xy_c = swap(after(o_xy, last), 1)
    last = finish(0, o_here, o_here_c)
    (share3,) = local_kernel(
        share_kernel,
        [chunk_shape],
        [place, after(attended_there, last), o_xy, o_xy_c],
        flops=chunk_flops,
    )
    came[1] = swap(share3, 4)
    finish(3, o_xy, o_xy_c)
    last = finish(1, o_x, o_x_c)
    for relative in EARLY:
        arrived[1, relative] = swap(after(arrived[0, relative], last), 1)
    (result,) = local_kernel(
        gather_kernel,
        [shape((micro, rows, width), bf16)],
        [place, *[arrived[turn, relative] for turn in range(2) for relative in EARLY]],
    )
    result = pl.pallas_call(
        gather_last_kernel,
        out_shape=shape((micro, rows, width), bf16),
        in_specs=[SMEM, VMEM, VMEM, pl.BlockSpec(memory_space=pl.ANY)],
        out_specs=pl.BlockSpec(memory_space=pl.ANY),
        scratch_shapes=[pltpu.SemaphoreType.DMA((2,))],
        input_output_aliases={3: 0},
        compiler_params=pltpu.CompilerParams(vmem_limit_bytes=4 * MIB),
    )(place, arrived[0, LATE], arrived[1, LATE], result)
    return result[None]


def solution(mesh):
    devices = mesh.shape["dp"]

    def body(held, norm_gain, w_qkv, q_gain, k_gain, w_out, lengths):
        paired = KV_HEADS == 2 and HEADS == KV_HEADS * GROUP and held.shape[1] == 2
        whole_heads = (2 * w_qkv.shape[2]) % HEAD == 0
        form = on_chip_grid if devices == 8 and paired and whole_heads else on_device
        return form(held, norm_gain, w_qkv, q_gain, k_gain, w_out, lengths)

    in_specs = (
        P("section", None, "dp", None),
        P("section", None),
        P("section", None, "dp"),
        P("section", None),
        P("section", None),
        P("section", None, "dp"),
        P("section", None, None),
    )
    out_specs = P("section", None, "dp", None)
    return jax.shard_map(
        body, mesh=mesh, in_specs=in_specs, out_specs=out_specs, check_vma=False
    )
```

```python
import functools
import math

import jax
import jax.numpy as jnp
from jax import lax
from jax.experimental import pallas as pl
from jax.experimental.pallas import tpu as pltpu
from jax.sharding import PartitionSpec as P

HEADS = 16
KV_HEADS = 2
HEAD = 128
GROUP = 8


EPSILON = 1e-06
THETA = 1000000.0
NEGATIVE = -1e30


def from_behind(value, axis, steps):
    count = lax.axis_size(axis)
    pairs = [(source, (source + steps) % count) for source in range(count)]
    return lax.ppermute(value, axis, pairs)


def rms_scale(values, gain):
    return values * lax.rsqrt(jnp.mean(values * values, axis=-1, keepdims=True) + EPSILON) * gain


def rotary(values, places):
    width = values.shape[-1]
    middle = width // 2
    spacing = jnp.exp(jnp.arange(middle, dtype=jnp.float32) * (-2.0 * math.log(THETA) / width))
    angle = places.astype(jnp.float32)[..., None] * spacing
    cosine = jnp.cos(angle)[..., None, :]
    sine = jnp.sin(angle)[..., None, :]
    former = values[..., :middle]
    latter = values[..., middle:]
    return jnp.concatenate(
        [former * cosine - latter * sine, latter * cosine + former * sine], axis=-1
    )


def locate(positions, doc_lengths):
    ends = jnp.cumsum(doc_lengths, axis=-1)
    before = (ends[:, None, :] <= positions[None, :, None]).astype(jnp.int32)
    return (jnp.sum(before, axis=-1), jnp.sum(before * doc_lengths[:, None, :], axis=-1))


def attend_rows(query_rows, key_rows, value_rows, allowed):
    scores = jnp.einsum(
        "kqd,nkd->kqn", query_rows, key_rows, preferred_element_type=jnp.float32
    ) / math.sqrt(HEAD)
    highest = jnp.max(jnp.where(allowed[None], scores, NEGATIVE), axis=-1)
    weights = jnp.where(allowed[None], jnp.exp(scores - highest[..., None]), 0.0).astype(
        jnp.bfloat16
    )
    total = jnp.sum(weights.astype(jnp.float32), axis=-1)
    summed = jnp.einsum("kqn,nkd->kqd", weights, value_rows, preferred_element_type=jnp.float32)
    return summed / total[..., None]


def on_device(held, norm_gain, w_qkv, q_gain, k_gain, w_out, lengths):
    micro = held.shape[1]
    rows = held.shape[2]
    width = held.shape[3]
    inner = HEADS * HEAD
    key_width = KV_HEADS * HEAD
    middle = rows // 2
    devices = lax.axis_size("dp")
    here = lax.axis_index("dp")
    total_tokens = rows * devices
    doc_most = min(4096, total_tokens // 2)
    reach = min(total_tokens, doc_most + middle)
    doc_lengths = lengths[0]
    resident = held[0].astype(jnp.float32).reshape(micro * rows, width)
    normed = rms_scale(resident, norm_gain[0]).astype(jnp.bfloat16)
    projected = jnp.dot(
        normed,
        lax.all_gather(w_qkv[0], "dp", axis=1, tiled=True),
        preferred_element_type=jnp.float32,
    ).reshape(micro, rows, inner + 2 * key_width)
    own_index = here * rows + jnp.arange(rows, dtype=jnp.int32)
    own_start = locate(own_index, doc_lengths)[1]
    places = own_index[None, :] - own_start
    queries = rotary(
        rms_scale(projected[..., :inner].reshape(micro, rows, HEADS, HEAD), q_gain[0]), places
    ).astype(jnp.bfloat16)
    keys = rotary(
        rms_scale(
            projected[..., inner : inner + key_width].reshape(micro, rows, KV_HEADS, HEAD),
            k_gain[0],
        ),
        places,
    ).astype(jnp.bfloat16)
    values = projected[..., inner + key_width :].astype(jnp.bfloat16)
    packed = jnp.concatenate([keys.reshape(micro, rows, key_width), values], axis=-1)
    gathered = lax.all_gather(packed, "dp", axis=1, tiled=True)
    latter_queries = queries[:, middle:]
    latter_index = own_index[middle:]
    group_index = jnp.stack([own_index[:middle], latter_index])
    group_doc = locate(group_index.reshape(-1), doc_lengths)[0].reshape(micro, 2, middle)
    arranged = jnp.stack([queries[:, :middle], latter_queries], axis=1)
    arranged = arranged.reshape(micro, 2, middle, KV_HEADS, GROUP, HEAD).transpose(0, 1, 3, 4, 2, 5)
    arranged = arranged.reshape(micro, 2, KV_HEADS, GROUP * middle, HEAD)
    row_index = jnp.tile(group_index, (1, GROUP))
    row_doc = jnp.tile(group_doc, (1, 1, GROUP))
    finished = []
    for which_micro in range(micro):
        for which_half in range(2):
            first = group_index[which_half, 0]
            key_first = jnp.clip(first + middle - reach, 0, total_tokens - reach)
            window = lax.dynamic_slice_in_dim(gathered[which_micro], key_first, reach, 0)
            key_index = key_first + jnp.arange(reach, dtype=jnp.int32)
            key_doc = locate(key_index, doc_lengths[which_micro : which_micro + 1])[0][0]
            key_part = window[:, :key_width].reshape(reach, KV_HEADS, HEAD)
            value_part = window[:, key_width:].reshape(reach, KV_HEADS, HEAD)
            allowed = (row_doc[which_micro, which_half][:, None] == key_doc[None, :]) & (
                row_index[which_half][:, None] >= key_index[None, :]
            )
            ratio = attend_rows(
                arranged[which_micro, which_half], key_part, value_part, allowed
            ).astype(jnp.bfloat16)
            finished.append(
                ratio.reshape(KV_HEADS, GROUP, middle, HEAD)
                .transpose(2, 0, 1, 3)
                .reshape(middle, inner)
            )
    former_part = jnp.stack(finished[0::2])
    latter_part = jnp.stack(finished[1::2])
    attended = jnp.concatenate([former_part, latter_part], axis=1).reshape(micro * rows, inner)
    mixed = jnp.dot(
        attended,
        lax.all_gather(w_out[0], "dp", axis=1, tiled=True),
        preferred_element_type=jnp.float32,
    )
    result = (resident + mixed).astype(jnp.bfloat16).reshape(1, micro, rows, width)
    return from_behind(result, "section", 1)


MIB = 1 << 20
VMEM = pl.BlockSpec(memory_space=pltpu.VMEM)
SMEM = pl.BlockSpec(memory_space=pltpu.SMEM)


def local_kernel(body, outs, inputs, scratch=(), flops=0, grant=12, scalars=1):
    moved = sum(math.prod(s.shape) * s.dtype.itemsize for s in (*outs, *inputs))
    return pl.pallas_call(
        body,
        out_shape=tuple(outs),
        in_specs=[SMEM] * scalars + [VMEM] * (len(inputs) - scalars),
        out_specs=tuple(VMEM for _ in outs),
        scratch_shapes=list(scratch),
        compiler_params=pltpu.CompilerParams(vmem_limit_bytes=grant * MIB),
        cost_estimate=pl.CostEstimate(flops=flops, bytes_accessed=moved, transcendentals=0),
    )(*inputs)


def prepare_kernel(
    here_ref,
    lengths_ref,
    spacing_ref,
    w_ref,
    place_ref,
    bias_ref,
    cos_ref,
    sin_ref,
    here_out,
    there_out,
):
    here = here_ref[0]
    line, column, core = here >> 2, (here >> 1) & 1, here & 1
    chip = here >> 1
    half = here_out.shape[0]
    here_out[...] = w_ref[pl.ds(pl.multiple_of(line * half, half), half), :]
    there_out[...] = w_ref[pl.ds(pl.multiple_of((1 - line) * half, half), half), :]
    documents = lengths_ref.shape[1]
    sizes = [lengths_ref[core, j] for j in range(documents)]
    ends = [sizes[0]]
    for size in sizes[1:]:
        ends.append(ends[-1] + size)

    def locate_in(index):
        number = jnp.zeros_like(index)
        start = jnp.zeros_like(index)
        for end, size in zip(ends, sizes):
            past = (end <= index).astype(jnp.int32)
            number = number + past
            start = start + past * size
        return number, start

    rows = cos_ref.shape[0] // 4
    lane = lax.broadcasted_iota(jnp.int32, (1, rows), 1)
    keys = []
    for bits in (0, 1, 4, 5, 2, 3, 6, 7):
        index = (here ^ bits) * rows + lane
        keys.append((index, locate_in(index)[0]))
    first_half = lax.broadcasted_iota(jnp.int32, (rows, HEAD), 1) < HEAD // 2
    for block, bits in enumerate((0, 1, 4, 5)):
        span = slice(block * rows, (block + 1) * rows)
        index = (here ^ bits) * rows + lax.broadcasted_iota(jnp.int32, (rows, HEAD), 0)
        number, start = locate_in(index)
        angle = (index - start).astype(jnp.float32) * spacing_ref[...]
        sine = jnp.sin(angle)
        cos_ref[span, :] = jnp.cos(angle)
        sin_ref[span, :] = jnp.where(first_half, -sine, sine)
        for other, (key_index, key_number) in enumerate(keys):
            allowed = (number[:, :1] == key_number) & (index[:, :1] >= key_index)
            bias_ref[span, other * rows : (other + 1) * rows] = jnp.where(
                allowed, 0.0, NEGATIVE
            ).astype(jnp.float32)

    def number_at(index):
        number = jnp.int32(0)
        for end in ends:
            number = number + jnp.where(end <= index, 1, 0)
        return number

    place_ref[0] = line
    place_ref[1] = column
    place_ref[2] = core
    for row, row_bits in enumerate((0, 2)):
        row_chip = chip ^ row_bits
        for key, key_bits in enumerate((0, 2, 1, 3)):
            key_chip = chip ^ key_bits
            shares = number_at(key_chip * 2 * rows + 2 * rows - 1) >= number_at(row_chip * 2 * rows)
            meets = (key_chip == row_chip) | ((key_chip < row_chip) & shares)
            place_ref[3 + 4 * row + key] = jnp.where(meets, 1, 0)


def project_block(projected, head, cosine, sine, gains_ref):
    is_value = head >= HEADS + KV_HEADS
    is_query = head < HEADS
    gain = jnp.where(is_query, gains_ref[0][...], gains_ref[1][...])
    scale = lax.rsqrt(jnp.mean(projected * projected, axis=-1, keepdims=True) + EPSILON)
    v = projected * scale * gain
    turned = v * cosine + pltpu.roll(v, HEAD // 2, 1) * sine
    return jnp.where(is_value, projected, turned).astype(jnp.bfloat16)


def project_with(normed, w_own, w_partner, middle, core, write):
    part = w_own.shape[0]
    whole = part // HEAD
    rest = part - whole * HEAD
    spread = whole + 1 if rest else whole
    for piece, turn in ((w_own, core), (w_partner, 1 - core)):
        start = pl.multiple_of(turn * rest, rest) if rest else 0
        projected = lax.dot_general(
            normed,
            piece[pl.ds(start, whole * HEAD), :],
            (((1,), (1,)), ((), ())),
            preferred_element_type=jnp.float32,
        )
        for block in range(whole):
            write(turn * spread + block, projected[:, block * HEAD : (block + 1) * HEAD])
    if rest:
        projected = lax.dot_general(
            normed, middle[...], (((1,), (1,)), ((), ())), preferred_element_type=jnp.float32
        )
        write(whole, projected)


def join_middle(core, middle, w_own, w_partner):
    part = w_own.shape[0]
    rest = part % HEAD
    if rest:
        for piece, turn in ((w_own, core), (w_partner, 1 - core)):
            there = pl.multiple_of(turn * rest, rest)
            here = pl.multiple_of((1 - turn) * (part - rest), rest)
            middle[pl.ds(there, rest), :] = piece[pl.ds(here, rest), :]


def norm_rows(core, x_ref, gain_ref):
    x = x_ref[core].astype(jnp.float32)
    scale = lax.rsqrt(jnp.mean(x * x, axis=-1, keepdims=True) + EPSILON)
    return (x * scale * gain_ref[...]).astype(jnp.bfloat16)


def norm_kernel(place_ref, x_ref, gain_ref, normed_ref):
    normed_ref[...] = norm_rows(place_ref[2], x_ref, gain_ref)


def project_own_kernel(
    offset,
    keep,
    place_ref,
    ready_ref,
    x_ref,
    gain_ref,
    w_own,
    w_partner,
    cos_ref,
    sin_ref,
    q_gain_ref,
    k_gain_ref,
    out_ref,
    normed_ref,
    *rest_refs,
):
    line, column, core = place_ref[0], place_ref[1], place_ref[2]
    *kept, middle = rest_refs
    join_middle(core, middle, w_own, w_partner)
    if keep:
        kept[0][...] = w_partner[...]
    rows = ready_ref.shape[0]
    normed_ref[:rows, :] = ready_ref[...]
    normed_ref[rows:, :] = norm_rows(core, x_ref, gain_ref)
    blocks = out_ref.shape[1] // HEAD
    span = slice(offset, offset + 2 * rows)

    def write(block, projected):
        head = (line * 2 + column) * blocks + block
        out_ref[:, pl.ds(pl.multiple_of(block * HEAD, HEAD), HEAD)] = project_block(
            projected, head, cos_ref[span, :], sin_ref[span, :], (q_gain_ref, k_gain_ref)
        )

    project_with(normed_ref[...], w_own, w_partner, middle, core, write)


def project_far_kernel(
    order,
    place_ref,
    normed0_ref,
    normed1_ref,
    w_own,
    w_partner,
    cos_ref,
    sin_ref,
    q_gain_ref,
    k_gain_ref,
    near0_ref,
    near1_ref,
    *refs,
):
    *outs, middle = refs
    full, swap_ref, kv_ref = outs[:3]
    line, column, core = place_ref[0], place_ref[1], place_ref[2]
    chip_width = near0_ref.shape[1]
    blocks = chip_width // HEAD
    which = 1 - column
    step = normed0_ref.shape[0]

    def copy_near(part, out):
        out[:, pl.ds(pl.multiple_of(column * chip_width, HEAD), chip_width)] = jnp.where(
            part == 0, near0_ref[...], near1_ref[...]
        )

    def project(part, out):
        normed = jnp.where(part == 0, normed0_ref[...], normed1_ref[...])
        span = pl.ds(pl.multiple_of(part * step, step), step)
        cosine, sine = cos_ref[span, :], sin_ref[span, :]

        def write(block, projected):
            head = (line * 2 + which) * blocks + block
            start = pl.multiple_of((which * blocks + block) * HEAD, HEAD)
            out[:, pl.ds(start, HEAD)] = project_block(
                projected, head, cosine, sine, (q_gain_ref, k_gain_ref)
            )

        project_with(normed, w_own, w_partner, middle, core, write)

    if order == 0:
        copy_near(column, full)

        @pl.when(column == 0)
        def _():
            join_middle(core, middle, w_own, w_partner)
            project(0, full)
    else:
        join_middle(core, middle, w_own, w_partner)
        copy_near(1 - column, full)
        project(1 - column, full)

        @pl.when(column == 1)
        def _():
            copy_near(1, outs[3])
            project(1, outs[3])

    inner = HEADS // 2 * HEAD
    pair = swap_ref.shape[1]
    half = pair // 2
    left = inner - pair

    @pl.when(line == 0)
    def _():
        swap_ref[...] = full[:, inner : inner + pair]
        kv_ref[...] = jnp.zeros_like(kv_ref)

    @pl.when(line == 1)
    def _():
        for out, skip in ((swap_ref, 0), (kv_ref, half)):
            out[:, :half] = full[:, left + skip : left + skip + half]
            out[:, half:] = full[:, left + skip + pair : left + skip + pair + half]


SHRINK = math.log2(math.e) / math.sqrt(HEAD)


def with_ones(values):
    return jnp.concatenate([values, jnp.ones_like(values)], axis=1)


def query_of(head, part, place_ref, full_refs, swap_refs):
    line, column = place_ref[0], place_ref[1]
    moved = swap_refs[0].shape[1] // HEAD
    start = pl.multiple_of(jnp.maximum(head - moved * line, 0) * HEAD, HEAD)
    lanes = pl.ds(start, HEAD)
    first = jnp.where(column == 0, full_refs[0][:, lanes], full_refs[2][:, lanes])
    q = jnp.where(column == part, first, full_refs[1][:, lanes])
    if head < moved:
        there = slice(head * HEAD, (head + 1) * HEAD)
        came = jnp.where(column == 1 - part, swap_refs[0][:, there], swap_refs[1][:, there])
        q = jnp.where(line == 1, came, q)
    return q


def scores_of(q, keys, bias):
    return (
        lax.dot_general(q, keys, (((1,), (1,)), ((), ())), preferred_element_type=jnp.float32)
        + bias
    )


def attend_near_kernel(
    part,
    place_ref,
    full0_ref,
    full1_ref,
    full2_ref,
    swap_a_ref,
    swap_b_ref,
    kv_a_ref,
    kv_b_ref,
    bias_ref,
    sum_ref,
    top_ref,
    near,
):
    line, column = place_ref[0], place_ref[1]
    rows = sum_ref.shape[0]
    half = kv_a_ref.shape[1] // 2
    heads = top_ref.shape[1] // HEAD
    span = slice(part * rows, (part + 1) * rows)
    for turn, swap_ref, kv_ref in ((1 - column, swap_a_ref, kv_a_ref), (column, swap_b_ref, kv_b_ref)):
        start = pl.multiple_of(turn * rows, rows)
        near[pl.ds(start, rows), :] = jnp.where(line == 0, swap_ref[...], kv_ref[...])

    def attend(block):
        keys = near[block, :half]
        values = with_ones(near[block, half:])
        bias = bias_ref[span, block]
        for head in range(heads):
            q = query_of(head, part, place_ref, (full0_ref, full1_ref, full2_ref), (swap_a_ref, swap_b_ref))
            s = scores_of(q, keys, bias)
            top = jnp.max(s, axis=-1, keepdims=True)
            weight = jnp.exp2((s - top) * SHRINK).astype(jnp.bfloat16)
            sum_ref[:, 2 * head * HEAD : 2 * (head + 1) * HEAD] = jnp.dot(
                weight, values, preferred_element_type=jnp.float32
            )
            top_ref[:, head * HEAD : (head + 1) * HEAD] = jnp.broadcast_to(top, (rows, HEAD))

    both = place_ref[3 + part * 4 + 1 - part] == 1

    @pl.when(both)
    def _():
        attend(slice(0, 2 * rows))

    @pl.when(jnp.logical_not(both))
    def _():
        attend(span)


def attend_far_kernel(
    part,
    place_ref,
    full0_ref,
    full1_ref,
    full2_ref,
    swap_a_ref,
    swap_b_ref,
    far0_ref,
    far1_ref,
    bias_ref,
    sum_ref,
    top_ref,
    out_ref,
):
    line, column = place_ref[0], place_ref[1]
    rows = out_ref.shape[0]
    half = far0_ref.shape[1] // 2
    heads = top_ref.shape[1] // HEAD
    span = slice(part * rows, (part + 1) * rows)
    block = 2 + column if part == 1 else 3 - column
    meets = place_ref[3 + part * 4 + block] == 1

    def finish(head, summed):
        out_ref[:, head * HEAD : (head + 1) * HEAD] = (
            summed[:, :HEAD] / summed[:, HEAD:]
        ).astype(jnp.bfloat16)

    @pl.when(jnp.logical_not(meets))
    def _():
        for head in range(heads):
            finish(head, sum_ref[:, 2 * head * HEAD : 2 * (head + 1) * HEAD])

    @pl.when(meets)
    def _():
        far = jnp.where(line == 0, far0_ref[...], far1_ref[...])
        keys = far[:, :half]
        values = with_ones(far[:, half:])
        bias = bias_ref[span, pl.ds(pl.multiple_of(block * rows, rows), rows)]
        for head in range(heads):
            q = query_of(head, part, place_ref, (full0_ref, full1_ref, full2_ref), (swap_a_ref, swap_b_ref))
            s = scores_of(q, keys, bias)
            before = top_ref[:, head * HEAD : (head + 1) * HEAD]
            top = jnp.maximum(before, jnp.max(s, axis=-1, keepdims=True))
            wide = jnp.concatenate([top] * (rows // HEAD), axis=1)
            weight = jnp.exp2((s - wide) * SHRINK).astype(jnp.bfloat16)
            kept = jnp.exp2((before - top) * SHRINK)
            kept = jnp.concatenate([kept, kept], axis=1)
            summed = sum_ref[:, 2 * head * HEAD : 2 * (head + 1) * HEAD] * kept + jnp.dot(
                weight, values, preferred_element_type=jnp.float32
            )
            finish(head, summed)


def attend_kernel(part, place_ref, *refs):
    fulls, swaps, kvs, fars, bias, (out_ref, near, sums, tops) = (
        refs[0:3], refs[3:5], refs[5:7], refs[7:9], refs[9], refs[10:14]
    )
    attend_near_kernel(part, place_ref, *fulls, *swaps, *kvs, bias, sums, tops, near)
    attend_far_kernel(part, place_ref, *fulls, *swaps, *fars, bias, sums, tops, out_ref)


def attend_share_kernel(part, place_ref, *refs):
    *before, w0_ref, w1_ref, out_ref, share0_ref, share1_ref = refs
    attend_far_kernel(part, place_ref, *before, out_ref)
    share_apart_kernel(place_ref, out_ref, w0_ref, w1_ref, share0_ref, share1_ref)


def share_apart_kernel(place_ref, a_ref, w0_ref, w1_ref, share0_ref, share1_ref):
    for w_ref, share_ref in ((w0_ref, share0_ref), (w1_ref, share1_ref)):
        share_ref[...] = jnp.dot(
            a_ref[...], w_ref[...], preferred_element_type=jnp.float32
        ).astype(jnp.bfloat16)


def share_two_kernel(place_ref, a_ref, w0_ref, w1_ref, w2_ref, w3_ref, out0_ref, out1_ref):
    share_kernel(place_ref, a_ref, w0_ref, w1_ref, out0_ref)
    share_kernel(place_ref, a_ref, w2_ref, w3_ref, out1_ref)


def share_kernel(place_ref, a_ref, w0_ref, w1_ref, out_ref):
    core = place_ref[2]
    width = w0_ref.shape[1]
    for turn, w_ref in enumerate((w0_ref, w1_ref)):
        start = pl.multiple_of((core ^ turn) * width, HEAD)
        out_ref[:, pl.ds(start, width)] = jnp.dot(
            a_ref[...], w_ref[...], preferred_element_type=jnp.float32
        ).astype(jnp.bfloat16)


def column_of(turn, turns, core, width):
    return 0 if len(turns) == 1 else pl.multiple_of((core ^ turn) * width, HEAD)


def finish_kernel(relative, turns, place_ref, a_ref, came_ref, x0_ref, x1_ref, *refs):
    w_refs, out_refs = refs[: len(turns)], refs[len(turns) :]
    chip = place_ref[0] * 2 + place_ref[1]
    core = place_ref[2]
    width = w_refs[0].shape[1]
    rows = x0_ref.shape[1]
    for turn, w_ref in zip(turns, w_refs):
        start = column_of(turn, turns, core, width)
        mixed = jnp.dot(
            a_ref[...], w_ref[...], preferred_element_type=jnp.float32
        ) + came_ref[:, pl.ds(start, width)].astype(jnp.float32)
        where = pl.multiple_of(((chip ^ relative) * 2 + (core ^ turn)) * width, HEAD)
        for number, x_ref in enumerate((x0_ref, x1_ref)):
            span = slice(number * rows, (number + 1) * rows)
            value = (
                x_ref[core, :, pl.ds(where, width)].astype(jnp.float32) + mixed[span, :]
            ).astype(jnp.bfloat16)
            if len(out_refs) == 1:
                out_refs[0][span, pl.ds(start, width)] = value
            else:
                out_refs[number][:, pl.ds(start, width)] = value


def place_of(cross, chunk, place_ref, wide):
    relative, turns = chunk
    core = place_ref[2] ^ cross
    chip = (place_ref[0] * 2 + place_ref[1]) ^ relative
    if len(turns) == 2:
        return core, pl.multiple_of(chip * wide, HEAD)
    return core, pl.multiple_of((chip * 2 + (core ^ turns[0])) * wide, HEAD)


def gather_kernel(place_ref, *refs):
    out_ref = refs[-1]
    rows = out_ref.shape[1]
    for cross in range(2):
        for number, chunk in enumerate(EARLY):
            piece = refs[cross * len(EARLY) + number]
            wide = piece.shape[1]
            core, start = place_of(cross, chunk, place_ref, wide)
            out_ref[core, :, pl.ds(start, wide)] = piece[cross * rows : (cross + 1) * rows, :]


def gather_last_kernel(place_ref, *refs):
    *pieces, before_ref, out_ref, semaphores = refs
    copies = []
    for cross in range(2):
        for number, chunk in enumerate(LATE):
            index = cross * len(LATE) + number
            wide = pieces[index].shape[1]
            core, start = place_of(cross, chunk, place_ref, wide)
            there = out_ref.at[core, :, pl.ds(start, wide)]
            copies.append(pltpu.make_async_copy(pieces[index], there, semaphores.at[index]))
    for copy in copies:
        copy.start()
    for copy in copies:
        copy.wait()


BOTH = (0, 1)
EARLY = ((2, (0,)), (2, (1,)), (0, BOTH))
LATE = ((3, BOTH), (1, (0,)), (1, (1,)))


def on_chip_grid(held, norm_gain, w_qkv, q_gain, k_gain, w_out, lengths):
    micro, rows, width = held.shape[1:]
    devices = lax.axis_size("dp")
    sections = lax.axis_size("section")
    here = lax.axis_index("dp")
    inner = w_out.shape[1]
    pair = KV_HEADS * HEAD

    def swap(value, bits, among=range(8)):
        return lax.ppermute(value, "dp", [(i, i ^ bits) for i in among])

    def after(value, *others):
        return lax.optimization_barrier((value, *others))[0]

    kept = held[0]
    w_in = w_qkv[0].T
    w_across = swap(w_in, 2)
    x_y = swap(kept, 4)
    x_c = swap(kept, 1)
    w_c = swap(w_in, 1)

    w_o = w_out[0]
    half = inner // 2
    own_rows = micro * 2 * rows
    spread = [-2.0 * math.log(THETA) / HEAD * (lane % (HEAD // 2)) for lane in range(HEAD)]
    spacing = jnp.asarray([[math.exp(value) for value in spread]], jnp.float32)
    f32, bf16 = jnp.float32, jnp.bfloat16
    shape = jax.ShapeDtypeStruct
    place, bias, cosine, sine, o_here, o_there = pl.pallas_call(
        prepare_kernel,
        out_shape=(
            shape((11,), jnp.int32),
            shape((own_rows, 2 * own_rows), f32),
            shape((own_rows, HEAD), f32),
            shape((own_rows, HEAD), f32),
            shape((half, w_o.shape[1]), bf16),
            shape((half, w_o.shape[1]), bf16),
        ),
        in_specs=[SMEM, SMEM, VMEM, VMEM],
        out_specs=(SMEM, VMEM, VMEM, VMEM, VMEM, VMEM),
        compiler_params=pltpu.CompilerParams(vmem_limit_bytes=12 * MIB),
    )(here[None], lengths[0], spacing, w_o)
    o_here_c = swap(o_here, 1)

    part = w_in.shape[0]
    flops = 2 * own_rows * width * 2 * part
    chip_rows = own_rows // 2

    def normalise(value):
        return local_kernel(
            norm_kernel, [shape((rows, width), bf16)], [place, value, norm_gain]
        )[0]

    def project_own(offset, ready, second, w_other, keep):
        return local_kernel(
            functools.partial(project_own_kernel, offset, keep),
            [shape((chip_rows, 2 * part), bf16), shape((chip_rows, width), bf16)]
            + [shape(w_c.shape, bf16)] * keep,
            [place, ready, second, norm_gain, w_in, w_other, cosine, sine, q_gain, k_gain],
            [pltpu.VMEM((HEAD, width), bf16)],
            flops // 2,
        )

    near0, normed0, w_c = project_own(0, normalise(kept), x_c, w_c, True)
    x_y, near0 = lax.optimization_barrier((x_y, near0))
    x_yc = swap(x_y, 1)
    ready = normalise(x_y)
    near1, normed1 = project_own(chip_rows, ready, x_yc, w_c, False)
    o_y = swap(o_there, 4)
    o_x = swap(after(o_here, x_y), 2)
    w_across_c = swap(after(w_across, ready), 1)

    def project_far(order, gate):
        return local_kernel(
            functools.partial(project_far_kernel, order),
            [shape((chip_rows, 4 * part), bf16)]
            + [shape((chip_rows, pair), bf16)] * 2
            + [shape((chip_rows, 4 * part), bf16)] * order,
            [
                place,
                normed0,
                normed1,
                w_across,
                w_across_c,
                cosine,
                sine,
                after(q_gain, gate),
                k_gain,
                near0,
                near1,
            ],
            [pltpu.VMEM((HEAD, width), bf16)],
            flops // 2,
        )

    full0, swapping_a, kv_b = project_far(0, near1)
    full1, swapping_b, kv_a, full2 = project_far(1, swapping_a)
    swap_a = swap(swapping_a, 4)
    swap_b = swap(swapping_b, 4)
    far1_a = swap(kv_a, 2, range(4, 8))
    far0_a = swap(swap_a, 2, range(4))
    o_y_c = swap(after(o_y, kv_a), 1)

    queries = (full0, full1, full2, swap_a, swap_b)
    partial_shapes = [shape((chip_rows, 2 * half), f32), shape((chip_rows, half), f32)]
    attend_flops = 2 * own_rows * own_rows * half
    chunk = 2 * w_o.shape[1]
    chunk_flops = own_rows * half * chunk
    chunk_shape = shape((chip_rows, chunk), bf16)
    half_shape = shape((chip_rows, chunk // 2), bf16)
    rows_shape = shape((chip_rows, half), bf16)
    sums_there = local_kernel(
        functools.partial(attend_near_kernel, 1),
        partial_shapes,
        [place, *queries, kv_a, kv_b, bias],
        [pltpu.VMEM((own_rows, pair), bf16)],
        attend_flops,
    )
    far1_b = swap(after(kv_b, sums_there[1]), 2, range(4, 8))
    far0_b = swap(after(swap_b, sums_there[1]), 2, range(4))
    o_xy = swap(after(o_y, sums_there[1]), 2)
    o_x_c = swap(after(o_x, sums_there[1]), 1)
    attended_there, share0, share0_c = local_kernel(
        functools.partial(attend_share_kernel, 1),
        [rows_shape, half_shape, half_shape],
        [place, *queries, far0_a, far1_a, bias, *sums_there, o_here, o_here_c],
        flops=attend_flops // 2 + chunk_flops,
    )

    ring = [
        (s * devices + i, (s + 1) % sections * devices + i)
        for s in range(sections)
        for i in range(devices)
    ]
    cross = [(source, target ^ 1) for source, target in ring]
    arrived = {}

    def finish(relative, turns, pieces):
        key = (relative, turns)
        late = key in LATE
        taken = [pieces[turn] for turn in turns]
        wide = sum(piece.shape[1] for piece in taken)
        values = local_kernel(
            functools.partial(finish_kernel, relative, turns),
            [shape((rows, wide), bf16)] * 2 if late else [shape((2 * rows, wide), bf16)],
            [place, attended_here, came[key], kept, x_c, *taken],
            flops=own_rows * half * wide,
        )
        arrived[0, key] = lax.ppermute(values[0], ("section", "dp"), ring)
        if late:
            arrived[1, key] = lax.ppermute(values[1], ("section", "dp"), cross)
        return values[0]

    came = {(2, (0,)): swap(share0, 4), (2, (1,)): swap(share0_c, 4)}
    (attended_here,) = local_kernel(
        functools.partial(attend_kernel, 0),
        [rows_shape],
        [place, *queries, kv_a, kv_b, far0_b, far1_b, after(bias, share0)],
        [pltpu.VMEM((own_rows, pair), bf16)]
        + [pltpu.VMEM(each.shape, each.dtype) for each in partial_shapes],
        2 * attend_flops,
    )
    share2, share1 = local_kernel(
        share_two_kernel,
        [chunk_shape, chunk_shape],
        [place, after(attended_there, share0), o_y, o_y_c, o_x, o_x_c],
        flops=2 * chunk_flops,
    )
    came[0, BOTH] = swap(share2, 4)
    came[3, BOTH] = swap(share1, 4)
    attended_here = after(attended_here, share1)
    last = finish(2, (0,), (o_y, o_y_c))
    attended_here = after(attended_here, last)
    last = finish(2, (1,), (o_y, o_y_c))
    attended_here = after(attended_here, last)
    o_xy_c = swap(after(o_xy, last), 1)
    last = finish(0, BOTH, (o_here, o_here_c))
    share3, share3_c = local_kernel(
        share_apart_kernel,
        [half_shape, half_shape],
        [place, after(attended_there, last), o_xy, o_xy_c],
        flops=chunk_flops,
    )
    came[1, (0,)] = swap(share3, 4)
    came[1, (1,)] = swap(share3_c, 4)
    last = finish(3, BOTH, (o_xy, o_xy_c))
    attended_here = after(attended_here, last)
    last = finish(1, (0,), (o_x, o_x_c))
    attended_here = after(attended_here, last)
    last = finish(1, (1,), (o_x, o_x_c))
    for key in EARLY:
        arrived[1, key] = swap(after(arrived[0, key], last), 1)
    (result,) = local_kernel(
        gather_kernel,
        [shape((micro, rows, width), bf16)],
        [place, *[arrived[turn, key] for turn in range(2) for key in EARLY]],
    )
    late = [arrived[turn, key] for turn in range(2) for key in LATE]
    result = pl.pallas_call(
        gather_last_kernel,
        out_shape=shape((micro, rows, width), bf16),
        in_specs=[SMEM] + [VMEM] * len(late) + [pl.BlockSpec(memory_space=pl.ANY)],
        out_specs=pl.BlockSpec(memory_space=pl.ANY),
        scratch_shapes=[pltpu.SemaphoreType.DMA((len(late),))],
        input_output_aliases={1 + len(late): 0},
        compiler_params=pltpu.CompilerParams(vmem_limit_bytes=4 * MIB),
    )(place, *late, result)
    return result[None]


def solution(mesh):
    devices = mesh.shape["dp"]

    def body(held, norm_gain, w_qkv, q_gain, k_gain, w_out, lengths):
        paired = KV_HEADS == 2 and HEADS == KV_HEADS * GROUP and held.shape[1] == 2
        whole_heads = (2 * w_qkv.shape[2]) % HEAD == 0
        form = on_chip_grid if devices == 8 and paired and whole_heads else on_device
        return form(held, norm_gain, w_qkv, q_gain, k_gain, w_out, lengths)

    in_specs = (
        P("section", None, "dp", None),
        P("section", None),
        P("section", None, "dp"),
        P("section", None),
        P("section", None),
        P("section", None, "dp"),
        P("section", None, None),
    )
    out_specs = P("section", None, "dp", None)
    return jax.shard_map(
        body, mesh=mesh, in_specs=in_specs, out_specs=out_specs, check_vma=False
    )
```

```python
import functools
import math

import jax
import jax.numpy as jnp
from jax import lax
from jax.experimental import pallas as pl
from jax.experimental.pallas import tpu as pltpu
from jax.sharding import PartitionSpec as P

HEADS = 16
KV_HEADS = 2
HEAD = 128
GROUP = 8


EPSILON = 1e-06
THETA = 1000000.0
NEGATIVE = -1e30


def from_behind(value, axis, steps):
    count = lax.axis_size(axis)
    pairs = [(source, (source + steps) % count) for source in range(count)]
    return lax.ppermute(value, axis, pairs)


def rms_scale(values, gain):
    return values * lax.rsqrt(jnp.mean(values * values, axis=-1, keepdims=True) + EPSILON) * gain


def rotary(values, places):
    width = values.shape[-1]
    middle = width // 2
    spacing = jnp.exp(jnp.arange(middle, dtype=jnp.float32) * (-2.0 * math.log(THETA) / width))
    angle = places.astype(jnp.float32)[..., None] * spacing
    cosine = jnp.cos(angle)[..., None, :]
    sine = jnp.sin(angle)[..., None, :]
    former = values[..., :middle]
    latter = values[..., middle:]
    return jnp.concatenate(
        [former * cosine - latter * sine, latter * cosine + former * sine], axis=-1
    )


def locate(positions, doc_lengths):
    ends = jnp.cumsum(doc_lengths, axis=-1)
    before = (ends[:, None, :] <= positions[None, :, None]).astype(jnp.int32)
    return (jnp.sum(before, axis=-1), jnp.sum(before * doc_lengths[:, None, :], axis=-1))


def attend_rows(query_rows, key_rows, value_rows, allowed):
    scores = jnp.einsum(
        "kqd,nkd->kqn", query_rows, key_rows, preferred_element_type=jnp.float32
    ) / math.sqrt(HEAD)
    highest = jnp.max(jnp.where(allowed[None], scores, NEGATIVE), axis=-1)
    weights = jnp.where(allowed[None], jnp.exp(scores - highest[..., None]), 0.0).astype(
        jnp.bfloat16
    )
    total = jnp.sum(weights.astype(jnp.float32), axis=-1)
    summed = jnp.einsum("kqn,nkd->kqd", weights, value_rows, preferred_element_type=jnp.float32)
    return summed / total[..., None]


def on_device(held, norm_gain, w_qkv, q_gain, k_gain, w_out, lengths):
    micro = held.shape[1]
    rows = held.shape[2]
    width = held.shape[3]
    inner = HEADS * HEAD
    key_width = KV_HEADS * HEAD
    middle = rows // 2
    devices = lax.axis_size("dp")
    here = lax.axis_index("dp")
    total_tokens = rows * devices
    doc_most = min(4096, total_tokens // 2)
    reach = min(total_tokens, doc_most + middle)
    doc_lengths = lengths[0]
    resident = held[0].astype(jnp.float32).reshape(micro * rows, width)
    normed = rms_scale(resident, norm_gain[0]).astype(jnp.bfloat16)
    projected = jnp.dot(
        normed,
        lax.all_gather(w_qkv[0], "dp", axis=1, tiled=True),
        preferred_element_type=jnp.float32,
    ).reshape(micro, rows, inner + 2 * key_width)
    own_index = here * rows + jnp.arange(rows, dtype=jnp.int32)
    own_start = locate(own_index, doc_lengths)[1]
    places = own_index[None, :] - own_start
    queries = rotary(
        rms_scale(projected[..., :inner].reshape(micro, rows, HEADS, HEAD), q_gain[0]), places
    ).astype(jnp.bfloat16)
    keys = rotary(
        rms_scale(
            projected[..., inner : inner + key_width].reshape(micro, rows, KV_HEADS, HEAD),
            k_gain[0],
        ),
        places,
    ).astype(jnp.bfloat16)
    values = projected[..., inner + key_width :].astype(jnp.bfloat16)
    packed = jnp.concatenate([keys.reshape(micro, rows, key_width), values], axis=-1)
    gathered = lax.all_gather(packed, "dp", axis=1, tiled=True)
    latter_queries = queries[:, middle:]
    latter_index = own_index[middle:]
    group_index = jnp.stack([own_index[:middle], latter_index])
    group_doc = locate(group_index.reshape(-1), doc_lengths)[0].reshape(micro, 2, middle)
    arranged = jnp.stack([queries[:, :middle], latter_queries], axis=1)
    arranged = arranged.reshape(micro, 2, middle, KV_HEADS, GROUP, HEAD).transpose(0, 1, 3, 4, 2, 5)
    arranged = arranged.reshape(micro, 2, KV_HEADS, GROUP * middle, HEAD)
    row_index = jnp.tile(group_index, (1, GROUP))
    row_doc = jnp.tile(group_doc, (1, 1, GROUP))
    finished = []
    for which_micro in range(micro):
        for which_half in range(2):
            first = group_index[which_half, 0]
            key_first = jnp.clip(first + middle - reach, 0, total_tokens - reach)
            window = lax.dynamic_slice_in_dim(gathered[which_micro], key_first, reach, 0)
            key_index = key_first + jnp.arange(reach, dtype=jnp.int32)
            key_doc = locate(key_index, doc_lengths[which_micro : which_micro + 1])[0][0]
            key_part = window[:, :key_width].reshape(reach, KV_HEADS, HEAD)
            value_part = window[:, key_width:].reshape(reach, KV_HEADS, HEAD)
            allowed = (row_doc[which_micro, which_half][:, None] == key_doc[None, :]) & (
                row_index[which_half][:, None] >= key_index[None, :]
            )
            ratio = attend_rows(
                arranged[which_micro, which_half], key_part, value_part, allowed
            ).astype(jnp.bfloat16)
            finished.append(
                ratio.reshape(KV_HEADS, GROUP, middle, HEAD)
                .transpose(2, 0, 1, 3)
                .reshape(middle, inner)
            )
    former_part = jnp.stack(finished[0::2])
    latter_part = jnp.stack(finished[1::2])
    attended = jnp.concatenate([former_part, latter_part], axis=1).reshape(micro * rows, inner)
    mixed = jnp.dot(
        attended,
        lax.all_gather(w_out[0], "dp", axis=1, tiled=True),
        preferred_element_type=jnp.float32,
    )
    result = (resident + mixed).astype(jnp.bfloat16).reshape(1, micro, rows, width)
    return from_behind(result, "section", 1)


MIB = 1 << 20
VMEM = pl.BlockSpec(memory_space=pltpu.VMEM)
SMEM = pl.BlockSpec(memory_space=pltpu.SMEM)


def local_kernel(body, outs, inputs, scratch=(), flops=0, grant=12, scalars=1):
    moved = sum(math.prod(s.shape) * s.dtype.itemsize for s in (*outs, *inputs))
    return pl.pallas_call(
        body,
        out_shape=tuple(outs),
        in_specs=[SMEM] * scalars + [VMEM] * (len(inputs) - scalars),
        out_specs=tuple(VMEM for _ in outs),
        scratch_shapes=list(scratch),
        compiler_params=pltpu.CompilerParams(vmem_limit_bytes=grant * MIB),
        cost_estimate=pl.CostEstimate(flops=flops, bytes_accessed=moved, transcendentals=0),
    )(*inputs)


def prepare_kernel(
    here_ref,
    lengths_ref,
    spacing_ref,
    w_ref,
    place_ref,
    bias_ref,
    cos_ref,
    sin_ref,
    here_out,
    there_out,
):
    here = here_ref[0]
    line, column, core = here >> 2, (here >> 1) & 1, here & 1
    chip = here >> 1
    half = here_out.shape[0]
    here_out[...] = w_ref[pl.ds(pl.multiple_of(line * half, half), half), :]
    there_out[...] = w_ref[pl.ds(pl.multiple_of((1 - line) * half, half), half), :]
    documents = lengths_ref.shape[1]
    sizes = [lengths_ref[core, j] for j in range(documents)]
    ends = [sizes[0]]
    for size in sizes[1:]:
        ends.append(ends[-1] + size)

    def locate_in(index):
        number = jnp.zeros_like(index)
        start = jnp.zeros_like(index)
        for end, size in zip(ends, sizes):
            past = (end <= index).astype(jnp.int32)
            number = number + past
            start = start + past * size
        return number, start

    rows = cos_ref.shape[0] // 4
    lane = lax.broadcasted_iota(jnp.int32, (1, rows), 1)
    keys = []
    for bits in (0, 1, 4, 5, 2, 3, 6, 7):
        index = (here ^ bits) * rows + lane
        keys.append((index, locate_in(index)[0]))
    first_half = lax.broadcasted_iota(jnp.int32, (rows, HEAD), 1) < HEAD // 2
    for block, bits in enumerate((0, 1, 4, 5)):
        span = slice(block * rows, (block + 1) * rows)
        index = (here ^ bits) * rows + lax.broadcasted_iota(jnp.int32, (rows, HEAD), 0)
        number, start = locate_in(index)
        angle = (index - start).astype(jnp.float32) * spacing_ref[...]
        sine = jnp.sin(angle)
        cos_ref[span, :] = jnp.cos(angle)
        sin_ref[span, :] = jnp.where(first_half, -sine, sine)
        for other, (key_index, key_number) in enumerate(keys):
            allowed = (number[:, :1] == key_number) & (index[:, :1] >= key_index)
            bias_ref[span, other * rows : (other + 1) * rows] = jnp.where(
                allowed, 0.0, NEGATIVE
            ).astype(jnp.float32)

    def number_at(index):
        number = jnp.int32(0)
        for end in ends:
            number = number + jnp.where(end <= index, 1, 0)
        return number

    place_ref[0] = line
    place_ref[1] = column
    place_ref[2] = core
    for row, row_bits in enumerate((0, 2)):
        row_chip = chip ^ row_bits
        for key, key_bits in enumerate((0, 2, 1, 3)):
            key_chip = chip ^ key_bits
            shares = number_at(key_chip * 2 * rows + 2 * rows - 1) >= number_at(row_chip * 2 * rows)
            meets = (key_chip == row_chip) | ((key_chip < row_chip) & shares)
            place_ref[3 + 4 * row + key] = jnp.where(meets, 1, 0)


def project_block(projected, head, cosine, sine, gains_ref):
    is_value = head >= HEADS + KV_HEADS
    is_query = head < HEADS
    gain = jnp.where(is_query, gains_ref[0][...], gains_ref[1][...])
    scale = lax.rsqrt(jnp.mean(projected * projected, axis=-1, keepdims=True) + EPSILON)
    v = projected * scale * gain
    turned = v * cosine + pltpu.roll(v, HEAD // 2, 1) * sine
    return jnp.where(is_value, projected, turned).astype(jnp.bfloat16)


def project_with(normed, w_own, w_partner, middle, core, write):
    part = w_own.shape[0]
    whole = part // HEAD
    rest = part - whole * HEAD
    spread = whole + 1 if rest else whole
    for piece, turn in ((w_own, core), (w_partner, 1 - core)):
        start = pl.multiple_of(turn * rest, rest) if rest else 0
        projected = lax.dot_general(
            normed,
            piece[pl.ds(start, whole * HEAD), :],
            (((1,), (1,)), ((), ())),
            preferred_element_type=jnp.float32,
        )
        for block in range(whole):
            write(turn * spread + block, projected[:, block * HEAD : (block + 1) * HEAD])
    if rest:
        projected = lax.dot_general(
            normed, middle[...], (((1,), (1,)), ((), ())), preferred_element_type=jnp.float32
        )
        write(whole, projected)


def join_middle(core, middle, w_own, w_partner):
    part = w_own.shape[0]
    rest = part % HEAD
    if rest:
        for piece, turn in ((w_own, core), (w_partner, 1 - core)):
            there = pl.multiple_of(turn * rest, rest)
            here = pl.multiple_of((1 - turn) * (part - rest), rest)
            middle[pl.ds(there, rest), :] = piece[pl.ds(here, rest), :]


def norm_rows(core, x_ref, gain_ref):
    x = x_ref[core].astype(jnp.float32)
    scale = lax.rsqrt(jnp.mean(x * x, axis=-1, keepdims=True) + EPSILON)
    return (x * scale * gain_ref[...]).astype(jnp.bfloat16)


def norm_kernel(place_ref, x_ref, gain_ref, normed_ref):
    normed_ref[...] = norm_rows(place_ref[2], x_ref, gain_ref)


def project_own_kernel(
    offset,
    keep,
    place_ref,
    ready_ref,
    x_ref,
    gain_ref,
    w_own,
    w_partner,
    cos_ref,
    sin_ref,
    q_gain_ref,
    k_gain_ref,
    out_ref,
    normed_ref,
    *rest_refs,
):
    line, column, core = place_ref[0], place_ref[1], place_ref[2]
    *kept, middle = rest_refs
    join_middle(core, middle, w_own, w_partner)
    if keep:
        kept[0][...] = w_partner[...]
    rows = ready_ref.shape[0]
    normed_ref[:rows, :] = ready_ref[...]
    normed_ref[rows:, :] = norm_rows(core, x_ref, gain_ref)
    blocks = out_ref.shape[1] // HEAD
    span = slice(offset, offset + 2 * rows)

    def write(block, projected):
        head = (line * 2 + column) * blocks + block
        out_ref[:, pl.ds(pl.multiple_of(block * HEAD, HEAD), HEAD)] = project_block(
            projected, head, cos_ref[span, :], sin_ref[span, :], (q_gain_ref, k_gain_ref)
        )

    project_with(normed_ref[...], w_own, w_partner, middle, core, write)


def project_far_kernel(
    order,
    place_ref,
    normed0_ref,
    normed1_ref,
    w_own,
    w_partner,
    cos_ref,
    sin_ref,
    q_gain_ref,
    k_gain_ref,
    near0_ref,
    near1_ref,
    *refs,
):
    *outs, middle = refs
    full, swap_ref, kv_ref = outs[:3]
    line, column, core = place_ref[0], place_ref[1], place_ref[2]
    chip_width = near0_ref.shape[1]
    blocks = chip_width // HEAD
    which = 1 - column
    step = normed0_ref.shape[0]

    def copy_near(part, out):
        out[:, pl.ds(pl.multiple_of(column * chip_width, HEAD), chip_width)] = jnp.where(
            part == 0, near0_ref[...], near1_ref[...]
        )

    def project(part, out):
        normed = jnp.where(part == 0, normed0_ref[...], normed1_ref[...])
        span = pl.ds(pl.multiple_of(part * step, step), step)
        cosine, sine = cos_ref[span, :], sin_ref[span, :]

        def write(block, projected):
            head = (line * 2 + which) * blocks + block
            start = pl.multiple_of((which * blocks + block) * HEAD, HEAD)
            out[:, pl.ds(start, HEAD)] = project_block(
                projected, head, cosine, sine, (q_gain_ref, k_gain_ref)
            )

        project_with(normed, w_own, w_partner, middle, core, write)

    if order == 0:
        copy_near(column, full)

        @pl.when(column == 0)
        def _():
            join_middle(core, middle, w_own, w_partner)
            project(0, full)
    else:
        join_middle(core, middle, w_own, w_partner)
        copy_near(1 - column, full)
        project(1 - column, full)

        @pl.when(column == 1)
        def _():
            copy_near(1, outs[3])
            project(1, outs[3])

    inner = HEADS // 2 * HEAD
    pair = swap_ref.shape[1]
    half = pair // 2
    left = inner - pair

    @pl.when(line == 0)
    def _():
        swap_ref[...] = full[:, inner : inner + pair]
        kv_ref[...] = jnp.zeros_like(kv_ref)

    @pl.when(line == 1)
    def _():
        for out, skip in ((swap_ref, 0), (kv_ref, half)):
            out[:, :half] = full[:, left + skip : left + skip + half]
            out[:, half:] = full[:, left + skip + pair : left + skip + pair + half]


SHRINK = math.log2(math.e) / math.sqrt(HEAD)


def with_ones(values):
    return jnp.concatenate([values, jnp.ones_like(values)], axis=1)


def query_of(head, part, place_ref, full_refs, swap_refs):
    line, column = place_ref[0], place_ref[1]
    moved = swap_refs[0].shape[1] // HEAD
    start = pl.multiple_of(jnp.maximum(head - moved * line, 0) * HEAD, HEAD)
    lanes = pl.ds(start, HEAD)
    first = jnp.where(column == 0, full_refs[0][:, lanes], full_refs[2][:, lanes])
    q = jnp.where(column == part, first, full_refs[1][:, lanes])
    if head < moved:
        there = slice(head * HEAD, (head + 1) * HEAD)
        came = jnp.where(column == 1 - part, swap_refs[0][:, there], swap_refs[1][:, there])
        q = jnp.where(line == 1, came, q)
    return q


def scores_of(q, keys, bias):
    return (
        lax.dot_general(q, keys, (((1,), (1,)), ((), ())), preferred_element_type=jnp.float32)
        + bias
    )


def attend_near_kernel(
    part,
    place_ref,
    full0_ref,
    full1_ref,
    full2_ref,
    swap_a_ref,
    swap_b_ref,
    kv_a_ref,
    kv_b_ref,
    bias_ref,
    sum_ref,
    top_ref,
    near,
):
    line, column = place_ref[0], place_ref[1]
    rows = sum_ref.shape[0]
    half = kv_a_ref.shape[1] // 2
    heads = top_ref.shape[1] // HEAD
    span = slice(part * rows, (part + 1) * rows)
    for turn, swap_ref, kv_ref in ((1 - column, swap_a_ref, kv_a_ref), (column, swap_b_ref, kv_b_ref)):
        start = pl.multiple_of(turn * rows, rows)
        near[pl.ds(start, rows), :] = jnp.where(line == 0, swap_ref[...], kv_ref[...])

    def attend(block):
        keys = near[block, :half]
        values = with_ones(near[block, half:])
        bias = bias_ref[span, block]
        for head in range(heads):
            q = query_of(head, part, place_ref, (full0_ref, full1_ref, full2_ref), (swap_a_ref, swap_b_ref))
            s = scores_of(q, keys, bias)
            top = jnp.max(s, axis=-1, keepdims=True)
            weight = jnp.exp2((s - top) * SHRINK).astype(jnp.bfloat16)
            sum_ref[:, 2 * head * HEAD : 2 * (head + 1) * HEAD] = jnp.dot(
                weight, values, preferred_element_type=jnp.float32
            )
            top_ref[:, head * HEAD : (head + 1) * HEAD] = jnp.broadcast_to(top, (rows, HEAD))

    both = place_ref[3 + part * 4 + 1 - part] == 1

    @pl.when(both)
    def _():
        attend(slice(0, 2 * rows))

    @pl.when(jnp.logical_not(both))
    def _():
        attend(span)


def attend_far_kernel(
    part,
    place_ref,
    full0_ref,
    full1_ref,
    full2_ref,
    swap_a_ref,
    swap_b_ref,
    far0_ref,
    far1_ref,
    bias_ref,
    sum_ref,
    top_ref,
    out_ref,
):
    line, column = place_ref[0], place_ref[1]
    rows = out_ref.shape[0]
    half = far0_ref.shape[1] // 2
    heads = top_ref.shape[1] // HEAD
    span = slice(part * rows, (part + 1) * rows)
    block = 2 + column if part == 1 else 3 - column
    meets = place_ref[3 + part * 4 + block] == 1

    def finish(head, summed):
        out_ref[:, head * HEAD : (head + 1) * HEAD] = (
            summed[:, :HEAD] / summed[:, HEAD:]
        ).astype(jnp.bfloat16)

    @pl.when(jnp.logical_not(meets))
    def _():
        for head in range(heads):
            finish(head, sum_ref[:, 2 * head * HEAD : 2 * (head + 1) * HEAD])

    @pl.when(meets)
    def _():
        far = jnp.where(line == 0, far0_ref[...], far1_ref[...])
        keys = far[:, :half]
        values = with_ones(far[:, half:])
        bias = bias_ref[span, pl.ds(pl.multiple_of(block * rows, rows), rows)]
        for head in range(heads):
            q = query_of(head, part, place_ref, (full0_ref, full1_ref, full2_ref), (swap_a_ref, swap_b_ref))
            s = scores_of(q, keys, bias)
            before = top_ref[:, head * HEAD : (head + 1) * HEAD]
            top = jnp.maximum(before, jnp.max(s, axis=-1, keepdims=True))
            wide = jnp.concatenate([top] * (rows // HEAD), axis=1)
            weight = jnp.exp2((s - wide) * SHRINK).astype(jnp.bfloat16)
            kept = jnp.exp2((before - top) * SHRINK)
            kept = jnp.concatenate([kept, kept], axis=1)
            summed = sum_ref[:, 2 * head * HEAD : 2 * (head + 1) * HEAD] * kept + jnp.dot(
                weight, values, preferred_element_type=jnp.float32
            )
            finish(head, summed)


def attend_kernel(part, place_ref, *refs):
    fulls, swaps, kvs, fars, bias, (out_ref, near, sums, tops) = (
        refs[0:3], refs[3:5], refs[5:7], refs[7:9], refs[9], refs[10:14]
    )
    attend_near_kernel(part, place_ref, *fulls, *swaps, *kvs, bias, sums, tops, near)
    attend_far_kernel(part, place_ref, *fulls, *swaps, *fars, bias, sums, tops, out_ref)


def attend_share_kernel(part, place_ref, *refs):
    *before, w0_ref, w1_ref, out_ref, share_ref = refs
    attend_far_kernel(part, place_ref, *before, out_ref)
    share_kernel(place_ref, out_ref, w0_ref, w1_ref, share_ref)


def share_apart_kernel(place_ref, a_ref, w0_ref, w1_ref, share0_ref, share1_ref):
    for w_ref, share_ref in ((w0_ref, share0_ref), (w1_ref, share1_ref)):
        share_ref[...] = jnp.dot(
            a_ref[...], w_ref[...], preferred_element_type=jnp.float32
        ).astype(jnp.bfloat16)


def share_two_kernel(place_ref, a_ref, w0_ref, w1_ref, w2_ref, w3_ref, out0_ref, out1_ref):
    share_kernel(place_ref, a_ref, w0_ref, w1_ref, out0_ref)
    share_kernel(place_ref, a_ref, w2_ref, w3_ref, out1_ref)


def share_kernel(place_ref, a_ref, w0_ref, w1_ref, out_ref):
    core = place_ref[2]
    width = w0_ref.shape[1]
    for turn, w_ref in enumerate((w0_ref, w1_ref)):
        start = pl.multiple_of((core ^ turn) * width, HEAD)
        out_ref[:, pl.ds(start, width)] = jnp.dot(
            a_ref[...], w_ref[...], preferred_element_type=jnp.float32
        ).astype(jnp.bfloat16)


def column_of(turn, turns, core, width):
    return 0 if len(turns) == 1 else pl.multiple_of((core ^ turn) * width, HEAD)


def finish_kernel(relative, turns, place_ref, a_ref, came_ref, x0_ref, x1_ref, *refs):
    w_refs, out_refs = refs[: len(turns)], refs[len(turns) :]
    chip = place_ref[0] * 2 + place_ref[1]
    core = place_ref[2]
    width = w_refs[0].shape[1]
    rows = x0_ref.shape[1]
    for turn, w_ref in zip(turns, w_refs):
        start = column_of(turn, turns, core, width)
        mixed = jnp.dot(
            a_ref[...], w_ref[...], preferred_element_type=jnp.float32
        ) + came_ref[:, pl.ds(start, width)].astype(jnp.float32)
        where = pl.multiple_of(((chip ^ relative) * 2 + (core ^ turn)) * width, HEAD)
        for number, x_ref in enumerate((x0_ref, x1_ref)):
            span = slice(number * rows, (number + 1) * rows)
            value = (
                x_ref[core, :, pl.ds(where, width)].astype(jnp.float32) + mixed[span, :]
            ).astype(jnp.bfloat16)
            if len(out_refs) == 1:
                out_refs[0][span, pl.ds(start, width)] = value
            else:
                out_refs[number][:, pl.ds(start, width)] = value


def place_of(cross, chunk, place_ref, wide):
    relative, turns = chunk
    core = place_ref[2] ^ cross
    chip = (place_ref[0] * 2 + place_ref[1]) ^ relative
    if len(turns) == 2:
        return core, pl.multiple_of(chip * wide, HEAD)
    return core, pl.multiple_of((chip * 2 + (core ^ turns[0])) * wide, HEAD)


def gather_kernel(place_ref, *refs):
    out_ref = refs[-1]
    rows = out_ref.shape[1]
    for cross in range(2):
        for number, chunk in enumerate(EARLY):
            piece = refs[cross * len(EARLY) + number]
            wide = piece.shape[1]
            core, start = place_of(cross, chunk, place_ref, wide)
            out_ref[core, :, pl.ds(start, wide)] = piece[cross * rows : (cross + 1) * rows, :]


def gather_last_kernel(place_ref, *refs):
    *pieces, before_ref, out_ref, semaphores = refs
    copies = []
    for cross in range(2):
        for number, chunk in enumerate(LATE):
            index = cross * len(LATE) + number
            wide = pieces[index].shape[1]
            core, start = place_of(cross, chunk, place_ref, wide)
            there = out_ref.at[core, :, pl.ds(start, wide)]
            copies.append(pltpu.make_async_copy(pieces[index], there, semaphores.at[index]))
    for copy in copies:
        copy.start()
    for copy in copies:
        copy.wait()


BOTH = (0, 1)
EARLY = ((2, BOTH), (0, BOTH))
LATE = ((3, BOTH), (1, (0,)), (1, (1,)))


def on_chip_grid(held, norm_gain, w_qkv, q_gain, k_gain, w_out, lengths):
    micro, rows, width = held.shape[1:]
    devices = lax.axis_size("dp")
    sections = lax.axis_size("section")
    here = lax.axis_index("dp")
    inner = w_out.shape[1]
    pair = KV_HEADS * HEAD

    def swap(value, bits, among=range(8)):
        return lax.ppermute(value, "dp", [(i, i ^ bits) for i in among])

    def after(value, *others):
        return lax.optimization_barrier((value, *others))[0]

    kept = held[0]
    w_in = w_qkv[0].T
    w_across = swap(w_in, 2)
    x_y = swap(kept, 4)
    x_c = swap(kept, 1)
    w_c = swap(w_in, 1)

    w_o = w_out[0]
    half = inner // 2
    own_rows = micro * 2 * rows
    spread = [-2.0 * math.log(THETA) / HEAD * (lane % (HEAD // 2)) for lane in range(HEAD)]
    spacing = jnp.asarray([[math.exp(value) for value in spread]], jnp.float32)
    f32, bf16 = jnp.float32, jnp.bfloat16
    shape = jax.ShapeDtypeStruct
    place, bias, cosine, sine, o_here, o_there = pl.pallas_call(
        prepare_kernel,
        out_shape=(
            shape((11,), jnp.int32),
            shape((own_rows, 2 * own_rows), f32),
            shape((own_rows, HEAD), f32),
            shape((own_rows, HEAD), f32),
            shape((half, w_o.shape[1]), bf16),
            shape((half, w_o.shape[1]), bf16),
        ),
        in_specs=[SMEM, SMEM, VMEM, VMEM],
        out_specs=(SMEM, VMEM, VMEM, VMEM, VMEM, VMEM),
        compiler_params=pltpu.CompilerParams(vmem_limit_bytes=12 * MIB),
    )(here[None], lengths[0], spacing, w_o)
    o_here_c = swap(o_here, 1)

    part = w_in.shape[0]
    flops = 2 * own_rows * width * 2 * part
    chip_rows = own_rows // 2

    def normalise(value):
        return local_kernel(
            norm_kernel, [shape((rows, width), bf16)], [place, value, norm_gain]
        )[0]

    def project_own(offset, ready, second, w_other, keep):
        return local_kernel(
            functools.partial(project_own_kernel, offset, keep),
            [shape((chip_rows, 2 * part), bf16), shape((chip_rows, width), bf16)]
            + [shape(w_c.shape, bf16)] * keep,
            [place, ready, second, norm_gain, w_in, w_other, cosine, sine, q_gain, k_gain],
            [pltpu.VMEM((HEAD, width), bf16)],
            flops // 2,
        )

    near0, normed0, w_c = project_own(0, normalise(kept), x_c, w_c, True)
    x_y, near0 = lax.optimization_barrier((x_y, near0))
    x_yc = swap(x_y, 1)
    ready = normalise(x_y)
    near1, normed1 = project_own(chip_rows, ready, x_yc, w_c, False)
    o_y = swap(o_there, 4)
    o_x = swap(after(o_here, x_y), 2)
    w_across_c = swap(after(w_across, ready), 1)

    def project_far(order, gate):
        return local_kernel(
            functools.partial(project_far_kernel, order),
            [shape((chip_rows, 4 * part), bf16)]
            + [shape((chip_rows, pair), bf16)] * 2
            + [shape((chip_rows, 4 * part), bf16)] * order,
            [
                place,
                normed0,
                normed1,
                w_across,
                w_across_c,
                cosine,
                sine,
                after(q_gain, gate),
                k_gain,
                near0,
                near1,
            ],
            [pltpu.VMEM((HEAD, width), bf16)],
            flops // 2,
        )

    full0, swapping_a, kv_b = project_far(0, near1)
    full1, swapping_b, kv_a, full2 = project_far(1, swapping_a)
    swap_a = swap(swapping_a, 4)
    swap_b = swap(swapping_b, 4)
    far1_a = swap(kv_a, 2, range(4, 8))
    far0_a = swap(swap_a, 2, range(4))
    o_y_c = swap(after(o_y, kv_a), 1)

    queries = (full0, full1, full2, swap_a, swap_b)
    partial_shapes = [shape((chip_rows, 2 * half), f32), shape((chip_rows, half), f32)]
    attend_flops = 2 * own_rows * own_rows * half
    chunk = 2 * w_o.shape[1]
    chunk_flops = own_rows * half * chunk
    chunk_shape = shape((chip_rows, chunk), bf16)
    half_shape = shape((chip_rows, chunk // 2), bf16)
    rows_shape = shape((chip_rows, half), bf16)
    sums_there = local_kernel(
        functools.partial(attend_near_kernel, 1),
        partial_shapes,
        [place, *queries, kv_a, kv_b, bias],
        [pltpu.VMEM((own_rows, pair), bf16)],
        attend_flops,
    )
    far1_b = swap(kv_b, 2, range(4, 8))
    far0_b = swap(swap_b, 2, range(4))
    o_xy = swap(after(o_y, sums_there[1]), 2)
    o_x_c = swap(after(o_x, sums_there[1]), 1)
    attended_there, share0 = local_kernel(
        functools.partial(attend_share_kernel, 1),
        [rows_shape, chunk_shape],
        [place, *queries, far0_a, far1_a, bias, *sums_there, o_here, o_here_c],
        flops=attend_flops // 2 + chunk_flops,
    )

    ring = [
        (s * devices + i, (s + 1) % sections * devices + i)
        for s in range(sections)
        for i in range(devices)
    ]
    cross = [(source, target ^ 1) for source, target in ring]
    arrived = {}

    def finish(relative, turns, pieces):
        key = (relative, turns)
        late = key in LATE
        taken = [pieces[turn] for turn in turns]
        wide = sum(piece.shape[1] for piece in taken)
        values = local_kernel(
            functools.partial(finish_kernel, relative, turns),
            [shape((rows, wide), bf16)] * 2 if late else [shape((2 * rows, wide), bf16)],
            [place, attended_here, came[key], kept, x_c, *taken],
            flops=own_rows * half * wide,
        )
        arrived[0, key] = lax.ppermute(values[0], ("section", "dp"), ring)
        if late:
            arrived[1, key] = lax.ppermute(values[1], ("section", "dp"), cross)
        return values[0]

    came = {(2, BOTH): swap(share0, 4)}
    (attended_here,) = local_kernel(
        functools.partial(attend_kernel, 0),
        [rows_shape],
        [place, *queries, kv_a, kv_b, far0_b, far1_b, after(bias, share0)],
        [pltpu.VMEM((own_rows, pair), bf16)]
        + [pltpu.VMEM(each.shape, each.dtype) for each in partial_shapes],
        2 * attend_flops,
    )
    share2, share1 = local_kernel(
        share_two_kernel,
        [chunk_shape, chunk_shape],
        [place, after(attended_there, share0), o_y, o_y_c, o_x, o_x_c],
        flops=2 * chunk_flops,
    )
    came[0, BOTH] = swap(share2, 4)
    came[3, BOTH] = swap(share1, 4)
    attended_here = after(attended_here, share1)
    last = finish(2, BOTH, (o_y, o_y_c))
    attended_here = after(attended_here, last)
    o_xy_c = swap(after(o_xy, last), 1)
    last = finish(0, BOTH, (o_here, o_here_c))
    share3, share3_c = local_kernel(
        share_apart_kernel,
        [half_shape, half_shape],
        [place, after(attended_there, last), o_xy, o_xy_c],
        flops=chunk_flops,
    )
    came[1, (0,)] = swap(share3, 4)
    came[1, (1,)] = swap(share3_c, 4)
    last = finish(3, BOTH, (o_xy, o_xy_c))
    attended_here = after(attended_here, last)
    last = finish(1, (0,), (o_x, o_x_c))
    attended_here = after(attended_here, last)
    last = finish(1, (1,), (o_x, o_x_c))
    for key in EARLY:
        arrived[1, key] = swap(after(arrived[0, key], last), 1)
    (result,) = local_kernel(
        gather_kernel,
        [shape((micro, rows, width), bf16)],
        [place, *[arrived[turn, key] for turn in range(2) for key in EARLY]],
    )
    late = [arrived[turn, key] for turn in range(2) for key in LATE]
    result = pl.pallas_call(
        gather_last_kernel,
        out_shape=shape((micro, rows, width), bf16),
        in_specs=[SMEM] + [VMEM] * len(late) + [pl.BlockSpec(memory_space=pl.ANY)],
        out_specs=pl.BlockSpec(memory_space=pl.ANY),
        scratch_shapes=[pltpu.SemaphoreType.DMA((len(late),))],
        input_output_aliases={1 + len(late): 0},
        compiler_params=pltpu.CompilerParams(vmem_limit_bytes=4 * MIB),
    )(place, *late, result)
    return result[None]


def solution(mesh):
    devices = mesh.shape["dp"]

    def body(held, norm_gain, w_qkv, q_gain, k_gain, w_out, lengths):
        paired = KV_HEADS == 2 and HEADS == KV_HEADS * GROUP and held.shape[1] == 2
        whole_heads = (2 * w_qkv.shape[2]) % HEAD == 0
        form = on_chip_grid if devices == 8 and paired and whole_heads else on_device
        return form(held, norm_gain, w_qkv, q_gain, k_gain, w_out, lengths)

    in_specs = (
        P("section", None, "dp", None),
        P("section", None),
        P("section", None, "dp"),
        P("section", None),
        P("section", None),
        P("section", None, "dp"),
        P("section", None, None),
    )
    out_specs = P("section", None, "dp", None)
    return jax.shard_map(
        body, mesh=mesh, in_specs=in_specs, out_specs=out_specs, check_vma=False
    )
```
